32 devices in a mesh: dp: 8 (over z, y), tensor: 4 (over x, core).
Axes of the slice: x: 2, y: 2, z: 4, core: 2. Of those that a mesh axis runs over, the one named last changes fastest.
Arguments:
- residual: bfloat16 [2048, 8192], P(('dp', 'tensor')), may hold values from -6 to 6
- streams: bfloat16 [3, 2048, 8192], P(None, 'dp', 'tensor'), may hold values from -6 to 6
- short_filter: float32 [3, 3, 8192], P(None, None, 'tensor'), may hold values from -3 to 3
- long_filter: float32 [512, 128], P('tensor'), may hold values from -0.5 to 0.5
- skip: float32 [8192], P('tensor'), may hold values from -4 to 4
- gain: float32 [8192], replicated, may hold values from 0.5 to 1.5
- cotangent: bfloat16 [2048, 8192], P(('dp', 'tensor')), may hold values from -6 to 6
Outputs:
- normed: bfloat16 [2048, 8192], P(('dp', 'tensor'))
- grad_residual: bfloat16 [2048, 8192], P(('dp', 'tensor'))
- stream_grad: bfloat16 [3, 2048, 8192], P(None, 'dp', 'tensor')
- long_grad: float32 [512, 128], P('tensor')
- short_grad: float32 [3, 3, 8192], P(None, None, 'tensor')
- skip_grad: float32 [8192], P('tensor')
- gain_grad: float32 [8192], P('tensor')
The draws below stay inside these ranges and needn't reach their ends.
All inputs are finite; a program needn't handle non-finite values.
Results may differ from the reference program's by a relative error of at most 0.025.
Values may be sent and summed in bfloat16 or wider, within the bound.
No kernel may reach another device: no remote copies, remote signals or barrier semaphores. Data moves between devices by JAX's collectives and lax.ppermute only.
A program may use at most 192 MiB of HBM per device.

```python
import jax
import jax.numpy as jnp
from jax import lax

D = 8192
TAPS = 128
GROUP = 16
TOKENS = 2048


def raised(array, rng, source, target, shards_of, factor):
    owner, partner = [(jnp.arange(array.shape[axis_at]) // (array.shape[axis_at] // shards_of)).reshape([-1 if axis == axis_at else 1 for axis in range(array.ndim)]) for axis_at in (source, target)]
    chosen = jax.random.permutation(rng, shards_of)[partner]
    strong = (owner == chosen) | (owner == (partner + shards_of // 2) % shards_of)
    return jnp.where(strong, factor * array, array)


def steps_of(stream_key, shape, split, least, top_value):
    def one(position, parts):
        heights = jax.random.uniform(jax.random.fold_in(jax.random.fold_in(stream_key, 6), position), (parts,), jnp.float32, least / len(split), top_value / len(split))
        return jnp.repeat(jnp.exp(heights), shape[position] // parts).reshape((-1,) + (1,) * (len(shape) - position - 1))

    level = one(*split[0])
    for cut in split[1:]:
        level = level * one(*cut)
    return level


def gaussian(rng, extent, width, most, split=(), held_as=jnp.bfloat16):
    drawn = width * jax.random.normal(rng, extent, jnp.float32)
    if split:
        drawn = drawn * steps_of(rng, extent, split, -0.22, 0.18)
    return jnp.clip(drawn, -most, most).astype(held_as)


def gaussian_with(own_key, dims, width, most, cuts, heavy, kind=jnp.bfloat16):
    array = width * jax.random.normal(own_key, dims, jnp.float32)
    if cuts:
        array = array * steps_of(own_key, dims, cuts, -0.22, 0.18)
    return jnp.clip(raised(array, jax.random.fold_in(own_key, 3), *heavy), -most, most).astype(kind)


def setup_inputs(seed: int = 0) -> dict:
    key_of = jax.random.split(jax.random.key(seed), 8)
    residual = gaussian(key_of[0], (TOKENS, D), 1.0, 6.0, ((0, 32),))
    streams = gaussian(key_of[1], (3, TOKENS, D), 1.0, 6.0, ((1, 8), (2, 4)))
    short_filter = gaussian(key_of[2], (3, 3, D), 0.6, 3.0, ((2, 4),), jnp.float32)
    long_filter = gaussian(key_of[3], (D // GROUP, TAPS), TAPS ** -0.5, 0.5, ((0, 4),), jnp.float32)
    skip = gaussian(key_of[4], (D,), 1.0, 4.0, ((0, 4),), jnp.float32)
    gain = jnp.clip(1.0 + 0.1 * jax.random.normal(key_of[5], (D,), jnp.float32), 0.5, 1.5)
    cotangent = gaussian_with(key_of[6], (TOKENS, D), 1.0, 6.0, ((0, 32),), (0, 1, 32, 2.75))
    return {"residual": residual, "streams": streams, "short_filter": short_filter, "long_filter": long_filter, "skip": skip, "gain": gain, "cotangent": cotangent}


norm_eps = 1e-05

def featurize(padded, short_taps):
    length = padded.shape[1] - 2
    return short_taps[:, 0][:, None, :] * padded[:, 2:] + short_taps[:, 1][:, None, :] * padded[:, 1:length + 1] + short_taps[:, 2][:, None, :] * padded[:, :length]

def causal_conv(signal, kernel, length):
    spectrum = jnp.fft.rfft(signal, n=2 * length, axis=0) * jnp.fft.rfft(kernel, n=2 * length, axis=0)
    return jnp.fft.irfft(spectrum, n=2 * length, axis=0)[:length].astype(jnp.float32)

def correlate(leading, trailing, length, keep_rows):
    spectrum = jnp.fft.rfft(leading, n=2 * length, axis=0) * jnp.conj(jnp.fft.rfft(trailing, n=2 * length, axis=0))
    return jnp.fft.irfft(spectrum, n=2 * length, axis=0)[:keep_rows].astype(jnp.float32)

def reference(residual, streams, short_filter, long_filter, skip, gain, cotangent):
    length = TOKENS
    slab_width = 512 if D % 512 == 0 else D
    slab_count = D // slab_width
    filter_half = lax.optimization_barrier(long_filter.astype(jnp.bfloat16))
    per_channel = jnp.repeat(filter_half, GROUP, axis=0)
    begin_list = jnp.arange(slab_count, dtype=jnp.int32) * slab_width

    def forward_piece(begin_at):
        stream_piece = lax.dynamic_slice_in_dim(streams, begin_at, slab_width, axis=2)
        taps_piece = lax.dynamic_slice_in_dim(short_filter, begin_at, slab_width, axis=2)
        kernel = lax.dynamic_slice_in_dim(per_channel, begin_at, slab_width, axis=0).astype(jnp.float32).T
        skip_piece = lax.dynamic_slice_in_dim(skip, begin_at, slab_width, axis=0)
        padded = jnp.pad(stream_piece, ((0, 0), (2, 0), (0, 0)))
        features = featurize(padded, taps_piece)
        gated_half = lax.optimization_barrier((features[1] * features[2]).astype(jnp.bfloat16))
        gated_rows = gated_half.astype(jnp.float32)
        mixed_rows = causal_conv(gated_rows, kernel, length) + skip_piece[None, :] * gated_rows
        return (padded, features, gated_rows, mixed_rows, kernel, taps_piece, skip_piece)

    def output_piece(begin_at):
        padded, features, gated_rows, mixed_rows, kernel, taps_piece, skip_piece = forward_piece(begin_at)
        return (features[0] * mixed_rows).astype(jnp.bfloat16)
    pieces = lax.map(output_piece, begin_list)
    output = jnp.moveaxis(pieces, 0, 1).reshape(length, D)
    row_block = 1024 if length % 1024 == 0 else length
    row_begins = jnp.arange(length // row_block, dtype=jnp.int32) * row_block

    def norm_piece(begin_at):
        resid_rows = lax.dynamic_slice_in_dim(residual, begin_at, row_block, axis=0).astype(jnp.float32)
        out_rows = lax.dynamic_slice_in_dim(output, begin_at, row_block, axis=0).astype(jnp.float32)
        cot_rows = lax.dynamic_slice_in_dim(cotangent, begin_at, row_block, axis=0).astype(jnp.float32)
        summed = resid_rows + out_rows
        inverse = lax.rsqrt(lax.optimization_barrier(jnp.mean(summed * summed, axis=1, keepdims=True)) + norm_eps)
        unit_rows = summed * inverse
        normed_rows = (unit_rows * gain[None, :]).astype(jnp.bfloat16)
        scaled = cot_rows * gain[None, :]
        along_unit = lax.optimization_barrier(jnp.mean(scaled * unit_rows, axis=1, keepdims=True))
        grad_rows = (inverse * (scaled - unit_rows * along_unit)).astype(jnp.bfloat16)
        return (normed_rows, grad_rows, lax.optimization_barrier(jnp.sum(cot_rows * unit_rows, axis=0)))
    normed_parts, grad_parts, gain_parts = lax.map(norm_piece, row_begins)
    normed = normed_parts.reshape(length, D)
    grad_residual = grad_parts.reshape(length, D)
    gain_grad = lax.optimization_barrier(jnp.sum(gain_parts, axis=0))

    def backward_piece(begin_at):
        padded, features, gated_rows, mixed_rows, kernel, taps_piece, skip_piece = forward_piece(begin_at)
        grad_out = lax.dynamic_slice_in_dim(grad_residual, begin_at, slab_width, axis=1).astype(jnp.float32)
        grad_half = lax.optimization_barrier((grad_out * features[0]).astype(jnp.bfloat16))
        grad_mixed = grad_half.astype(jnp.float32)
        grad_query = grad_out * mixed_rows
        grad_gated = correlate(grad_mixed, kernel, length, length) + skip_piece[None, :] * grad_mixed
        feature_grad = jnp.stack([grad_query, grad_gated * features[2], grad_gated * features[1]])
        extended = jnp.pad(feature_grad, ((0, 0), (0, 2), (0, 0)))
        stream_part = (taps_piece[:, 0][:, None, :] * extended[:, :length] + taps_piece[:, 1][:, None, :] * extended[:, 1:length + 1] + taps_piece[:, 2][:, None, :] * extended[:, 2:]).astype(jnp.bfloat16)
        short_part = jnp.stack([lax.optimization_barrier(jnp.sum(feature_grad * padded[:, 2 - offset:2 - offset + length], axis=1)) for offset in range(3)], axis=1)
        filter_part = correlate(grad_mixed, gated_rows, length, TAPS)
        filter_part = filter_part.reshape(TAPS, slab_width // GROUP, GROUP).sum(axis=2).T
        skip_part = lax.optimization_barrier(jnp.sum(grad_mixed * gated_rows, axis=0))
        return (stream_part, short_part, filter_part, skip_part)
    stream_parts, short_parts, filter_parts, skip_parts = lax.map(backward_piece, begin_list)
    stream_grad = jnp.moveaxis(stream_parts, 0, 2).reshape(3, length, D)
    short_grad = jnp.moveaxis(short_parts, 0, 2).reshape(3, 3, D)
    long_grad = filter_parts.reshape(D // GROUP, TAPS)
    skip_grad = skip_parts.reshape(D)
    return (normed, grad_residual, stream_grad, long_grad, short_grad, skip_grad, gain_grad)
```

```python
import functools

import jax
import jax.numpy as jnp
from jax import lax
from jax.experimental import pallas as pl
from jax.experimental.pallas import tpu as pltpu
from jax.sharding import PartitionSpec as P

norm_eps = 1e-05
LANES = 128
TAPS = 128
WIDTH = 16
PER = LANES // WIDTH
VMEM_LIMIT = 40 * 2**20
f32 = jnp.float32
bf16 = jnp.bfloat16


def params():
    return pltpu.CompilerParams(vmem_limit_bytes=VMEM_LIMIT)


def dot(a, b):
    return lax.dot_general(a, b, (((1,), (0,)), ((), ())), preferred_element_type=f32)


def dot_nt(a, b):
    return lax.dot_general(a, b, (((1,), (1,)), ((), ())), preferred_element_type=f32)


def lane_group(shape):
    return lax.broadcasted_iota(jnp.int32, shape, len(shape) - 1) % LANES // WIDTH


def pick_groups(stacked, rows):
    out = stacked[:rows]
    which = lane_group(out.shape)
    for g in range(1, PER):
        out = jnp.where(which == g, stacked[g * rows : (g + 1) * rows], out)
    return out


def shifted(scratch, halo, current):
    length = current.shape[0]
    scratch[6:8, :] = halo
    scratch[8 : 8 + length, :] = current
    return scratch[7 : 7 + length, :], scratch[6 : 6 + length, :]


def feature(scratch, halo_ref, streams_ref, taps_ref, s, lanes):
    now = streams_ref[s, :, lanes].astype(f32)
    one, two = shifted(scratch, halo_ref[s, :, lanes].astype(f32), now)
    taps = taps_ref[s, :, lanes]
    return taps[0:1] * now + taps[1:2] * one + taps[2:3] * two


def bands_kernel(filter_ref, ahead_ref, behind_ref):
    rows = filter_ref[...]
    half = rows.astype(bf16)
    flip = (
        lax.broadcasted_iota(jnp.int32, (TAPS, TAPS), 0) + lax.broadcasted_iota(jnp.int32, (TAPS, TAPS), 1) == TAPS - 1
    )
    back = dot(half, flip.astype(f32).astype(bf16))
    fore = half.astype(f32)
    zero = jnp.zeros((TAPS, TAPS), f32)
    for g in range(rows.shape[0]):
        for source, out, first in ((back, ahead_ref, 1), (fore, behind_ref, 0)):
            wide = jnp.concatenate([jnp.broadcast_to(source[g : g + 1], (TAPS, TAPS)), zero], axis=1)
            out[g] = pltpu.roll(wide, first, 1, stride=1, stride_axis=0).astype(bf16)


def forward_kernel(
    streams_ref, edge_ref, before_ref, taps_ref, skip_ref, ahead_ref, output_ref, mixed_ref, gated_ref, scratch
):
    length = streams_ref.shape[1]
    for col in range(streams_ref.shape[2] // LANES):
        lanes = slice(col * LANES, (col + 1) * LANES)
        f0, f1, f2 = (
            feature(scratch.at[s], edge_ref, streams_ref, taps_ref, s, lanes) for s in range(3)
        )
        gated = (f1 * f2).astype(bf16)
        gated_ref[:, lanes] = gated
        extended = jnp.concatenate([before_ref[:, lanes], gated], axis=0)
        bands = ahead_ref[col * PER : (col + 1) * PER].reshape(PER * TAPS, 2 * TAPS)
        skip = skip_ref[:, lanes]
        for pair in range(length // (2 * TAPS)):
            at = pair * 2 * TAPS
            both = jnp.concatenate([extended[at : at + 2 * TAPS], extended[at + TAPS : at + 3 * TAPS]], axis=1)
            result = pick_groups(dot(bands, both), TAPS)
            for b in range(2):
                rows = slice(at + b * TAPS, at + (b + 1) * TAPS)
                mixed = result[:, b * LANES : (b + 1) * LANES] + skip * gated[rows].astype(f32)
                mixed_ref[rows, lanes] = mixed
                output_ref[rows, lanes] = (f0[rows] * mixed).astype(bf16)


def norm_kernel(chunks, *refs):
    received, rest = refs[:chunks], refs[chunks:]
    residual_ref, cot_ref, gain_ref, normed_ref, grad_ref = rest[:5]
    sent, (share_ref, summed_ref, total_ref) = rest[5 : 5 + chunks], rest[5 + chunks :]
    sources, rows, part = received[0].shape
    width_all = residual_ref.shape[1]
    squares = jnp.zeros((rows, LANES), f32)
    products = jnp.zeros((rows, LANES), f32)
    pieces = [
        (s, k, slice((s * chunks + k) * part, (s * chunks + k + 1) * part))
        for s in range(sources)
        for k in range(chunks)
    ]
    for s, k, where in pieces:
        summed = residual_ref[:, where].astype(f32) + received[k][s].astype(f32)
        summed_ref[:, where] = summed
        scaled = cot_ref[:, where].astype(f32) * gain_ref[:, where]
        both = (summed * summed, scaled * summed)
        for col in range(part // LANES):
            lanes = slice(col * LANES, (col + 1) * LANES)
            squares = squares + both[0][:, lanes]
            products = products + both[1][:, lanes]
    inverse = lax.rsqrt(jnp.sum(squares, axis=1, keepdims=True) / width_all + norm_eps)
    along = inverse * jnp.sum(products, axis=1, keepdims=True) / width_all
    first = pl.program_id(0) == 0
    for s, k, where in pieces:
        unit = summed_ref[:, where] * inverse
        gain = gain_ref[:, where]
        cot = cot_ref[:, where].astype(f32)
        normed_ref[:, where] = (unit * gain).astype(bf16)
        grad = (inverse * (cot * gain - unit * along)).astype(bf16)
        grad_ref[:, where] = grad
        sent[k][s] = grad
        share = jnp.sum((cot * unit).reshape(rows // 8, 8, part), axis=0)
        total_ref[:, where] = jnp.where(first, share, total_ref[:, where] + share)

    @pl.when(pl.program_id(0) == pl.num_programs(0) - 1)
    def _():
        share_ref[...] = jnp.sum(total_ref[...], axis=0, keepdims=True)


def head_kernel(
    streams_ref, edge_ref, taps_ref, skip_ref, behind_ref, grad_ref, mixed_ref, inner_ref, head_ref, scratch
):
    for col in range(streams_ref.shape[2] // LANES):
        lanes = slice(col * LANES, (col + 1) * LANES)
        f0 = feature(scratch, edge_ref, streams_ref, taps_ref, 0, lanes)
        inner = (grad_ref[:, lanes].astype(f32) * f0).astype(bf16)
        inner_ref[:, lanes] = inner
        early = [
            taps_ref[s, 0:1, lanes] * streams_ref[s, 0:16, lanes].astype(f32)[:8]
            for s in range(3)
        ]
        features = []
        for s in (1, 2):
            taps = taps_ref[s, :, lanes]
            now = streams_ref[s, 0:16, lanes].astype(f32)
            scratch[6:8, :] = edge_ref[s, :, lanes].astype(f32)
            scratch[8:24, :] = now
            features.append(early[s] + taps[1:2] * scratch[7:15, :] + taps[2:3] * scratch[6:14, :])
        bands = behind_ref[col * PER : (col + 1) * PER, 0:16, :].reshape(PER * 16, 2 * TAPS)
        conv = pick_groups(dot(bands, inner[: 2 * TAPS]), 16)[:8]
        grad_gated = conv + skip_ref[:, lanes] * inner[0:16].astype(f32)[:8]
        head_ref[0, :, lanes] = (grad_ref[0:16, lanes].astype(f32)[:8] * mixed_ref[0:8, lanes])[:2]
        head_ref[1, :, lanes] = (grad_gated * features[1])[:2]
        head_ref[2, :, lanes] = (grad_gated * features[0])[:2]


def sums_kernel(
    streams_ref, edge_ref, gated_ref, before_ref, inner_ref, grad_ref, mixed_ref, gain_ref, early_ref, scratch
):
    length = streams_ref.shape[1]
    flip = (
        lax.broadcasted_iota(jnp.int32, (2 * TAPS, 2 * TAPS), 0)
        + lax.broadcasted_iota(jnp.int32, (2 * TAPS, 2 * TAPS), 1)
        == 2 * TAPS - 1
    )
    flip = flip.astype(f32).astype(bf16)
    which = lane_group((TAPS, 2 * LANES))
    masks = [jnp.where(which == g, 1.0, 0.0).astype(bf16) for g in range(PER)]
    for col in range(streams_ref.shape[2] // LANES):
        lanes = slice(col * LANES, (col + 1) * LANES)
        gated = gated_ref[:, lanes]
        inner = inner_ref[:, lanes]
        extended = jnp.concatenate([before_ref[:, lanes], gated], axis=0)
        pairs = 0.0
        for pair in range(length // (2 * TAPS)):
            at = pair * 2 * TAPS
            both = jnp.concatenate([extended[at : at + 2 * TAPS], extended[at + TAPS : at + 3 * TAPS]], axis=1)
            backward = dot(flip, both).astype(bf16)
            grads = jnp.concatenate([inner[at : at + TAPS], inner[at + TAPS : at + 2 * TAPS]], axis=1)
            stacked = jnp.concatenate([grads * mask for mask in masks], axis=0)
            pairs = pairs + dot_nt(stacked, backward)
        base = col * 16
        for g in range(PER):
            skewed = pltpu.roll(pairs[g * TAPS : (g + 1) * TAPS], TAPS + 1, 1, stride=1, stride_axis=0)
            early_ref[base + g : base + g + 1, :] = jnp.sum(skewed[:, :TAPS], axis=0, keepdims=True)
        early_ref[base + 8 : base + 9, :] = jnp.sum(inner.astype(f32) * gated.astype(f32), axis=0, keepdims=True)
        early_ref[base + 9 : base + 10, :] = jnp.sum(gain_ref[:, lanes], axis=0, keepdims=True)
        grad_query = grad_ref[:, lanes].astype(f32) * mixed_ref[:, lanes]
        now = streams_ref[0, :, lanes].astype(f32)
        one, two = shifted(scratch, edge_ref[0, :, lanes].astype(f32), now)
        for j, shift in enumerate((now, one, two)):
            early_ref[base + 10 + j : base + 11 + j, :] = jnp.sum(grad_query * shift, axis=0, keepdims=True)
        early_ref[base + 13 : base + 16, :] = jnp.zeros((3, LANES), f32)


def backward_kernel(
    aliased,
    streams_ref,
    edge_ref,
    taps_ref,
    skip_ref,
    behind_ref,
    grad_ref,
    mixed_ref,
    inner_ref,
    after_ref,
    next_ref,
    *refs,
):
    stream_grad_ref, late_ref, scratch, ahead = refs[1:] if aliased else refs
    length = streams_ref.shape[1]
    for col in range(streams_ref.shape[2] // LANES):
        lanes = slice(col * LANES, (col + 1) * LANES)
        inner = inner_ref[:, lanes]
        extended = jnp.concatenate([inner, after_ref[:, lanes]], axis=0)
        bands = behind_ref[col * PER : (col + 1) * PER].reshape(PER * TAPS, 2 * TAPS)
        parts = []
        for pair in range(length // (2 * TAPS)):
            at = pair * 2 * TAPS
            both = jnp.concatenate([extended[at : at + 2 * TAPS], extended[at + TAPS : at + 3 * TAPS]], axis=1)
            result = pick_groups(dot(bands, both), TAPS)
            parts += [result[:, :LANES], result[:, LANES:]]
        grad_gated = jnp.concatenate(parts, axis=0) + skip_ref[:, lanes] * inner.astype(f32)
        shifts, features = {}, {}
        for s in (1, 2):
            now = streams_ref[s, :, lanes].astype(f32)
            one, two = shifted(scratch.at[s], edge_ref[s, :, lanes].astype(f32), now)
            taps = taps_ref[s, :, lanes]
            shifts[s] = (now, one, two)
            features[s] = taps[0:1] * now + taps[1:2] * one + taps[2:3] * two
        grads = (
            grad_ref[:, lanes].astype(f32) * mixed_ref[:, lanes],
            grad_gated * features[2],
            grad_gated * features[1],
        )
        for s in range(3):
            ahead[s, 0:length, :] = grads[s]
            ahead[s, length : length + 2, :] = next_ref[s, :, lanes]
            taps = taps_ref[s, :, lanes]
            stream_grad_ref[s, :, lanes] = (
                taps[0:1] * grads[s] + taps[1:2] * ahead[s, 1 : length + 1, :] + taps[2:3] * ahead[s, 2 : length + 2, :]
            ).astype(bf16)
        for s in (1, 2):
            for j in range(3):
                row = col * 8 + (s - 1) * 3 + j
                late_ref[row : row + 1, :] = jnp.sum(grads[s] * shifts[s][j], axis=0, keepdims=True)
        late_ref[col * 8 + 6 : col * 8 + 8, :] = jnp.zeros((2, LANES), f32)


def from_behind(value, axis, steps):
    count = lax.axis_size(axis)
    first, last = (max(0, -steps), min(count, count - steps))
    return lax.ppermute(value, axis, [(source, source + steps) for source in range(first, last)])


def sum_over(value, axis):
    count, reach = lax.axis_size(axis), 1
    while reach < count:
        value = lax.reduce_precision(value, 8, 7)
        other = lax.ppermute(value.astype(bf16), axis, [(i, i ^ reach) for i in range(count)])
        value = value + other.astype(f32)
        reach *= 2
    return value


def local(residual, streams, short_filter, long_filter, skip, gain, cotangent):
    tokens_here, channels = streams.shape[1:]
    groups = long_filter.shape[0]
    rows_here, width_all = residual.shape
    owners = lax.axis_size("tensor")
    assert long_filter.shape[1] == TAPS and channels == groups * WIDTH and tokens_here % (2 * TAPS) == 0
    chunks = 2
    part = channels // chunks
    step = min(part, 512)
    steps = part // step
    cols = step // LANES
    skip_row = skip[None, :]
    gain_row = gain[None, :]

    def spec(shape, index):
        return pl.BlockSpec(shape, index)

    def wide(rows, offset=0):
        return spec((rows, step), lambda i: (0, i + offset))

    def deep(first, rows, offset=0):
        return spec((first, rows, step), lambda i: (0, 0, i + offset))

    def band(offset):
        return spec((step // WIDTH, TAPS, 2 * TAPS), lambda i: (i + offset, 0, 0))

    def padded(count=None):
        shape = (tokens_here + 8, LANES)
        return pltpu.VMEM(shape if count is None else (count,) + shape, f32)

    edge = from_behind(streams[:, tokens_here - 2 :], "dp", 1)
    tail = streams[1:, tokens_here - TAPS - 2 :].astype(f32)
    tail_features = (
        short_filter[1:, 0][:, None, :] * tail[:, 2:]
        + short_filter[1:, 1][:, None, :] * tail[:, 1:-1]
        + short_filter[1:, 2][:, None, :] * tail[:, :-2]
    )
    tail_gated = (tail_features[0] * tail_features[1]).astype(bf16)
    before = [from_behind(tail_gated[:, k * part : (k + 1) * part], "dp", 1) for k in range(chunks)]

    band_shape = jax.ShapeDtypeStruct((groups, TAPS, 2 * TAPS), bf16)
    ahead_bands, behind_bands = pl.pallas_call(
        bands_kernel,
        grid=(groups // PER,),
        in_specs=[spec((PER, TAPS), lambda i: (i, 0))],
        out_specs=[spec((PER, TAPS, 2 * TAPS), lambda i: (i, 0, 0))] * 2,
        out_shape=[band_shape] * 2,
        compiler_params=params(),
        name="bands",
    )(long_filter)

    mixed, gated, received = [], [], []
    for k in range(chunks):
        output, mixed_k, gated_k = pl.pallas_call(
            forward_kernel,
            grid=(steps,),
            in_specs=[
                deep(3, tokens_here, k * steps),
                deep(3, 2, k * steps),
                wide(TAPS),
                deep(3, 3, k * steps),
                wide(1, k * steps),
                band(k * steps),
            ],
            out_specs=[wide(tokens_here)] * 3,
            out_shape=[jax.ShapeDtypeStruct((tokens_here, part), t) for t in (bf16, f32, bf16)],
            scratch_shapes=[padded(3)],
            compiler_params=params(),
            name="forward",
        )(streams, edge, before[k], short_filter, skip_row, ahead_bands)
        mixed.append(mixed_k)
        gated.append(gated_k)
        received.append(
            lax.all_to_all(output.reshape(owners, rows_here, part), "tensor", split_axis=0, concat_axis=0, tiled=True)
        )

    block = min(rows_here, 16)
    by_rows = spec((block, width_all), lambda i: (i, 0))
    by_owner = spec((owners, block, part), lambda i: (0, i, 0))
    whole_row = spec((1, width_all), lambda i: (0, 0))
    results = pl.pallas_call(
        functools.partial(norm_kernel, chunks),
        grid=(rows_here // block,),
        in_specs=[by_owner] * chunks + [by_rows, by_rows, whole_row],
        out_specs=[by_rows, by_rows] + [by_owner] * chunks + [whole_row],
        out_shape=[jax.ShapeDtypeStruct(residual.shape, bf16)] * 2
        + [jax.ShapeDtypeStruct((owners, rows_here, part), bf16)] * chunks
        + [jax.ShapeDtypeStruct((1, width_all), f32)],
        scratch_shapes=[pltpu.VMEM((block, width_all), f32), pltpu.VMEM((8, width_all), f32)],
        compiler_params=params(),
        name="norm",
    )(*received, residual, cotangent, gain_row)
    normed, grad_residual, sent, gain_share = results[0], results[1], results[2 : 2 + chunks], results[-1]

    grads = [
        lax.all_to_all(piece, "tensor", split_axis=0, concat_axis=0, tiled=True).reshape(tokens_here, part)
        for piece in sent
    ]
    gain_parts = lax.all_to_all(
        gain_share.reshape(owners, channels), "tensor", split_axis=0, concat_axis=0, tiled=True
    )

    inner, after, following = [], [], []
    for k in range(chunks):
        inner_k, head_k = pl.pallas_call(
            head_kernel,
            grid=(steps,),
            in_specs=[
                deep(3, tokens_here, k * steps),
                deep(3, 2, k * steps),
                deep(3, 3, k * steps),
                wide(1, k * steps),
                band(k * steps),
                wide(tokens_here),
                wide(tokens_here),
            ],
            out_specs=[wide(tokens_here), deep(3, 2)],
            out_shape=[
                jax.ShapeDtypeStruct((tokens_here, part), bf16),
                jax.ShapeDtypeStruct((3, 2, part), f32),
            ],
            scratch_shapes=[padded()],
            compiler_params=params(),
            name="head",
        )(streams, edge, short_filter, skip_row, behind_bands, grads[k], mixed[k])
        inner.append(inner_k)
        after.append(from_behind(inner_k[:TAPS], "dp", -1))
        following.append(from_behind(head_k, "dp", -1))

    early = []
    for k in range(chunks):
        early.append(
            pl.pallas_call(
                sums_kernel,
                grid=(steps,),
                in_specs=[
                    deep(1, tokens_here, k * steps),
                    deep(1, 2, k * steps),
                    wide(tokens_here),
                    wide(TAPS),
                    wide(tokens_here),
                    wide(tokens_here),
                    wide(tokens_here),
                    wide(owners, k * steps),
                ],
                out_specs=spec((cols * 16, LANES), lambda i: (i, 0)),
                out_shape=jax.ShapeDtypeStruct((part // LANES * 16, LANES), f32),
                scratch_shapes=[padded()],
                compiler_params=params(),
                name="sums",
            )(streams, edge, gated[k], before[k], inner[k], grads[k], mixed[k], gain_parts)
        )
    early = sum_over(jnp.concatenate(early, axis=0), "dp").reshape(channels // LANES, 16, LANES)

    stream_grad, late = None, []
    for k in range(chunks):
        aliased = stream_grad is not None
        operands = [streams, edge, short_filter, skip_row, behind_bands, grads[k], mixed[k], inner[k], after[k], following[k]]
        in_specs = [
            deep(3, tokens_here, k * steps),
            deep(3, 2, k * steps),
            deep(3, 3, k * steps),
            wide(1, k * steps),
            band(k * steps),
            wide(tokens_here),
            wide(tokens_here),
            wide(tokens_here),
            wide(TAPS),
            deep(3, 2),
        ]
        if aliased:
            operands.append(stream_grad)
            in_specs.append(pl.BlockSpec(memory_space=pl.ANY))
        stream_grad, late_k = pl.pallas_call(
            functools.partial(backward_kernel, aliased),
            grid=(steps,),
            in_specs=in_specs,
            out_specs=[
                deep(3, tokens_here, k * steps),
                spec((cols * 8, LANES), lambda i: (i, 0)),
            ],
            out_shape=[
                jax.ShapeDtypeStruct(streams.shape, bf16),
                jax.ShapeDtypeStruct((part // LANES * 8, LANES), f32),
            ],
            scratch_shapes=[padded(3), padded(3)],
            input_output_aliases={len(operands) - 1: 0} if aliased else {},
            compiler_params=params(),
            name="backward",
        )(*operands)
        late.append(late_k)
    late = sum_over(jnp.concatenate(late, axis=0), "dp").reshape(channels // LANES, 8, LANES)

    long_grad = early[:, :8].reshape(groups, TAPS)
    skip_grad = early[:, 8].reshape(channels)
    gain_grad = early[:, 9].reshape(channels)
    short_rows = jnp.concatenate([early[:, 10:13], late[:, :6]], axis=1)
    short_grad = jnp.swapaxes(short_rows, 0, 1).reshape(3, 3, channels)
    return (normed, grad_residual, stream_grad, long_grad, short_grad, skip_grad, gain_grad)


def solution(mesh):
    placed = (
        P(("dp", "tensor"), None),
        P(None, "dp", "tensor"),
        P(None, None, "tensor"),
        P("tensor", None),
        P("tensor"),
        P(),
        P(("dp", "tensor"), None),
    )
    return jax.shard_map(
        local,
        mesh=mesh,
        in_specs=placed,
        out_specs=(
            P(("dp", "tensor"), None),
            P(("dp", "tensor"), None),
            P(None, "dp", "tensor"),
            P("tensor", None),
            P(None, None, "tensor"),
            P("tensor"),
            P("tensor"),
        ),
        check_vma=False,
    )
```

```python
import functools

import jax
import jax.numpy as jnp
from jax import lax
from jax.experimental import pallas as pl
from jax.experimental.pallas import tpu as pltpu
from jax.sharding import PartitionSpec as P

norm_eps = 1e-05
LANES = 128
TAPS = 128
WIDTH = 16
PER = LANES // WIDTH
BLOCK = 64
SPAN = 256
VMEM_LIMIT = 56 * 2**20
f32 = jnp.float32
bf16 = jnp.bfloat16


def params():
    return pltpu.CompilerParams(vmem_limit_bytes=VMEM_LIMIT)


def dot(a, b):
    return lax.dot_general(a, b, (((1,), (0,)), ((), ())), preferred_element_type=f32)


def dot_nt(a, b):
    return lax.dot_general(a, b, (((1,), (1,)), ((), ())), preferred_element_type=f32)


def lane_group(shape):
    return lax.broadcasted_iota(jnp.int32, shape, len(shape) - 1) % LANES // WIDTH


def pick_groups(stacked, rows):
    out = stacked[:rows]
    which = lane_group(out.shape)
    for g in range(1, PER):
        out = jnp.where(which == g, stacked[g * rows : (g + 1) * rows], out)
    return out


def shifted(scratch, halo, current):
    length = current.shape[0]
    scratch[6:8, :] = halo
    scratch[8 : 8 + length, :] = current
    return scratch[7 : 7 + length, :], scratch[6 : 6 + length, :]


def band(row, first, rows):
    wide = jnp.concatenate([row, jnp.zeros((1, SPAN - TAPS), f32)], axis=1)
    return pltpu.roll(jnp.broadcast_to(wide, (rows, SPAN)), first, 1, stride=1, stride_axis=0).astype(bf16)


def anti_identity(size):
    total = lax.broadcasted_iota(jnp.int32, (size, size), 0) + lax.broadcasted_iota(jnp.int32, (size, size), 1)
    return jnp.where(total == size - 1, 1.0, 0.0).astype(bf16)


def windows(extended, length):
    return jnp.concatenate([extended[at : at + SPAN] for at in range(0, length, BLOCK)], axis=1)


def convolve(bands, extended, length, rows=BLOCK):
    stacked = dot(bands.reshape(PER * rows, SPAN), windows(extended, length))
    result = pick_groups(stacked, rows)
    return [result[:, at : at + LANES] for at in range(0, result.shape[1], LANES)]


def bands_kernel(filter_ref, ahead_ref, behind_ref):
    half = filter_ref[...].astype(bf16)
    back = dot(half, anti_identity(TAPS))
    fore = half.astype(f32)
    for g in range(half.shape[0]):
        ahead_ref[g] = band(back[g : g + 1], SPAN - TAPS - BLOCK + 1, BLOCK)
        behind_ref[g] = band(fore[g : g + 1], 0, BLOCK)


def open_kernel(
    cot_ref, residual_ref, last0_ref, last1_ref, last2_ref, prior1_ref, prior2_ref, taps_ref, packed_ref, halo_ref, scratch
):
    owners, _, _, channels = packed_ref.shape
    for j in range(owners):
        where = slice(j * channels, (j + 1) * channels)
        packed_ref[j, 0] = cot_ref[:, where]
        packed_ref[j, 1] = residual_ref[:, where]
    for col in range(halo_ref.shape[1] // LANES):
        lanes = slice(col * LANES, (col + 1) * LANES)
        features = []
        for s, last, prior in ((1, last1_ref, prior1_ref), (2, last2_ref, prior2_ref)):
            now = last[0, :, lanes].astype(f32)
            one, two = shifted(scratch.at[s], prior[0, :, lanes].astype(f32)[14:], now)
            taps = taps_ref[s, :, lanes]
            features.append(taps[0:1] * now + taps[1:2] * one + taps[2:3] * two)
        halo_ref[:TAPS, lanes] = (features[0] * features[1]).astype(bf16)
        edges = scratch.at[0]
        edges[0:2, :] = last0_ref[0, :, lanes].astype(f32)[14:]
        edges[2:4, :] = scratch[1, TAPS + 6 : TAPS + 8, :]
        edges[4:6, :] = scratch[2, TAPS + 6 : TAPS + 8, :]
        edges[6:8, :] = jnp.zeros((2, LANES), f32)
        halo_ref[TAPS : TAPS + 8, lanes] = edges[0:8, :].astype(bf16)


def edge(halo_ref, s, lanes):
    return halo_ref[TAPS : TAPS + 8, lanes].astype(f32)[2 * s : 2 * s + 2]


def feature(scratch, halo_ref, streams_ref, taps_ref, s, lanes, index):
    now = streams_ref[index, :, lanes].astype(f32)
    one, two = shifted(scratch, edge(halo_ref, s, lanes), now)
    taps = taps_ref[s, :, lanes]
    return taps[0:1] * now + taps[1:2] * one + taps[2:3] * two


def forward_kernel(streams_ref, halo_ref, taps_ref, skip_ref, ahead_ref, output_ref, mixed_ref, gated_ref, scratch):
    length = streams_ref.shape[1]
    for col in range(streams_ref.shape[2] // LANES):
        lanes = slice(col * LANES, (col + 1) * LANES)
        f0, f1, f2 = (feature(scratch.at[s], halo_ref, streams_ref, taps_ref, s, lanes, s) for s in range(3))
        gated = (f1 * f2).astype(bf16)
        gated_ref[:, lanes] = gated
        zero = jnp.zeros((SPAN - TAPS - BLOCK, LANES), bf16)
        extended = jnp.concatenate([zero, halo_ref[:TAPS, lanes], gated], axis=0)
        skip = skip_ref[:, lanes]
        for b, result in enumerate(convolve(ahead_ref[col * PER : (col + 1) * PER], extended, length)):
            rows = slice(b * BLOCK, (b + 1) * BLOCK)
            mixed = result + skip * gated[rows].astype(f32)
            mixed_ref[rows, lanes] = mixed
            output_ref[rows, lanes] = (f0[rows] * mixed).astype(bf16)


def columns_of(received_ref, which, lanes):
    piece = received_ref[:, which, :, lanes].astype(f32)
    return piece.reshape(piece.shape[0] * piece.shape[1], LANES)


def stats_kernel(received_ref, output_ref, gain_ref, stats_ref, squares_ref, products_ref):
    @pl.when(pl.program_id(0) == 0)
    def _():
        squares_ref[...] = jnp.zeros_like(squares_ref)
        products_ref[...] = jnp.zeros_like(products_ref)

    squares, products = squares_ref[...], products_ref[...]
    for col in range(output_ref.shape[1] // LANES):
        lanes = slice(col * LANES, (col + 1) * LANES)
        summed = columns_of(received_ref, 1, lanes) + output_ref[:, lanes].astype(f32)
        squares = squares + summed * summed
        products = products + columns_of(received_ref, 0, lanes) * gain_ref[:, lanes] * summed
    squares_ref[...] = squares
    products_ref[...] = products

    @pl.when(pl.program_id(0) == pl.num_programs(0) - 1)
    def _():
        for row, sums in ((0, squares), (1, products)):
            stats_ref[row : row + 1, :] = jnp.sum(sums.T, axis=0, keepdims=True)


def norm_kernel(received_ref, residual_ref, cot_ref, gain_ref, normed_ref, grad_ref, summed_ref):
    sources, rows, part = received_ref.shape
    width_all = residual_ref.shape[1]
    squares = jnp.zeros((rows, LANES), f32)
    products = jnp.zeros((rows, LANES), f32)
    for s in range(sources):
        where = slice(s * part, (s + 1) * part)
        summed = residual_ref[:, where].astype(f32) + received_ref[s].astype(f32)
        summed_ref[:, where] = summed
        scaled = cot_ref[:, where].astype(f32) * gain_ref[:, where]
        both = (summed * summed, scaled * summed)
        for col in range(part // LANES):
            lanes = slice(col * LANES, (col + 1) * LANES)
            squares = squares + both[0][:, lanes]
            products = products + both[1][:, lanes]
    inverse = lax.rsqrt(jnp.sum(squares, axis=1, keepdims=True) / width_all + norm_eps)
    along = inverse * jnp.sum(products, axis=1, keepdims=True) / width_all
    for s in range(sources):
        where = slice(s * part, (s + 1) * part)
        unit = summed_ref[:, where] * inverse
        gain = gain_ref[:, where]
        normed_ref[:, where] = (unit * gain).astype(bf16)
        grad_ref[:, where] = (inverse * (cot_ref[:, where].astype(f32) * gain - unit * along)).astype(bf16)


def head_kernel(
    width_all,
    streams_ref,
    first1_ref,
    first2_ref,
    halo_ref,
    taps_ref,
    skip_ref,
    filter_ref,
    stats_ref,
    received_ref,
    output_ref,
    gain_ref,
    mixed_ref,
    grad_ref,
    inner_ref,
    first_ref,
    share_ref,
    scratch,
    inverse_ref,
    along_ref,
):
    @pl.when(pl.program_id(0) == 0)
    def _():
        tokens = stats_ref.shape[1]
        squares = jnp.broadcast_to(stats_ref[0:1, :], (LANES, tokens)).T
        products = jnp.broadcast_to(stats_ref[1:2, :], (LANES, tokens)).T
        inverse = lax.rsqrt(squares / width_all + norm_eps)
        inverse_ref[...] = inverse
        along_ref[...] = inverse * products / width_all

    inverse, along = inverse_ref[...], along_ref[...]
    for col in range(streams_ref.shape[2] // LANES):
        lanes = slice(col * LANES, (col + 1) * LANES)
        cot = columns_of(received_ref, 0, lanes)
        unit = (columns_of(received_ref, 1, lanes) + output_ref[:, lanes].astype(f32)) * inverse
        share_ref[:, lanes] = jnp.sum(cot * unit, axis=0, keepdims=True)
        grad_half = (inverse * (cot * gain_ref[:, lanes] - unit * along)).astype(bf16)
        grad_ref[:, lanes] = grad_half
        grad = grad_half.astype(f32)
        f0 = feature(scratch, halo_ref, streams_ref, taps_ref, 0, lanes, 0)
        inner = (grad * f0).astype(bf16)
        inner_ref[:, lanes] = inner
        first_ref[:TAPS, lanes] = inner[:TAPS]
        features = []
        for s, top in ((1, first1_ref), (2, first2_ref)):
            taps = taps_ref[s, :, lanes]
            now = top[0, :, lanes].astype(f32)
            scratch[6:8, :] = edge(halo_ref, s, lanes)
            scratch[8:24, :] = now
            features.append(taps[0:1] * now[:8] + taps[1:2] * scratch[7:15, :] + taps[2:3] * scratch[6:14, :])
        half = filter_ref[col * PER : (col + 1) * PER].astype(bf16).astype(f32)
        bands = jnp.stack([band(half[g : g + 1], 0, 16) for g in range(PER)])
        conv = convolve(bands, inner, BLOCK, 16)[0][:8]
        grad_gated = conv + skip_ref[:, lanes] * inner[:16].astype(f32)[:8]
        scratch[0:2, :] = (grad[:8] * mixed_ref[0:8, lanes])[:2]
        scratch[2:4, :] = (grad_gated * features[1])[:2]
        scratch[4:6, :] = (grad_gated * features[0])[:2]
        scratch[6:8, :] = jnp.zeros((2, LANES), f32)
        rows = scratch[0:8, :]
        high = rows.astype(bf16)
        first_ref[TAPS : TAPS + 8, lanes] = high
        first_ref[TAPS + 8 : TAPS + 16, lanes] = (rows - high.astype(f32)).astype(bf16)


def sums_kernel(streams_ref, halo_ref, gated_ref, inner_ref, grad_ref, mixed_ref, gain_ref, early_ref, scratch):
    length = streams_ref.shape[1]
    blocks = length // BLOCK
    flip = anti_identity(SPAN)
    which = lane_group((BLOCK, blocks * LANES))
    masks = [jnp.where(which == g, 1.0, 0.0).astype(bf16) for g in range(PER)]
    zero = jnp.zeros((SPAN - TAPS - BLOCK, LANES), bf16)
    for col in range(streams_ref.shape[2] // LANES):
        lanes = slice(col * LANES, (col + 1) * LANES)
        gated = gated_ref[:, lanes]
        inner = inner_ref[:, lanes]
        extended = jnp.concatenate([zero, halo_ref[:TAPS, lanes], gated], axis=0)
        backward = dot(flip, windows(extended, length)).astype(bf16)
        grads = jnp.concatenate([inner[at : at + BLOCK] for at in range(0, length, BLOCK)], axis=1)
        pairs = dot_nt(jnp.concatenate([grads * mask for mask in masks], axis=0), backward)
        base = col * 16
        for g in range(PER):
            skewed = pltpu.roll(pairs[g * BLOCK : (g + 1) * BLOCK], SPAN - BLOCK + 1, 1, stride=1, stride_axis=0)
            early_ref[base + g : base + g + 1, :] = jnp.sum(skewed[:, :TAPS], axis=0, keepdims=True)
        early_ref[base + 8 : base + 9, :] = jnp.sum(inner.astype(f32) * gated.astype(f32), axis=0, keepdims=True)
        early_ref[base + 9 : base + 10, :] = gain_ref[:, lanes]
        grad_query = grad_ref[:, lanes].astype(f32) * mixed_ref[:, lanes]
        now = streams_ref[0, :, lanes].astype(f32)
        one, two = shifted(scratch, edge(halo_ref, 0, lanes), now)
        for j, shift in enumerate((now, one, two)):
            early_ref[base + 10 + j : base + 11 + j, :] = jnp.sum(grad_query * shift, axis=0, keepdims=True)
        early_ref[base + 13 : base + 16, :] = jnp.zeros((3, LANES), f32)


def backward_kernel(
    aliased,
    streams_ref,
    halo_ref,
    taps_ref,
    skip_ref,
    behind_ref,
    grad_ref,
    mixed_ref,
    inner_ref,
    after_ref,
    *refs,
):
    stream_grad_ref, late_ref, scratch, ahead = refs[1:] if aliased else refs
    length = streams_ref.shape[1]
    for col in range(streams_ref.shape[2] // LANES):
        lanes = slice(col * LANES, (col + 1) * LANES)
        inner = inner_ref[:, lanes]
        zero = jnp.zeros((SPAN - TAPS - BLOCK, LANES), bf16)
        extended = jnp.concatenate([inner, after_ref[:TAPS, lanes], zero], axis=0)
        parts = convolve(behind_ref[col * PER : (col + 1) * PER], extended, length)
        grad_gated = jnp.concatenate(parts, axis=0) + skip_ref[:, lanes] * inner.astype(f32)
        shifts, features = {}, {}
        for s in (1, 2):
            now = streams_ref[s, :, lanes].astype(f32)
            one, two = shifted(scratch.at[s], edge(halo_ref, s, lanes), now)
            taps = taps_ref[s, :, lanes]
            shifts[s] = (now, one, two)
            features[s] = taps[0:1] * now + taps[1:2] * one + taps[2:3] * two
        grads = (
            grad_ref[:, lanes].astype(f32) * mixed_ref[:, lanes],
            grad_gated * features[2],
            grad_gated * features[1],
        )
        following = after_ref[TAPS : TAPS + 16, lanes].astype(f32)
        following = following[:8] + following[8:]
        for s in range(3):
            ahead[s, 0:length, :] = grads[s]
            ahead[s, length : length + 2, :] = following[2 * s : 2 * s + 2]
            taps = taps_ref[s, :, lanes]
            stream_grad_ref[s, :, lanes] = (
                taps[0:1] * grads[s] + taps[1:2] * ahead[s, 1 : length + 1, :] + taps[2:3] * ahead[s, 2 : length + 2, :]
            ).astype(bf16)
        for s in (1, 2):
            for j in range(3):
                row = col * 8 + (s - 1) * 3 + j
                late_ref[row : row + 1, :] = jnp.sum(grads[s] * shifts[s][j], axis=0, keepdims=True)
        late_ref[col * 8 + 6 : col * 8 + 8, :] = jnp.zeros((2, LANES), f32)


def from_behind(value, axis, steps):
    count = lax.axis_size(axis)
    first, last = (max(0, -steps), min(count, count - steps))
    return lax.ppermute(value, axis, [(source, source + steps) for source in range(first, last)])


def exchange_sum(value, axis):
    count, reach, other = lax.axis_size(axis), 1, None
    while reach < count:
        if other is not None:
            value = value + other.astype(f32)
        value = lax.reduce_precision(value, 8, 7)
        other = lax.ppermute(value.astype(bf16), axis, [(i, i ^ reach) for i in range(count)])
        reach *= 2
    return value, other


def close_kernel(mine_ref, other_ref, long_ref, short_ref, skip_ref, gain_ref):
    columns = skip_ref.shape[1] // LANES
    total = mine_ref[...] + other_ref[...].astype(f32)
    for col in range(columns):
        lanes = slice(col * LANES, (col + 1) * LANES)
        at, late = col * 16, columns * 16 + col * 8
        long_ref[col * PER : (col + 1) * PER, :] = total[at : at + PER]
        skip_ref[:, lanes] = total[at + 8 : at + 9]
        gain_ref[:, lanes] = total[at + 9 : at + 10]
        for j in range(3):
            short_ref[0, j : j + 1, lanes] = total[at + 10 + j : at + 11 + j]
            for s in (1, 2):
                row = late + (s - 1) * 3 + j
                short_ref[s, j : j + 1, lanes] = total[row : row + 1]


def local(residual, streams, short_filter, long_filter, skip, gain, cotangent):
    tokens_here, channels = streams.shape[1:]
    groups = long_filter.shape[0]
    rows_here, width_all = residual.shape
    owners = lax.axis_size("tensor")
    assert long_filter.shape[1] == TAPS and channels == groups * WIDTH and tokens_here % (2 * TAPS) == 0
    chunks = 2
    part = channels // chunks
    step = min(part, 512)
    steps, all_steps = part // step, channels // step
    cols = step // LANES
    skip_row = skip[None, :]
    gain_row = gain[None, :]
    gain_here = lax.dynamic_slice_in_dim(gain, lax.axis_index("tensor") * channels, channels)[None, :]

    spec = pl.BlockSpec

    def wide(rows, offset=0):
        return spec((rows, step), lambda i: (0, i + offset))

    def deep(first, rows, offset=0):
        return spec((first, rows, step), lambda i: (0, 0, i + offset))

    def bands_of(offset=0):
        return spec((step // WIDTH, BLOCK, SPAN), lambda i: (i + offset, 0, 0))

    def arrived(offset=0):
        return spec((owners, 2, rows_here, step), lambda i: (0, 0, 0, i + offset))

    def padded(count=None):
        shape = (tokens_here + 8, LANES)
        return pltpu.VMEM(shape if count is None else (count,) + shape, f32)

    def kernel(body, name, micros, **how):
        return pl.pallas_call(
            body,
            compiler_params=params(),
            cost_estimate=pl.CostEstimate(flops=0, bytes_accessed=micros * 1000, transcendentals=0),
            name=name,
            **how,
        )

    def last(s):
        return spec((1, TAPS, step), lambda i: (s, tokens_here // TAPS - 1, i))

    def rows16(s, back):
        return spec((1, 16, step), lambda i: (s, tokens_here // 16 - back, i))

    rows_a_step = rows_here // all_steps
    packed, halo = kernel(
        open_kernel,
        "open",
        3,
        grid=(all_steps,),
        in_specs=[
            spec((rows_a_step, width_all), lambda i: (i, 0)),
            spec((rows_a_step, width_all), lambda i: (i, 0)),
            rows16(0, 1),
            last(1),
            last(2),
            rows16(1, TAPS // 16 + 1),
            rows16(2, TAPS // 16 + 1),
            deep(3, 3),
        ],
        out_specs=[
            spec((owners, 2, rows_a_step, channels), lambda i: (0, 0, i, 0)),
            wide(TAPS + 8),
        ],
        out_shape=[
            jax.ShapeDtypeStruct((owners, 2, rows_here, channels), bf16),
            jax.ShapeDtypeStruct((TAPS + 8, channels), bf16),
        ],
        scratch_shapes=[padded(3)],
    )(cotangent, residual, streams, streams, streams, streams, streams, short_filter)
    halo = from_behind(halo, "dp", 1)
    received = lax.all_to_all(packed, "tensor", split_axis=0, concat_axis=0, tiled=True)

    band_shape = jax.ShapeDtypeStruct((groups, BLOCK, SPAN), bf16)
    each = min(groups, 16)
    ahead_bands, behind_bands = kernel(
        bands_kernel,
        "bands",
        5,
        grid=(groups // each,),
        in_specs=[spec((each, TAPS), lambda i: (i, 0))],
        out_specs=[spec((each, BLOCK, SPAN), lambda i: (i, 0, 0))] * 2,
        out_shape=[band_shape] * 2,
    )(long_filter)

    output, mixed, gated = kernel(
        forward_kernel,
        "forward",
        5,
        grid=(all_steps,),
        in_specs=[deep(3, tokens_here), wide(TAPS + 8), deep(3, 3), wide(1), bands_of()],
        out_specs=[wide(tokens_here)] * 3,
        out_shape=[jax.ShapeDtypeStruct((tokens_here, channels), t) for t in (bf16, f32, bf16)],
        scratch_shapes=[padded(3)],
    )(streams, halo, short_filter, skip_row, ahead_bands)
    stats = kernel(
        stats_kernel,
        "stats",
        2,
        grid=(all_steps,),
        in_specs=[arrived(), wide(tokens_here), wide(1)],
        out_specs=spec((2, tokens_here), lambda i: (0, 0)),
        out_shape=jax.ShapeDtypeStruct((2, tokens_here), f32),
        scratch_shapes=[pltpu.VMEM((tokens_here, LANES), f32)] * 2,
    )(received, output, gain_here)
    stats = lax.psum(stats, "tensor")
    stats, leaving = lax.optimization_barrier((stats, output))
    rows_received = lax.all_to_all(
        leaving.reshape(owners, rows_here, channels), "tensor", split_axis=0, concat_axis=0, tiled=True
    )

    grads, inner, after, shares = [], [], [], []
    for k in range(chunks):
        grad_k, inner_k, first_k, share_k = kernel(
            functools.partial(head_kernel, width_all),
            "head",
            2,
            grid=(steps,),
            in_specs=[
                deep(1, tokens_here, k * steps),
                spec((1, 16, step), lambda i, k=k: (1, 0, i + k * steps)),
                spec((1, 16, step), lambda i, k=k: (2, 0, i + k * steps)),
                wide(TAPS + 8, k * steps),
                deep(3, 3, k * steps),
                wide(1, k * steps),
                spec((step // WIDTH, TAPS), lambda i, k=k: (i + k * steps, 0)),
                spec((2, tokens_here), lambda i: (0, 0)),
                arrived(k * steps),
                wide(tokens_here, k * steps),
                wide(1, k * steps),
                spec((16, step), lambda i, k=k: (0, i + k * steps)),
            ],
            out_specs=[wide(tokens_here), wide(tokens_here), wide(TAPS + 16), wide(1)],
            out_shape=[
                jax.ShapeDtypeStruct((tokens_here, part), bf16),
                jax.ShapeDtypeStruct((tokens_here, part), bf16),
                jax.ShapeDtypeStruct((TAPS + 16, part), bf16),
                jax.ShapeDtypeStruct((1, part), f32),
            ],
            scratch_shapes=[padded()] + [pltpu.VMEM((tokens_here, LANES), f32)] * 2,
        )(streams, streams, streams, halo, short_filter, skip_row, long_filter, stats, received, output, gain_here, mixed)
        grads.append(grad_k)
        inner.append(inner_k)
        shares.append(share_k)
        after.append(from_behind(first_k, "dp", -1))

    early = []
    for k in range(chunks):
        early.append(
            kernel(
                sums_kernel,
                "sums",
                4,
                grid=(steps,),
                in_specs=[
                    deep(1, tokens_here, k * steps),
                    wide(TAPS + 8, k * steps),
                    wide(tokens_here, k * steps),
                    wide(tokens_here),
                    wide(tokens_here),
                    wide(tokens_here, k * steps),
                    wide(1),
                ],
                out_specs=spec((cols * 16, LANES), lambda i: (i, 0)),
                out_shape=jax.ShapeDtypeStruct((part // LANES * 16, LANES), f32),
                scratch_shapes=[padded()],
            )(streams, halo, gated, inner[k], grads[k], mixed, shares[k])
        )
    block = min(rows_here, 16)
    by_rows = spec((block, width_all), lambda i: (i, 0))
    normed, grad_residual = kernel(
        norm_kernel,
        "norm",
        4,
        grid=(rows_here // block,),
        in_specs=[
            spec((owners, block, channels), lambda i: (0, i, 0)),
            by_rows,
            by_rows,
            spec((1, width_all), lambda i: (0, 0)),
        ],
        out_specs=[by_rows, by_rows],
        out_shape=[jax.ShapeDtypeStruct(residual.shape, bf16)] * 2,
        scratch_shapes=[pltpu.VMEM((block, width_all), f32)],
    )(rows_received, residual, cotangent, gain_row)

    stream_grad, late = None, []
    for k in range(chunks):
        aliased = stream_grad is not None
        operands = [streams, halo, short_filter, skip_row, behind_bands, grads[k], mixed, inner[k], after[k]]
        in_specs = [
            deep(3, tokens_here, k * steps),
            wide(TAPS + 8, k * steps),
            deep(3, 3, k * steps),
            wide(1, k * steps),
            bands_of(k * steps),
            wide(tokens_here),
            wide(tokens_here, k * steps),
            wide(tokens_here),
            wide(TAPS + 16),
        ]
        if aliased:
            operands.append(stream_grad)
            in_specs.append(spec(memory_space=pl.ANY))
        stream_grad, late_k = kernel(
            functools.partial(backward_kernel, aliased),
            "backward",
            5,
            grid=(steps,),
            in_specs=in_specs,
            out_specs=[
                deep(3, tokens_here, k * steps),
                spec((cols * 8, LANES), lambda i: (i, 0)),
            ],
            out_shape=[
                jax.ShapeDtypeStruct(streams.shape, bf16),
                jax.ShapeDtypeStruct((part // LANES * 8, LANES), f32),
            ],
            scratch_shapes=[padded(3), padded(3)],
            input_output_aliases={len(operands) - 1: 0} if aliased else {},
        )(*operands)
        late.append(late_k)
    mine, other = exchange_sum(jnp.concatenate(early + late, axis=0), "dp")
    long_grad, short_grad, skip_grad, gain_grad = kernel(
        close_kernel,
        "close",
        1,
        out_shape=[
            jax.ShapeDtypeStruct((groups, TAPS), f32),
            jax.ShapeDtypeStruct((3, 3, channels), f32),
            jax.ShapeDtypeStruct((1, channels), f32),
            jax.ShapeDtypeStruct((1, channels), f32),
        ],
    )(mine, other)
    skip_grad, gain_grad = skip_grad.reshape(channels), gain_grad.reshape(channels)
    return (normed, grad_residual, stream_grad, long_grad, short_grad, skip_grad, gain_grad)


def solution(mesh):
    placed = (
        P(("dp", "tensor"), None),
        P(None, "dp", "tensor"),
        P(None, None, "tensor"),
        P("tensor", None),
        P("tensor"),
        P(),
        P(("dp", "tensor"), None),
    )
    return jax.shard_map(
        local,
        mesh=mesh,
        in_specs=placed,
        out_specs=(
            P(("dp", "tensor"), None),
            P(("dp", "tensor"), None),
            P(None, "dp", "tensor"),
            P("tensor", None),
            P(None, None, "tensor"),
            P("tensor"),
            P("tensor"),
        ),
        check_vma=False,
    )
```

```python
import functools

import jax
import jax.numpy as jnp
from jax import lax
from jax.experimental import pallas as pl
from jax.experimental.pallas import tpu as pltpu
from jax.sharding import PartitionSpec as P

norm_eps = 1e-05
LANES = 128
TAPS = 128
WIDTH = 16
PER = LANES // WIDTH
BLOCK = 64
SPAN = 256
VMEM_LIMIT = 62
SMALL_LIMIT = 8
f32 = jnp.float32
bf16 = jnp.bfloat16


def params(limit):
    return pltpu.CompilerParams(vmem_limit_bytes=limit * 2**20)


def dot(a, b):
    return lax.dot_general(a, b, (((1,), (0,)), ((), ())), preferred_element_type=f32)


def dot_nt(a, b):
    return lax.dot_general(a, b, (((1,), (1,)), ((), ())), preferred_element_type=f32)


def lane_group(shape):
    return lax.broadcasted_iota(jnp.int32, shape, len(shape) - 1) % LANES // WIDTH


def pick_groups(stacked, rows):
    out = stacked[:rows]
    which = lane_group(out.shape)
    for g in range(1, PER):
        out = jnp.where(which == g, stacked[g * rows : (g + 1) * rows], out)
    return out


def shifted(scratch, halo, current):
    length = current.shape[0]
    scratch[6:8, :] = halo
    scratch[8 : 8 + length, :] = current
    return scratch[7 : 7 + length, :], scratch[6 : 6 + length, :]


def band(row, first, rows):
    wide = jnp.concatenate([row, jnp.zeros((1, SPAN - TAPS), f32)], axis=1)
    return pltpu.roll(jnp.broadcast_to(wide, (rows, SPAN)), first, 1, stride=1, stride_axis=0).astype(bf16)


def anti_identity(size):
    total = lax.broadcasted_iota(jnp.int32, (size, size), 0) + lax.broadcasted_iota(jnp.int32, (size, size), 1)
    return jnp.where(total == size - 1, 1.0, 0.0).astype(bf16)


def windows(extended, length):
    return jnp.concatenate([extended[at : at + SPAN] for at in range(0, length, BLOCK)], axis=1)


def convolve(bands, extended, length, rows=BLOCK):
    stacked = dot(bands.reshape(PER * rows, SPAN), windows(extended, length))
    result = pick_groups(stacked, rows)
    return [result[:, at : at + LANES] for at in range(0, result.shape[1], LANES)]


def bands_kernel(filter_ref, ahead_ref, behind_ref):
    half = filter_ref[...].astype(bf16)
    back = dot(half, anti_identity(TAPS))
    fore = half.astype(f32)
    for g in range(half.shape[0]):
        ahead_ref[g] = band(back[g : g + 1], SPAN - TAPS - BLOCK + 1, BLOCK)
        behind_ref[g] = band(fore[g : g + 1], 0, BLOCK)


def open_kernel(
    cot_ref, residual_ref, streams_ref, taps_ref, packed_ref, halo_ref, pieces, ends, rows, scratch, in_sem, out_sem, end_sem
):
    owners, _, _, channels = packed_ref.shape
    length = streams_ref.shape[1]
    back = ends.shape[1]
    ending = pltpu.make_async_copy(streams_ref.at[:, pl.ds(length - back, back), :], ends, end_sem.at[0])
    ending.start()
    places = [(j, which) for j in range(owners) for which in range(2)]
    arriving = [
        pltpu.make_async_copy(
            (cot_ref, residual_ref)[which].at[:, pl.ds(j * channels, channels)], pieces.at[j, which], in_sem.at[j, which]
        )
        for j, which in places
    ]
    leaving = [
        pltpu.make_async_copy(pieces.at[j, which], packed_ref.at[j, which], out_sem.at[j, which]) for j, which in places
    ]
    for copy in arriving:
        copy.start()
    ending.wait()
    for col in range(channels // LANES):
        lanes = slice(col * LANES, (col + 1) * LANES)
        features = []
        for s in (1, 2):
            scratch[s, 0:back, :] = ends[s, :, lanes].astype(f32)
            taps = taps_ref[s, :, lanes]
            now, one, two = (scratch[s, back - TAPS - n : back - n, :] for n in range(3))
            features.append(taps[0:1] * now + taps[1:2] * one + taps[2:3] * two)
        rows[:TAPS, lanes] = (features[0] * features[1]).astype(bf16)
        edges = scratch.at[0]
        edges[0:2, :] = ends[0, back - 16 : back, lanes].astype(f32)[14:]
        edges[2:4, :] = scratch[1, back - 2 : back, :]
        edges[4:6, :] = scratch[2, back - 2 : back, :]
        edges[6:8, :] = jnp.zeros((2, LANES), f32)
        rows[TAPS : TAPS + 8, lanes] = edges[0:8, :].astype(bf16)
        if col == 0:
            for copy, onward in zip(arriving, leaving):
                copy.wait()
                onward.start()
    ending = pltpu.make_async_copy(rows, halo_ref, end_sem.at[1])
    ending.start()
    for copy in leaving:
        copy.wait()
    ending.wait()


def edge(halo_ref, s, lanes):
    return halo_ref[TAPS : TAPS + 8, lanes].astype(f32)[2 * s : 2 * s + 2]


def feature(scratch, halo_ref, streams_ref, taps_ref, s, lanes, index):
    now = streams_ref[index, :, lanes].astype(f32)
    one, two = shifted(scratch, edge(halo_ref, s, lanes), now)
    taps = taps_ref[s, :, lanes]
    return taps[0:1] * now + taps[1:2] * one + taps[2:3] * two


def forward_kernel(streams_ref, halo_ref, taps_ref, skip_ref, ahead_ref, output_ref, mixed_ref, gated_ref, scratch):
    length = streams_ref.shape[1]
    for col in range(streams_ref.shape[2] // LANES):
        lanes = slice(col * LANES, (col + 1) * LANES)
        f0, f1, f2 = (feature(scratch.at[s], halo_ref, streams_ref, taps_ref, s, lanes, s) for s in range(3))
        gated = (f1 * f2).astype(bf16)
        gated_ref[:, lanes] = gated
        zero = jnp.zeros((SPAN - TAPS - BLOCK, LANES), bf16)
        extended = jnp.concatenate([zero, halo_ref[:TAPS, lanes], gated], axis=0)
        skip = skip_ref[:, lanes]
        for b, result in enumerate(convolve(ahead_ref[col * PER : (col + 1) * PER], extended, length)):
            rows = slice(b * BLOCK, (b + 1) * BLOCK)
            mixed = result + skip * gated[rows].astype(f32)
            mixed_ref[rows, lanes] = mixed
            output_ref[rows, lanes] = (f0[rows] * mixed).astype(bf16)


def columns_of(received_ref, which, lanes):
    piece = received_ref[:, which, :, lanes].astype(f32)
    return piece.reshape(piece.shape[0] * piece.shape[1], LANES)


def stats_kernel(received_ref, output_ref, gain_ref, stats_ref, squares_ref, products_ref):
    @pl.when(pl.program_id(0) == 0)
    def _():
        squares_ref[...] = jnp.zeros_like(squares_ref)
        products_ref[...] = jnp.zeros_like(products_ref)

    squares, products = squares_ref[...], products_ref[...]
    for col in range(output_ref.shape[1] // LANES):
        lanes = slice(col * LANES, (col + 1) * LANES)
        summed = columns_of(received_ref, 1, lanes) + output_ref[:, lanes].astype(f32)
        squares = squares + summed * summed
        products = products + columns_of(received_ref, 0, lanes) * gain_ref[:, lanes] * summed
    squares_ref[...] = squares
    products_ref[...] = products

    @pl.when(pl.program_id(0) == pl.num_programs(0) - 1)
    def _():
        for row, sums in ((0, squares), (1, products)):
            stats_ref[row : row + 1, :] = jnp.sum(sums.T, axis=0, keepdims=True)


def norm_kernel(received_ref, residual_ref, cot_ref, gain_ref, normed_ref, grad_ref, summed_ref):
    sources, rows, part = received_ref.shape
    width_all = residual_ref.shape[1]
    squares = jnp.zeros((rows, LANES), f32)
    products = jnp.zeros((rows, LANES), f32)
    for s in range(sources):
        where = slice(s * part, (s + 1) * part)
        summed = residual_ref[:, where].astype(f32) + received_ref[s].astype(f32)
        summed_ref[:, where] = summed
        scaled = cot_ref[:, where].astype(f32) * gain_ref[:, where]
        both = (summed * summed, scaled * summed)
        for col in range(part // LANES):
            lanes = slice(col * LANES, (col + 1) * LANES)
            squares = squares + both[0][:, lanes]
            products = products + both[1][:, lanes]
    inverse = lax.rsqrt(jnp.sum(squares, axis=1, keepdims=True) / width_all + norm_eps)
    along = inverse * jnp.sum(products, axis=1, keepdims=True) / width_all
    for s in range(sources):
        where = slice(s * part, (s + 1) * part)
        unit = summed_ref[:, where] * inverse
        gain = gain_ref[:, where]
        normed_ref[:, where] = (unit * gain).astype(bf16)
        grad_ref[:, where] = (inverse * (cot_ref[:, where].astype(f32) * gain - unit * along)).astype(bf16)


def head_kernel(
    width_all,
    aliased,
    streams_ref,
    first1_ref,
    first2_ref,
    halo_ref,
    taps_ref,
    skip_ref,
    filter_ref,
    stats_ref,
    received_ref,
    output_ref,
    gain_ref,
    mixed_ref,
    *refs,
):
    grad_ref, inner_ref, share_ref, first_ref, scratch, inverse_ref, along_ref = refs[3:] if aliased else refs

    @pl.when(pl.program_id(0) == 0)
    def _():
        tokens = stats_ref.shape[1]
        squares = jnp.broadcast_to(stats_ref[0:1, :], (LANES, tokens)).T
        products = jnp.broadcast_to(stats_ref[1:2, :], (LANES, tokens)).T
        inverse = lax.rsqrt(squares / width_all + norm_eps)
        inverse_ref[...] = inverse
        along_ref[...] = inverse * products / width_all

    inverse, along = inverse_ref[...], along_ref[...]
    for col in range(streams_ref.shape[2] // LANES):
        lanes = slice(col * LANES, (col + 1) * LANES)
        cot = columns_of(received_ref, 0, lanes)
        unit = (columns_of(received_ref, 1, lanes) + output_ref[:, lanes].astype(f32)) * inverse
        share_ref[:, lanes] = jnp.sum(cot * unit, axis=0, keepdims=True)
        grad_half = (inverse * (cot * gain_ref[:, lanes] - unit * along)).astype(bf16)
        grad_ref[:, lanes] = grad_half
        grad = grad_half.astype(f32)
        f0 = feature(scratch, halo_ref, streams_ref, taps_ref, 0, lanes, 0)
        inner = (grad * f0).astype(bf16)
        inner_ref[:, lanes] = inner
        first_ref[:TAPS, lanes] = inner[:TAPS]
        features = []
        for s, top in ((1, first1_ref), (2, first2_ref)):
            taps = taps_ref[s, :, lanes]
            now = top[0, :, lanes].astype(f32)
            scratch[6:8, :] = edge(halo_ref, s, lanes)
            scratch[8:24, :] = now
            features.append(taps[0:1] * now[:8] + taps[1:2] * scratch[7:15, :] + taps[2:3] * scratch[6:14, :])
        half = filter_ref[col * PER : (col + 1) * PER].astype(bf16).astype(f32)
        bands = jnp.stack([band(half[g : g + 1], 0, 16) for g in range(PER)])
        conv = convolve(bands, inner, BLOCK, 16)[0][:8]
        grad_gated = conv + skip_ref[:, lanes] * inner[:16].astype(f32)[:8]
        scratch[0:2, :] = (grad[:8] * mixed_ref[0:8, lanes])[:2]
        scratch[2:4, :] = (grad_gated * features[1])[:2]
        scratch[4:6, :] = (grad_gated * features[0])[:2]
        scratch[6:8, :] = jnp.zeros((2, LANES), f32)
        rows = scratch[0:8, :]
        high = rows.astype(bf16)
        first_ref[TAPS : TAPS + 8, lanes] = high
        first_ref[TAPS + 8 : TAPS + 16, lanes] = (rows - high.astype(f32)).astype(bf16)


def sums_kernel(streams_ref, halo_ref, gated_ref, inner_ref, grad_ref, mixed_ref, gain_ref, early_ref, scratch):
    length = streams_ref.shape[1]
    blocks = length // BLOCK
    flip = anti_identity(SPAN)
    which = lane_group((BLOCK, blocks * LANES))
    masks = [jnp.where(which == g, 1.0, 0.0).astype(bf16) for g in range(PER)]
    zero = jnp.zeros((SPAN - TAPS - BLOCK, LANES), bf16)
    for col in range(streams_ref.shape[2] // LANES):
        lanes = slice(col * LANES, (col + 1) * LANES)
        gated = gated_ref[:, lanes]
        inner = inner_ref[:, lanes]
        extended = jnp.concatenate([zero, halo_ref[:TAPS, lanes], gated], axis=0)
        backward = dot(flip, windows(extended, length)).astype(bf16)
        grads = jnp.concatenate([inner[at : at + BLOCK] for at in range(0, length, BLOCK)], axis=1)
        pairs = dot_nt(jnp.concatenate([grads * mask for mask in masks], axis=0), backward)
        base = col * 16
        for g in range(PER):
            skewed = pltpu.roll(pairs[g * BLOCK : (g + 1) * BLOCK], SPAN - BLOCK + 1, 1, stride=1, stride_axis=0)
            early_ref[base + g : base + g + 1, :] = jnp.sum(skewed[:, :TAPS], axis=0, keepdims=True)
        early_ref[base + 8 : base + 9, :] = jnp.sum(inner.astype(f32) * gated.astype(f32), axis=0, keepdims=True)
        early_ref[base + 9 : base + 10, :] = gain_ref[:, lanes]
        grad_query = grad_ref[:, lanes].astype(f32) * mixed_ref[:, lanes]
        now = streams_ref[0, :, lanes].astype(f32)
        one, two = shifted(scratch, edge(halo_ref, 0, lanes), now)
        for j, shift in enumerate((now, one, two)):
            early_ref[base + 10 + j : base + 11 + j, :] = jnp.sum(grad_query * shift, axis=0, keepdims=True)
        early_ref[base + 13 : base + 16, :] = jnp.zeros((3, LANES), f32)


def backward_kernel(
    aliased,
    streams_ref,
    halo_ref,
    taps_ref,
    skip_ref,
    behind_ref,
    grad_ref,
    mixed_ref,
    inner_ref,
    after_ref,
    *refs,
):
    stream_grad_ref, late_ref, scratch, ahead = refs[2:] if aliased else refs
    length = streams_ref.shape[1]
    for col in range(streams_ref.shape[2] // LANES):
        lanes = slice(col * LANES, (col + 1) * LANES)
        inner = inner_ref[:, lanes]
        zero = jnp.zeros((SPAN - TAPS - BLOCK, LANES), bf16)
        extended = jnp.concatenate([inner, after_ref[:TAPS, lanes], zero], axis=0)
        parts = convolve(behind_ref[col * PER : (col + 1) * PER], extended, length)
        grad_gated = jnp.concatenate(parts, axis=0) + skip_ref[:, lanes] * inner.astype(f32)
        shifts, features = {}, {}
        for s in (1, 2):
            now = streams_ref[s, :, lanes].astype(f32)
            one, two = shifted(scratch.at[s], edge(halo_ref, s, lanes), now)
            taps = taps_ref[s, :, lanes]
            shifts[s] = (now, one, two)
            features[s] = taps[0:1] * now + taps[1:2] * one + taps[2:3] * two
        grads = (
            grad_ref[:, lanes].astype(f32) * mixed_ref[:, lanes],
            grad_gated * features[2],
            grad_gated * features[1],
        )
        following = after_ref[TAPS : TAPS + 16, lanes].astype(f32)
        following = following[:8] + following[8:]
        for s in range(3):
            ahead[s, 0:length, :] = grads[s]
            ahead[s, length : length + 2, :] = following[2 * s : 2 * s + 2]
            taps = taps_ref[s, :, lanes]
            stream_grad_ref[s, :, lanes] = (
                taps[0:1] * grads[s] + taps[1:2] * ahead[s, 1 : length + 1, :] + taps[2:3] * ahead[s, 2 : length + 2, :]
            ).astype(bf16)
        for s in (1, 2):
            for j in range(3):
                row = col * 8 + (s - 1) * 3 + j
                late_ref[row : row + 1, :] = jnp.sum(grads[s] * shifts[s][j], axis=0, keepdims=True)
        late_ref[col * 8 + 6 : col * 8 + 8, :] = jnp.zeros((2, LANES), f32)


def from_behind(value, axis, steps):
    count = lax.axis_size(axis)
    first, last = (max(0, -steps), min(count, count - steps))
    return lax.ppermute(value, axis, [(source, source + steps) for source in range(first, last)])


def exchange(value, other, axis, reach):
    if other is not None:
        value = value + other.astype(f32)
    value = lax.reduce_precision(value, 8, 7)
    count = lax.axis_size(axis)
    return value, lax.ppermute(value.astype(bf16), axis, [(i, i ^ reach) for i in range(count)])


def close_kernel(
    early_ref, early_other_ref, late_ref, late_other_ref, long_ref, short_ref, skip_ref, gain_ref
):
    early = early_ref[...] + early_other_ref[...].astype(f32)
    late = late_ref[...] + late_other_ref[...].astype(f32)
    for col in range(skip_ref.shape[1] // LANES):
        lanes = slice(col * LANES, (col + 1) * LANES)
        at = col * 16
        long_ref[col * PER : (col + 1) * PER, :] = early[at : at + PER]
        skip_ref[:, lanes] = early[at + 8 : at + 9]
        gain_ref[:, lanes] = early[at + 9 : at + 10]
        for j in range(3):
            short_ref[0, j : j + 1, lanes] = early[at + 10 + j : at + 11 + j]
            for s in (1, 2):
                row = col * 8 + (s - 1) * 3 + j
                short_ref[s, j : j + 1, lanes] = late[row : row + 1]


def local(residual, streams, short_filter, long_filter, skip, gain, cotangent):
    tokens_here, channels = streams.shape[1:]
    groups = long_filter.shape[0]
    rows_here, width_all = residual.shape
    owners = lax.axis_size("tensor")
    assert long_filter.shape[1] == TAPS and channels == groups * WIDTH and tokens_here % (2 * TAPS) == 0
    chunks = 1
    part = channels // chunks
    step = min(part, 512)
    steps, all_steps = part // step, channels // step
    cols = step // LANES
    skip_row = skip[None, :]
    gain_row = gain[None, :]
    gain_here = lax.dynamic_slice_in_dim(gain, lax.axis_index("tensor") * channels, channels)[None, :]

    spec = pl.BlockSpec

    def wide(rows, offset=0):
        return spec((rows, step), lambda i: (0, i + offset))

    def deep(first, rows, offset=0):
        return spec((first, rows, step), lambda i: (0, 0, i + offset))

    def bands_of(offset=0):
        return spec((step // WIDTH, BLOCK, SPAN), lambda i: (i + offset, 0, 0))

    def arrived(offset=0):
        return spec((owners, 2, rows_here, step), lambda i: (0, 0, 0, i + offset))

    def padded(count=None):
        shape = (tokens_here + 8, LANES)
        return pltpu.VMEM(shape if count is None else (count,) + shape, f32)

    def kernel(body, name, micros, limit=VMEM_LIMIT, **how):
        return pl.pallas_call(
            body,
            compiler_params=params(limit),
            cost_estimate=pl.CostEstimate(flops=0, bytes_accessed=micros * 1000, transcendentals=0),
            name=name,
            **how,
        )

    packed, halo = kernel(
        open_kernel,
        "open",
        3,
        in_specs=[spec(memory_space=pl.ANY)] * 3 + [spec(memory_space=pltpu.VMEM)],
        out_specs=[spec(memory_space=pl.ANY)] * 2,
        out_shape=[
            jax.ShapeDtypeStruct((owners, 2, rows_here, channels), bf16),
            jax.ShapeDtypeStruct((TAPS + 8, channels), bf16),
        ],
        scratch_shapes=[
            pltpu.VMEM((owners, 2, rows_here, channels), bf16),
            pltpu.VMEM((3, TAPS + 16, channels), bf16),
            pltpu.VMEM((TAPS + 8, channels), bf16),
            pltpu.VMEM((3, TAPS + 16, LANES), f32),
            pltpu.SemaphoreType.DMA((owners, 2)),
            pltpu.SemaphoreType.DMA((owners, 2)),
            pltpu.SemaphoreType.DMA((2,)),
        ],
    )(cotangent, residual, streams, short_filter)
    halo = from_behind(halo, "dp", 1)
    received = lax.all_to_all(packed, "tensor", split_axis=0, concat_axis=0, tiled=True)

    band_shape = jax.ShapeDtypeStruct((groups, BLOCK, SPAN), bf16)
    each = min(groups, 16)
    ahead_bands, behind_bands = kernel(
        bands_kernel,
        "bands",
        5,
        grid=(groups // each,),
        in_specs=[spec((each, TAPS), lambda i: (i, 0))],
        out_specs=[spec((each, BLOCK, SPAN), lambda i: (i, 0, 0))] * 2,
        out_shape=[band_shape] * 2,
    )(long_filter)

    output, mixed, gated = kernel(
        forward_kernel,
        "forward",
        5,
        grid=(all_steps,),
        in_specs=[deep(3, tokens_here), wide(TAPS + 8), deep(3, 3), wide(1), bands_of()],
        out_specs=[wide(tokens_here)] * 3,
        out_shape=[jax.ShapeDtypeStruct((tokens_here, channels), t) for t in (bf16, f32, bf16)],
        scratch_shapes=[padded(3)],
    )(streams, halo, short_filter, skip_row, ahead_bands)
    stats = kernel(
        stats_kernel,
        "stats",
        2,
        grid=(all_steps,),
        in_specs=[arrived(), wide(tokens_here), wide(1)],
        out_specs=spec((2, tokens_here), lambda i: (0, 0)),
        out_shape=jax.ShapeDtypeStruct((2, tokens_here), f32),
        scratch_shapes=[pltpu.VMEM((tokens_here, LANES), f32)] * 2,
    )(received, output, gain_here)
    stats = lax.psum(stats, "tensor")
    stats, leaving = lax.optimization_barrier((stats, output))
    rows_received = lax.all_to_all(
        leaving.reshape(owners, rows_here, channels), "tensor", split_axis=0, concat_axis=0, tiled=True
    )

    after, filled = [], []
    for k in range(chunks):
        grads, inner, shares, first = kernel(
            functools.partial(head_kernel, width_all, bool(filled)),
            "head",
            2,
            grid=(steps,),
            in_specs=[
                deep(1, tokens_here, k * steps),
                spec((1, 16, step), lambda i, k=k: (1, 0, i + k * steps)),
                spec((1, 16, step), lambda i, k=k: (2, 0, i + k * steps)),
                wide(TAPS + 8, k * steps),
                deep(3, 3, k * steps),
                wide(1, k * steps),
                spec((step // WIDTH, TAPS), lambda i, k=k: (i + k * steps, 0)),
                spec((2, tokens_here), lambda i: (0, 0)),
                arrived(k * steps),
                wide(tokens_here, k * steps),
                wide(1, k * steps),
                spec((16, step), lambda i, k=k: (0, i + k * steps)),
            ]
            + [spec(memory_space=pl.ANY)] * len(filled),
            out_specs=[
                wide(tokens_here, k * steps),
                wide(tokens_here, k * steps),
                wide(1, k * steps),
                wide(TAPS + 16),
            ],
            out_shape=[
                jax.ShapeDtypeStruct((tokens_here, channels), bf16),
                jax.ShapeDtypeStruct((tokens_here, channels), bf16),
                jax.ShapeDtypeStruct((1, channels), f32),
                jax.ShapeDtypeStruct((TAPS + 16, part), bf16),
            ],
            scratch_shapes=[padded()] + [pltpu.VMEM((tokens_here, LANES), f32)] * 2,
            input_output_aliases={12 + n: n for n in range(len(filled))},
        )(
            *(streams, streams, streams, halo, short_filter, skip_row, long_filter, stats, received, output),
            *(gain_here, mixed, *filled),
        )
        filled = [grads, inner, shares]
        after.append(from_behind(first, "dp", -1))

    early = kernel(
        sums_kernel,
        "sums",
        8,
        grid=(all_steps,),
        in_specs=[
            deep(1, tokens_here),
            wide(TAPS + 8),
            wide(tokens_here),
            wide(tokens_here),
            wide(tokens_here),
            wide(tokens_here),
            wide(1),
        ],
        out_specs=spec((cols * 16, LANES), lambda i: (i, 0)),
        out_shape=jax.ShapeDtypeStruct((channels // LANES * 16, LANES), f32),
        scratch_shapes=[padded()],
    )(streams, halo, gated, inner, grads, mixed, shares)

    block = min(rows_here, 16)
    by_rows = spec((block, width_all), lambda i: (i, 0))
    normed, grad_residual = kernel(
        norm_kernel,
        "norm",
        4,
        grid=(rows_here // block,),
        in_specs=[
            spec((owners, block, channels), lambda i: (0, i, 0)),
            by_rows,
            by_rows,
            spec((1, width_all), lambda i: (0, 0)),
        ],
        out_specs=[by_rows, by_rows],
        out_shape=[jax.ShapeDtypeStruct(residual.shape, bf16)] * 2,
        scratch_shapes=[pltpu.VMEM((block, width_all), f32)],
    )(rows_received, residual, cotangent, gain_row)

    reaches = [1 << n for n in range((lax.axis_size("dp") - 1).bit_length())]
    waiting = list(reaches)
    early_other, filled = None, []
    for k in range(chunks):
        if waiting:
            early = early if early_other is None else early + early_other.astype(f32)
            early, after[k] = lax.optimization_barrier((early, after[k]))
            early, early_other = exchange(early, None, "dp", waiting.pop(0))
        stream_grad, late = kernel(
            functools.partial(backward_kernel, bool(filled)),
            "backward",
            5,
            grid=(steps,),
            in_specs=[
                deep(3, tokens_here, k * steps),
                wide(TAPS + 8, k * steps),
                deep(3, 3, k * steps),
                wide(1, k * steps),
                bands_of(k * steps),
                wide(tokens_here, k * steps),
                wide(tokens_here, k * steps),
                wide(tokens_here, k * steps),
                wide(TAPS + 16),
            ]
            + [spec(memory_space=pl.ANY)] * len(filled),
            out_specs=[
                deep(3, tokens_here, k * steps),
                spec((cols * 8, LANES), lambda i, k=k: (i + k * steps, 0)),
            ],
            out_shape=[
                jax.ShapeDtypeStruct(streams.shape, bf16),
                jax.ShapeDtypeStruct((channels // LANES * 8, LANES), f32),
            ],
            scratch_shapes=[padded(3), padded(3)],
            input_output_aliases={9 + n: n for n in range(len(filled))},
        )(streams, halo, short_filter, skip_row, behind_bands, grads, mixed, inner, after[k], *filled)
        filled = [stream_grad, late]
    for reach in waiting:
        early, early_other = exchange(early, early_other, "dp", reach)
    late_other = None
    for reach in reaches:
        late, late_other = exchange(late, late_other, "dp", reach)
    late, normed, grad_residual = lax.optimization_barrier((late, normed, grad_residual))
    long_grad, short_grad, skip_grad, gain_grad = kernel(
        close_kernel,
        "close",
        1,
        SMALL_LIMIT,
        out_shape=[
            jax.ShapeDtypeStruct((groups, TAPS), f32),
            jax.ShapeDtypeStruct((3, 3, channels), f32),
            jax.ShapeDtypeStruct((1, channels), f32),
            jax.ShapeDtypeStruct((1, channels), f32),
        ],
    )(early, early_other, late, late_other)
    skip_grad, gain_grad = skip_grad.reshape(channels), gain_grad.reshape(channels)
    return (normed, grad_residual, stream_grad, long_grad, short_grad, skip_grad, gain_grad)


def solution(mesh):
    placed = (
        P(("dp", "tensor"), None),
        P(None, "dp", "tensor"),
        P(None, None, "tensor"),
        P("tensor", None),
        P("tensor"),
        P(),
        P(("dp", "tensor"), None),
    )
    return jax.shard_map(
        local,
        mesh=mesh,
        in_specs=placed,
        out_specs=(
            P(("dp", "tensor"), None),
            P(("dp", "tensor"), None),
            P(None, "dp", "tensor"),
            P("tensor", None),
            P(None, None, "tensor"),
            P("tensor"),
            P("tensor"),
        ),
        check_vma=False,
    )
```

```python
import functools

import jax
import jax.numpy as jnp
from jax import lax
from jax.experimental import pallas as pl
from jax.experimental.pallas import tpu as pltpu
from jax.sharding import PartitionSpec as P

norm_eps = 1e-05
LANES = 128
TAPS = 128
WIDTH = 16
PER = LANES // WIDTH
BLOCK = 64
SPAN = 256
VMEM_LIMIT = 62
SMALL_LIMIT = 8
NORM_LIMIT = 24
STEP = 512
f32 = jnp.float32
bf16 = jnp.bfloat16


def params(limit):
    return pltpu.CompilerParams(vmem_limit_bytes=limit * 2**20)


def dot(a, b):
    return lax.dot_general(a, b, (((1,), (0,)), ((), ())), preferred_element_type=f32)


def dot_nt(a, b):
    return lax.dot_general(a, b, (((1,), (1,)), ((), ())), preferred_element_type=f32)


def lane_group(shape):
    return lax.broadcasted_iota(jnp.int32, shape, len(shape) - 1) % LANES // WIDTH


def pick_groups(stacked, rows):
    out = stacked[:rows]
    which = lane_group(out.shape)
    for g in range(1, PER):
        out = jnp.where(which == g, stacked[g * rows : (g + 1) * rows], out)
    return out


def shifted(scratch, halo, current):
    length = current.shape[0]
    scratch[6:8, :] = halo
    scratch[8 : 8 + length, :] = current
    return scratch[7 : 7 + length, :], scratch[6 : 6 + length, :]


def band(row, first, rows):
    wide = jnp.concatenate([row, jnp.zeros((1, SPAN - TAPS), f32)], axis=1)
    return pltpu.roll(jnp.broadcast_to(wide, (rows, SPAN)), first, 1, stride=1, stride_axis=0).astype(bf16)


def anti_identity(size):
    total = lax.broadcasted_iota(jnp.int32, (size, size), 0) + lax.broadcasted_iota(jnp.int32, (size, size), 1)
    return jnp.where(total == size - 1, 1.0, 0.0).astype(bf16)


def windows(extended, length):
    return jnp.concatenate([extended[at : at + SPAN] for at in range(0, length, BLOCK)], axis=1)


def convolve(bands, extended, length, rows=BLOCK):
    stacked = dot(bands.reshape(PER * rows, SPAN), windows(extended, length))
    result = pick_groups(stacked, rows)
    return [result[:, at : at + LANES] for at in range(0, result.shape[1], LANES)]


def bands_kernel(filter_ref, ahead_ref, behind_ref):
    half = filter_ref[...].astype(bf16)
    back = dot(half, anti_identity(TAPS))
    fore = half.astype(f32)
    for g in range(half.shape[0]):
        ahead_ref[g] = band(back[g : g + 1], SPAN - TAPS - BLOCK + 1, BLOCK)
        behind_ref[g] = band(fore[g : g + 1], 0, BLOCK)


def open_kernel(
    cot_ref, residual_ref, streams_ref, taps_ref, packed_ref, halo_ref, pieces, ends, rows, scratch, in_sem, out_sem, end_sem
):
    owners, _, _, channels = packed_ref.shape
    length = streams_ref.shape[1]
    back = ends.shape[1]
    ending = pltpu.make_async_copy(streams_ref.at[:, pl.ds(length - back, back), :], ends, end_sem.at[0])
    ending.start()
    places = [(j, which) for j in range(owners) for which in range(2)]
    arriving = [
        pltpu.make_async_copy(
            (cot_ref, residual_ref)[which].at[:, pl.ds(j * channels, channels)], pieces.at[j, which], in_sem.at[j, which]
        )
        for j, which in places
    ]
    leaving = [
        pltpu.make_async_copy(pieces.at[j, which], packed_ref.at[j, which], out_sem.at[j, which]) for j, which in places
    ]
    for copy in arriving:
        copy.start()
    ending.wait()
    for col in range(channels // LANES):
        lanes = slice(col * LANES, (col + 1) * LANES)
        features = []
        for s in (1, 2):
            scratch[s, 0:back, :] = ends[s, :, lanes].astype(f32)
            taps = taps_ref[s, :, lanes]
            now, one, two = (scratch[s, back - TAPS - n : back - n, :] for n in range(3))
            features.append(taps[0:1] * now + taps[1:2] * one + taps[2:3] * two)
        rows[:TAPS, lanes] = (features[0] * features[1]).astype(bf16)
        edges = scratch.at[0]
        edges[0:2, :] = ends[0, back - 16 : back, lanes].astype(f32)[14:]
        edges[2:4, :] = scratch[1, back - 2 : back, :]
        edges[4:6, :] = scratch[2, back - 2 : back, :]
        edges[6:8, :] = jnp.zeros((2, LANES), f32)
        rows[TAPS : TAPS + 8, lanes] = edges[0:8, :].astype(bf16)
        if col == 0:
            for copy, onward in zip(arriving, leaving):
                copy.wait()
                onward.start()
    ending = pltpu.make_async_copy(rows, halo_ref, end_sem.at[1])
    ending.start()
    for copy in leaving:
        copy.wait()
    ending.wait()


def edge(halo_ref, s, lanes):
    return halo_ref[TAPS : TAPS + 8, lanes].astype(f32)[2 * s : 2 * s + 2]


def feature(scratch, halo_ref, streams_ref, taps_ref, s, lanes, index):
    now = streams_ref[index, :, lanes].astype(f32)
    one, two = shifted(scratch, edge(halo_ref, s, lanes), now)
    taps = taps_ref[s, :, lanes]
    return taps[0:1] * now + taps[1:2] * one + taps[2:3] * two


def forward_kernel(index, streams_ref, halo_ref, taps_ref, skip_ref, ahead_ref, output_ref, mixed_ref, gated_ref, scratch):
    length = streams_ref.shape[1]
    for col in range(streams_ref.shape[2] // LANES):
        lanes = slice(col * LANES, (col + 1) * LANES)
        f0, f1, f2 = (feature(scratch.at[s], halo_ref, streams_ref, taps_ref, s, lanes, s) for s in range(3))
        gated = (f1 * f2).astype(bf16)
        gated_ref[:, lanes] = gated
        zero = jnp.zeros((SPAN - TAPS - BLOCK, LANES), bf16)
        extended = jnp.concatenate([zero, halo_ref[:TAPS, lanes], gated], axis=0)
        skip = skip_ref[:, lanes]
        for b, result in enumerate(convolve(ahead_ref[col * PER : (col + 1) * PER], extended, length)):
            rows = slice(b * BLOCK, (b + 1) * BLOCK)
            mixed = result + skip * gated[rows].astype(f32)
            mixed_ref[rows, lanes] = mixed
            output_ref[rows, lanes] = (f0[rows] * mixed).astype(bf16)


def columns_of(received_ref, which, lanes):
    piece = received_ref[:, which, :, lanes].astype(f32)
    return piece.reshape(piece.shape[0] * piece.shape[1], LANES)


def stats_kernel(count, index, received_ref, output_ref, gain_ref, stats_ref, squares_ref, products_ref):
    @pl.when(index == 0)
    def _():
        squares_ref[...] = jnp.zeros_like(squares_ref)
        products_ref[...] = jnp.zeros_like(products_ref)

    squares, products = squares_ref[...], products_ref[...]
    for col in range(output_ref.shape[1] // LANES):
        lanes = slice(col * LANES, (col + 1) * LANES)
        summed = columns_of(received_ref, 1, lanes) + output_ref[:, lanes].astype(f32)
        squares = squares + summed * summed
        products = products + columns_of(received_ref, 0, lanes) * gain_ref[:, lanes] * summed
    squares_ref[...] = squares
    products_ref[...] = products

    @pl.when(index == count - 1)
    def _():
        for row, sums in ((0, squares), (1, products)):
            stats_ref[row : row + 1, :] = jnp.sum(sums.T, axis=0, keepdims=True)


def norm_kernel(received_ref, residual_ref, cot_ref, gain_ref, normed_ref, grad_ref, summed_ref):
    sources, rows, part = received_ref.shape
    width_all = residual_ref.shape[1]
    squares = jnp.zeros((rows, LANES), f32)
    products = jnp.zeros((rows, LANES), f32)
    for s in range(sources):
        where = slice(s * part, (s + 1) * part)
        summed = residual_ref[:, where].astype(f32) + received_ref[s].astype(f32)
        summed_ref[:, where] = summed
        scaled = cot_ref[:, where].astype(f32) * gain_ref[:, where]
        both = (summed * summed, scaled * summed)
        for col in range(part // LANES):
            lanes = slice(col * LANES, (col + 1) * LANES)
            squares = squares + both[0][:, lanes]
            products = products + both[1][:, lanes]
    inverse = lax.rsqrt(jnp.sum(squares, axis=1, keepdims=True) / width_all + norm_eps)
    along = inverse * jnp.sum(products, axis=1, keepdims=True) / width_all
    for s in range(sources):
        where = slice(s * part, (s + 1) * part)
        unit = summed_ref[:, where] * inverse
        gain = gain_ref[:, where]
        normed_ref[:, where] = (unit * gain).astype(bf16)
        grad_ref[:, where] = (inverse * (cot_ref[:, where].astype(f32) * gain - unit * along)).astype(bf16)


def head_kernel(
    width_all,
    index,
    streams_ref,
    first1_ref,
    first2_ref,
    halo_ref,
    taps_ref,
    skip_ref,
    filter_ref,
    stats_ref,
    received_ref,
    output_ref,
    gain_ref,
    mixed_ref,
    grad_ref,
    inner_ref,
    share_ref,
    first_ref,
    scratch,
    inverse_ref,
    along_ref,
):
    @pl.when(index == 0)
    def _():
        tokens = stats_ref.shape[1]
        squares = jnp.broadcast_to(stats_ref[0:1, :], (LANES, tokens)).T
        products = jnp.broadcast_to(stats_ref[1:2, :], (LANES, tokens)).T
        inverse = lax.rsqrt(squares / width_all + norm_eps)
        inverse_ref[...] = inverse
        along_ref[...] = inverse * products / width_all

    inverse, along = inverse_ref[...], along_ref[...]
    for col in range(streams_ref.shape[2] // LANES):
        lanes = slice(col * LANES, (col + 1) * LANES)
        cot = columns_of(received_ref, 0, lanes)
        unit = (columns_of(received_ref, 1, lanes) + output_ref[:, lanes].astype(f32)) * inverse
        share_ref[:, lanes] = jnp.sum(cot * unit, axis=0, keepdims=True)
        grad_half = (inverse * (cot * gain_ref[:, lanes] - unit * along)).astype(bf16)
        grad_ref[:, lanes] = grad_half
        grad = grad_half.astype(f32)
        f0 = feature(scratch, halo_ref, streams_ref, taps_ref, 0, lanes, 0)
        inner = (grad * f0).astype(bf16)
        inner_ref[:, lanes] = inner
        first_ref[:TAPS, lanes] = inner[:TAPS]
        features = []
        for s, top in ((1, first1_ref), (2, first2_ref)):
            taps = taps_ref[s, :, lanes]
            now = top[0, :, lanes].astype(f32)
            scratch[6:8, :] = edge(halo_ref, s, lanes)
            scratch[8:24, :] = now
            features.append(taps[0:1] * now[:8] + taps[1:2] * scratch[7:15, :] + taps[2:3] * scratch[6:14, :])
        half = filter_ref[col * PER : (col + 1) * PER].astype(bf16).astype(f32)
        bands = jnp.stack([band(half[g : g + 1], 0, 16) for g in range(PER)])
        conv = convolve(bands, inner, BLOCK, 16)[0][:8]
        grad_gated = conv + skip_ref[:, lanes] * inner[:16].astype(f32)[:8]
        scratch[0:2, :] = (grad[:8] * mixed_ref[0:8, lanes])[:2]
        scratch[2:4, :] = (grad_gated * features[1])[:2]
        scratch[4:6, :] = (grad_gated * features[0])[:2]
        scratch[6:8, :] = jnp.zeros((2, LANES), f32)
        rows = scratch[0:8, :]
        high = rows.astype(bf16)
        first_ref[TAPS : TAPS + 8, lanes] = high
        first_ref[TAPS + 8 : TAPS + 16, lanes] = (rows - high.astype(f32)).astype(bf16)


def sums_kernel(index, streams_ref, halo_ref, gated_ref, inner_ref, grad_ref, mixed_ref, gain_ref, early_ref, scratch):
    length = streams_ref.shape[1]
    blocks = length // BLOCK
    flip = anti_identity(SPAN)
    which = lane_group((BLOCK, blocks * LANES))
    masks = [jnp.where(which == g, 1.0, 0.0).astype(bf16) for g in range(PER)]
    zero = jnp.zeros((SPAN - TAPS - BLOCK, LANES), bf16)
    for col in range(streams_ref.shape[2] // LANES):
        lanes = slice(col * LANES, (col + 1) * LANES)
        gated = gated_ref[:, lanes]
        inner = inner_ref[:, lanes]
        extended = jnp.concatenate([zero, halo_ref[:TAPS, lanes], gated], axis=0)
        backward = dot(flip, windows(extended, length)).astype(bf16)
        grads = jnp.concatenate([inner[at : at + BLOCK] for at in range(0, length, BLOCK)], axis=1)
        pairs = dot_nt(jnp.concatenate([grads * mask for mask in masks], axis=0), backward)
        base = col * 16
        for g in range(PER):
            skewed = pltpu.roll(pairs[g * BLOCK : (g + 1) * BLOCK], SPAN - BLOCK + 1, 1, stride=1, stride_axis=0)
            early_ref[base + g : base + g + 1, :] = jnp.sum(skewed[:, :TAPS], axis=0, keepdims=True)
        early_ref[base + 8 : base + 9, :] = jnp.sum(inner.astype(f32) * gated.astype(f32), axis=0, keepdims=True)
        early_ref[base + 9 : base + 10, :] = gain_ref[:, lanes]
        grad_query = grad_ref[:, lanes].astype(f32) * mixed_ref[:, lanes]
        now = streams_ref[0, :, lanes].astype(f32)
        one, two = shifted(scratch, edge(halo_ref, 0, lanes), now)
        for j, shift in enumerate((now, one, two)):
            early_ref[base + 10 + j : base + 11 + j, :] = jnp.sum(grad_query * shift, axis=0, keepdims=True)
        early_ref[base + 13 : base + 16, :] = jnp.zeros((3, LANES), f32)


def backward_kernel(
    index,
    streams_ref,
    halo_ref,
    taps_ref,
    skip_ref,
    behind_ref,
    grad_ref,
    mixed_ref,
    inner_ref,
    after_ref,
    stream_grad_ref,
    late_ref,
    scratch,
    ahead,
):
    length = streams_ref.shape[1]
    for col in range(streams_ref.shape[2] // LANES):
        lanes = slice(col * LANES, (col + 1) * LANES)
        inner = inner_ref[:, lanes]
        zero = jnp.zeros((SPAN - TAPS - BLOCK, LANES), bf16)
        extended = jnp.concatenate([inner, after_ref[:TAPS, lanes], zero], axis=0)
        parts = convolve(behind_ref[col * PER : (col + 1) * PER], extended, length)
        grad_gated = jnp.concatenate(parts, axis=0) + skip_ref[:, lanes] * inner.astype(f32)
        shifts, features = {}, {}
        for s in (1, 2):
            now = streams_ref[s, :, lanes].astype(f32)
            one, two = shifted(scratch.at[s], edge(halo_ref, s, lanes), now)
            taps = taps_ref[s, :, lanes]
            shifts[s] = (now, one, two)
            features[s] = taps[0:1] * now + taps[1:2] * one + taps[2:3] * two
        grads = (
            grad_ref[:, lanes].astype(f32) * mixed_ref[:, lanes],
            grad_gated * features[2],
            grad_gated * features[1],
        )
        following = after_ref[TAPS : TAPS + 16, lanes].astype(f32)
        following = following[:8] + following[8:]
        for s in range(3):
            ahead[s, 0:length, :] = grads[s]
            ahead[s, length : length + 2, :] = following[2 * s : 2 * s + 2]
            taps = taps_ref[s, :, lanes]
            stream_grad_ref[s, :, lanes] = (
                taps[0:1] * grads[s] + taps[1:2] * ahead[s, 1 : length + 1, :] + taps[2:3] * ahead[s, 2 : length + 2, :]
            ).astype(bf16)
        for s in (1, 2):
            for j in range(3):
                row = col * 8 + (s - 1) * 3 + j
                late_ref[row : row + 1, :] = jnp.sum(grads[s] * shifts[s][j], axis=0, keepdims=True)
        late_ref[col * 8 + 6 : col * 8 + 8, :] = jnp.zeros((2, LANES), f32)


def from_behind(value, axis, steps):
    count = lax.axis_size(axis)
    first, last = (max(0, -steps), min(count, count - steps))
    return lax.ppermute(value, axis, [(source, source + steps) for source in range(first, last)])


def sent_to(value, axis, distances):
    value = lax.reduce_precision(value, 8, 7)
    count = lax.axis_size(axis)
    half = value.astype(bf16)
    return value, [lax.ppermute(half, axis, [(i, i ^ d) for i in range(count)]) for d in distances]


def added(value, others):
    terms = [value] + [other.astype(f32) for other in others]
    while len(terms) > 1:
        terms = [terms[i] + terms[i + 1] for i in range(0, len(terms), 2)]
    return terms[0]


def close_kernel(mine_ref, other_ref, long_ref, short_ref, skip_ref, gain_ref):
    total = mine_ref[...] + other_ref[...].astype(f32)
    early, late = total[: skip_ref.shape[1] // LANES * 16], total[skip_ref.shape[1] // LANES * 16 :]
    for col in range(skip_ref.shape[1] // LANES):
        lanes = slice(col * LANES, (col + 1) * LANES)
        at = col * 16
        long_ref[col * PER : (col + 1) * PER, :] = early[at : at + PER]
        skip_ref[:, lanes] = early[at + 8 : at + 9]
        gain_ref[:, lanes] = early[at + 9 : at + 10]
        for j in range(3):
            short_ref[0, j : j + 1, lanes] = early[at + 10 + j : at + 11 + j]
            for s in (1, 2):
                row = col * 8 + (s - 1) * 3 + j
                short_ref[s, j : j + 1, lanes] = late[row : row + 1]


def streamed(body, name, count, inputs, outputs, scratch_shapes=()):
    inputs = [(array if isinstance(array, tuple) else (array,), picks, split) for array, picks, split in inputs]
    firsts = [sum(len(arrays) for arrays, _, _ in inputs[:at]) for at in range(len(inputs) + 1)]

    def piece(ref, split, i, count=count):
        size = ref.shape[split] // count
        start = i * size
        if not isinstance(start, int):
            start = pl.multiple_of(start, size)
        return ref.at[tuple(pl.ds(start, size) if d == split else slice(None) for d in range(len(ref.shape)))]

    def kernel(*refs):
        n, m = len(inputs), len(outputs)
        sources, refs = refs[: firsts[-1]], refs[firsts[-1] :]
        targets, held, made = refs[:m], refs[m : m + n], refs[m + n : 2 * m + n]
        in_sem, out_sem = refs[2 * m + n : 2 * m + n + 2]
        own = refs[2 * m + n + 2 :]

        def fetch(at, i, array=0):
            arrays, picks, split = inputs[at]
            source, target = sources[firsts[at] + array], held[at]
            if picks:
                source = source.at[tuple(pl.ds(*picks[d]) if d in picks else slice(None) for d in range(arrays[0].ndim))]
            if isinstance(split, int):
                share = count // len(arrays)
                source, target = piece(source, split, i - array * share, share), piece(target, split, i)
            elif len(arrays) > 1:
                target = piece(target, split[0], array, len(arrays))
            return pltpu.make_async_copy(source, target, in_sem.at[at, array if isinstance(split, tuple) else i])

        def send(at, i):
            split = outputs[at][2]
            source, target = made[at], targets[at]
            if isinstance(split, int):
                source, target = piece(source, split, i), piece(target, split, i)
            return pltpu.make_async_copy(source, target, out_sem.at[at, i])

        whole_in = [at for at in range(n) if not isinstance(inputs[at][2], int)]
        split_in = [at for at in range(n) if isinstance(inputs[at][2], int)]
        whole_out = [at for at in range(m) if not isinstance(outputs[at][2], int)]
        split_out = [at for at in range(m) if isinstance(outputs[at][2], int)]
        whole_parts = [(at, array) for at in whole_in for array in range(len(inputs[at][0]))]
        for at, array in whole_parts:
            fetch(at, 0, array).start()
        for i in range(count):
            for at in split_in:
                fetch(at, i, i * len(inputs[at][0]) // count).start()
        for at, array in whole_parts:
            fetch(at, 0, array).wait()

        def step(i, carry):
            for at in split_in:
                target = piece(held[at], inputs[at][2], i)
                pltpu.make_async_copy(target, target, in_sem.at[at, i]).wait()
            views = [
                ref if split is None else piece(ref, split if isinstance(split, int) else split[0], i)
                for ref, split in zip((*held, *made), [x[2] for x in (*inputs, *outputs)])
            ]
            body(i, *views, *own)
            for at in split_out:
                send(at, i).start()
            return carry

        lax.fori_loop(0, count, step, 0)
        for at in whole_out:
            send(at, 0).start()
        for at in whole_out:
            send(at, 0).wait()
        for i in range(count):
            for at in split_out:
                send(at, i).wait()

    def held_shape(arrays, picks, split):
        shape = [picks[d][1] if d in picks else arrays[0].shape[d] for d in range(arrays[0].ndim)]
        if len(arrays) > 1:
            shape[split if isinstance(split, int) else split[0]] *= len(arrays)
        return tuple(shape)

    return pl.pallas_call(
        kernel,
        in_specs=[pl.BlockSpec(memory_space=pl.ANY)] * firsts[-1],
        out_specs=[pl.BlockSpec(memory_space=pl.ANY)] * len(outputs),
        out_shape=[jax.ShapeDtypeStruct(shape, dtype) for shape, dtype, _ in outputs],
        scratch_shapes=[pltpu.VMEM(held_shape(*each), each[0][0].dtype) for each in inputs]
        + [pltpu.VMEM(shape, dtype) for shape, dtype, _ in outputs]
        + [pltpu.SemaphoreType.DMA((len(inputs), count)), pltpu.SemaphoreType.DMA((len(outputs), count))]
        + list(scratch_shapes),
        compiler_params=params(VMEM_LIMIT),
        cost_estimate=pl.CostEstimate(flops=0, bytes_accessed=8000, transcendentals=0),
        name=name,
    )(*(array for arrays, _, _ in inputs for array in arrays))


def local(residual, streams, short_filter, long_filter, skip, gain, cotangent):
    tokens_here, channels = streams.shape[1:]
    groups = long_filter.shape[0]
    rows_here, width_all = residual.shape
    owners = lax.axis_size("tensor")
    assert long_filter.shape[1] == TAPS and channels == groups * WIDTH and tokens_here % (2 * TAPS) == 0
    columns = channels // LANES
    halves = 1
    part = channels // halves
    count = max(halves, channels // STEP)
    skip_row = skip[None, :]
    gain_row = gain[None, :]
    gain_here = lax.dynamic_slice_in_dim(gain, lax.axis_index("tensor") * channels, channels)[None, :]

    spec = pl.BlockSpec

    def padded(count=None):
        shape = (tokens_here + 8, LANES)
        return pltpu.VMEM(shape if count is None else (count,) + shape, f32)

    def kernel(body, name, micros, limit=VMEM_LIMIT, **how):
        return pl.pallas_call(
            body,
            compiler_params=params(limit),
            cost_estimate=pl.CostEstimate(flops=0, bytes_accessed=micros * 1000, transcendentals=0),
            name=name,
            **how,
        )

    packed, halo = kernel(
        open_kernel,
        "open",
        3,
        in_specs=[spec(memory_space=pl.ANY)] * 3 + [spec(memory_space=pltpu.VMEM)],
        out_specs=[spec(memory_space=pl.ANY)] * 2,
        out_shape=[
            jax.ShapeDtypeStruct((owners, 2, rows_here, channels), bf16),
            jax.ShapeDtypeStruct((TAPS + 8, channels), bf16),
        ],
        scratch_shapes=[
            pltpu.VMEM((owners, 2, rows_here, channels), bf16),
            pltpu.VMEM((3, TAPS + 16, channels), bf16),
            pltpu.VMEM((TAPS + 8, channels), bf16),
            pltpu.VMEM((3, TAPS + 16, LANES), f32),
            pltpu.SemaphoreType.DMA((owners, 2)),
            pltpu.SemaphoreType.DMA((owners, 2)),
            pltpu.SemaphoreType.DMA((2,)),
        ],
    )(cotangent, residual, streams, short_filter)
    halo = from_behind(halo, "dp", 1)
    received = lax.all_to_all(packed, "tensor", split_axis=0, concat_axis=0, tiled=True)

    band_shape = jax.ShapeDtypeStruct((groups, BLOCK, SPAN), bf16)
    each = min(groups, 16)
    ahead_bands, behind_bands = kernel(
        bands_kernel,
        "bands",
        5,
        grid=(groups // each,),
        in_specs=[spec((each, TAPS), lambda i: (i, 0))],
        out_specs=[spec((each, BLOCK, SPAN), lambda i: (i, 0, 0))] * 2,
        out_shape=[band_shape] * 2,
    )(long_filter)

    output, mixed, gated = streamed(
        forward_kernel,
        "forward",
        count,
        [(streams, {}, 2), (halo, {}, 1), (short_filter, {}, (2,)), (skip_row, {}, (1,)), (ahead_bands, {}, 0)],
        [((tokens_here, channels), t, 1) for t in (bf16, f32, bf16)],
        [padded(3)],
    )

    (stats,) = streamed(
        functools.partial(stats_kernel, count),
        "stats",
        count,
        [(received, {}, 3), (output, {}, 1), (gain_here, {}, (1,))],
        [((2, tokens_here), f32, None)],
        [pltpu.VMEM((tokens_here, LANES), f32)] * 2,
    )
    stats = lax.psum(stats, "tensor")
    heads = []
    for k in range(halves):
        here = (k * part, part)
        heads.append(
            streamed(
                functools.partial(head_kernel, width_all),
                "head",
                count // halves,
                [
                    (streams, {0: (0, 1), 2: here}, 2),
                    (streams, {0: (1, 1), 1: (0, 16), 2: here}, 2),
                    (streams, {0: (2, 1), 1: (0, 16), 2: here}, 2),
                    (halo, {1: here}, 1),
                    (short_filter, {2: here}, (2,)),
                    (skip_row, {1: here}, (1,)),
                    (long_filter, {0: (k * groups // halves, groups // halves)}, 0),
                    (stats, {}, None),
                    (received, {3: here}, 3),
                    (output, {1: here}, 1),
                    (gain_here, {1: here}, (1,)),
                    (mixed, {0: (0, 16), 1: here}, 1),
                ],
                [
                    ((tokens_here, part), bf16, 1),
                    ((tokens_here, part), bf16, 1),
                    ((1, part), f32, (1,)),
                    ((TAPS + 16, part), bf16, 1),
                ],
                [padded()] + [pltpu.VMEM((tokens_here, LANES), f32)] * 2,
            )
        )
    grads, inner, shares, first = (tuple(column) for column in zip(*heads))
    after = [from_behind(piece, "dp", -1) for piece in first]
    leaving, inner = lax.optimization_barrier((output, inner))
    rows_received = lax.all_to_all(
        leaving.reshape(owners, rows_here, channels), "tensor", split_axis=0, concat_axis=0, tiled=True
    )

    (early,) = streamed(
        sums_kernel,
        "sums",
        count,
        [
            (streams, {0: (0, 1)}, 2),
            (halo, {}, 1),
            (gated, {}, 1),
            (inner, {}, 1),
            (grads, {}, 1),
            (mixed, {}, 1),
            (shares, {}, (1,)),
        ],
        [((columns * 16, LANES), f32, 0)],
        [padded()],
    )

    stream_grad, late = streamed(
        backward_kernel,
        "backward",
        count,
        [
            (streams, {}, 2),
            (halo, {}, 1),
            (short_filter, {}, (2,)),
            (skip_row, {}, (1,)),
            (behind_bands, {}, 0),
            (grads, {}, 1),
            (mixed, {}, 1),
            (inner, {}, 1),
            (tuple(after), {}, 1),
        ],
        [(streams.shape, bf16, 2), ((columns * 8, LANES), f32, 0)],
        [padded(3), padded(3)],
    )
    bits = (lax.axis_size("dp") - 1).bit_length()
    stages = [[1 << n] if n + 1 == bits else [1 << n, 2 << n, 3 << n] for n in range(0, bits, 2)]
    total = jnp.concatenate([early, late], axis=0)
    for stage in stages[:-1]:
        mine, others = sent_to(total, "dp", stage)
        total = added(mine, others)
    block = min(rows_here, 16)
    by_rows = spec((block, width_all), lambda i: (i, 0))
    normed, grad_residual = kernel(
        norm_kernel,
        "norm",
        4,
        NORM_LIMIT,
        grid=(rows_here // block,),
        in_specs=[
            spec((owners, block, channels), lambda i: (0, i, 0)),
            by_rows,
            by_rows,
            spec((1, width_all), lambda i: (0, 0)),
        ],
        out_specs=[by_rows, by_rows],
        out_shape=[jax.ShapeDtypeStruct(residual.shape, bf16)] * 2,
        scratch_shapes=[pltpu.VMEM((block, width_all), f32)],
    )(rows_received, residual, cotangent, gain_row)

    mine, others = sent_to(total, "dp", stages[-1])
    mine, normed, grad_residual = lax.optimization_barrier((mine, normed, grad_residual))
    mine, other = (mine, others[0]) if len(others) == 1 else (added(mine, others[:1]), added(others[1], others[2:]))
    long_grad, short_grad, skip_grad, gain_grad = kernel(
        close_kernel,
        "close",
        1,
        SMALL_LIMIT,
        out_shape=[
            jax.ShapeDtypeStruct((groups, TAPS), f32),
            jax.ShapeDtypeStruct((3, 3, channels), f32),
            jax.ShapeDtypeStruct((1, channels), f32),
            jax.ShapeDtypeStruct((1, channels), f32),
        ],
    )(mine, other)
    skip_grad, gain_grad = skip_grad.reshape(channels), gain_grad.reshape(channels)
    return (normed, grad_residual, stream_grad, long_grad, short_grad, skip_grad, gain_grad)


def solution(mesh):
    placed = (
        P(("dp", "tensor"), None),
        P(None, "dp", "tensor"),
        P(None, None, "tensor"),
        P("tensor", None),
        P("tensor"),
        P(),
        P(("dp", "tensor"), None),
    )
    return jax.shard_map(
        local,
        mesh=mesh,
        in_specs=placed,
        out_specs=(
            P(("dp", "tensor"), None),
            P(("dp", "tensor"), None),
            P(None, "dp", "tensor"),
            P("tensor", None),
            P(None, None, "tensor"),
            P("tensor"),
            P("tensor"),
        ),
        check_vma=False,
    )
```

```python
import functools

import jax
import jax.numpy as jnp
from jax import lax
from jax.experimental import pallas as pl
from jax.experimental.pallas import tpu as pltpu
from jax.sharding import PartitionSpec as P

norm_eps = 1e-05
LANES = 128
TAPS = 128
WIDTH = 16
PER = LANES // WIDTH
BLOCK = 64
SPAN = 256
VMEM_LIMIT = 63.5
SMALL_LIMIT = 8
NORM_LIMIT = 63.5
STEP = 512
f32 = jnp.float32
bf16 = jnp.bfloat16


def params(limit):
    return pltpu.CompilerParams(vmem_limit_bytes=int(limit * 2**20))


def dot(a, b):
    return lax.dot_general(a, b, (((1,), (0,)), ((), ())), preferred_element_type=f32)


def dot_nt(a, b):
    return lax.dot_general(a, b, (((1,), (1,)), ((), ())), preferred_element_type=f32)


def lane_group(shape):
    return lax.broadcasted_iota(jnp.int32, shape, len(shape) - 1) % LANES // WIDTH


def pick_groups(stacked, rows):
    out = stacked[:rows]
    which = lane_group(out.shape)
    for g in range(1, PER):
        out = jnp.where(which == g, stacked[g * rows : (g + 1) * rows], out)
    return out


def shifted(scratch, halo, current):
    length = current.shape[0]
    scratch[6:8, :] = halo
    scratch[8 : 8 + length, :] = current
    return scratch[7 : 7 + length, :], scratch[6 : 6 + length, :]


def band(row, first, rows):
    wide = jnp.concatenate([row, jnp.zeros((1, SPAN - TAPS), f32)], axis=1)
    return pltpu.roll(jnp.broadcast_to(wide, (rows, SPAN)), first, 1, stride=1, stride_axis=0).astype(bf16)


def anti_identity(size):
    total = lax.broadcasted_iota(jnp.int32, (size, size), 0) + lax.broadcasted_iota(jnp.int32, (size, size), 1)
    return jnp.where(total == size - 1, 1.0, 0.0).astype(bf16)


def windows(extended, length):
    return jnp.concatenate([extended[at : at + SPAN] for at in range(0, length, BLOCK)], axis=1)


def convolve(bands, extended, length, rows=BLOCK):
    stacked = dot(bands.reshape(PER * rows, SPAN), windows(extended, length))
    result = pick_groups(stacked, rows)
    return [result[:, at : at + LANES] for at in range(0, result.shape[1], LANES)]


def bands_kernel(filter_ref, ahead_ref, behind_ref):
    half = filter_ref[...].astype(bf16)
    back = dot(half, anti_identity(TAPS))
    fore = half.astype(f32)
    for g in range(half.shape[0]):
        ahead_ref[g] = band(back[g : g + 1], SPAN - TAPS - BLOCK + 1, BLOCK)
        behind_ref[g] = band(fore[g : g + 1], 0, BLOCK)


def open_kernel(
    cot_ref, residual_ref, streams_ref, taps_ref, packed_ref, halo_ref, pieces, ends, last, rows, scratch, in_sem, out_sem, end_sem
):
    owners, _, _, channels = packed_ref.shape
    length = streams_ref.shape[1]
    back = ends.shape[1]
    ending = [
        pltpu.make_async_copy(streams_ref.at[pl.ds(1, 2), pl.ds(length - back, back), :], ends, end_sem.at[0]),
        pltpu.make_async_copy(streams_ref.at[0, pl.ds(length - 16, 16), :], last, end_sem.at[1]),
    ]
    for copy in ending:
        copy.start()
    places = [(j, which) for j in range(owners) for which in range(2)]
    arriving = [
        pltpu.make_async_copy(
            (cot_ref, residual_ref)[which].at[:, pl.ds(j * channels, channels)], pieces.at[j, which], in_sem.at[j, which]
        )
        for j, which in places
    ]
    leaving = [
        pltpu.make_async_copy(pieces.at[j, which], packed_ref.at[j, which], out_sem.at[j, which]) for j, which in places
    ]
    for copy in arriving:
        copy.start()
    for copy in ending:
        copy.wait()
    for col in range(channels // LANES):
        lanes = slice(col * LANES, (col + 1) * LANES)
        features = []
        for s in (1, 2):
            scratch[s, 0:back, :] = ends[s - 1, :, lanes].astype(f32)
            taps = taps_ref[s, :, lanes]
            now, one, two = (scratch[s, back - TAPS - n : back - n, :] for n in range(3))
            features.append(taps[0:1] * now + taps[1:2] * one + taps[2:3] * two)
        rows[:TAPS, lanes] = (features[0] * features[1]).astype(bf16)
        edges = scratch.at[0]
        edges[0:2, :] = last[:, lanes].astype(f32)[14:]
        edges[2:4, :] = scratch[1, back - 2 : back, :]
        edges[4:6, :] = scratch[2, back - 2 : back, :]
        edges[6:8, :] = jnp.zeros((2, LANES), f32)
        rows[TAPS : TAPS + 8, lanes] = edges[0:8, :].astype(bf16)
        if col == 0:
            for copy, onward in zip(arriving, leaving):
                copy.wait()
                onward.start()
    ending = pltpu.make_async_copy(rows, halo_ref, end_sem.at[2])
    ending.start()
    for copy in leaving:
        copy.wait()
    ending.wait()


def edge(halo_ref, s, lanes):
    return halo_ref[TAPS : TAPS + 8, lanes].astype(f32)[2 * s : 2 * s + 2]


def feature(scratch, halo_ref, streams_ref, taps_ref, s, lanes, index):
    now = streams_ref[index, :, lanes].astype(f32)
    one, two = shifted(scratch, edge(halo_ref, s, lanes), now)
    taps = taps_ref[s, :, lanes]
    return taps[0:1] * now + taps[1:2] * one + taps[2:3] * two


def forward_kernel(index, streams_ref, halo_ref, taps_ref, skip_ref, ahead_ref, output_ref, mixed_ref, gated_ref, scratch):
    length = streams_ref.shape[1]
    for col in range(streams_ref.shape[2] // LANES):
        lanes = slice(col * LANES, (col + 1) * LANES)
        f0, f1, f2 = (feature(scratch.at[s], halo_ref, streams_ref, taps_ref, s, lanes, s) for s in range(3))
        gated = (f1 * f2).astype(bf16)
        gated_ref[:, lanes] = gated
        zero = jnp.zeros((SPAN - TAPS - BLOCK, LANES), bf16)
        extended = jnp.concatenate([zero, halo_ref[:TAPS, lanes], gated], axis=0)
        skip = skip_ref[:, lanes]
        for b, result in enumerate(convolve(ahead_ref[col * PER : (col + 1) * PER], extended, length)):
            rows = slice(b * BLOCK, (b + 1) * BLOCK)
            mixed = result + skip * gated[rows].astype(f32)
            mixed_ref[rows, lanes] = mixed
            output_ref[rows, lanes] = (f0[rows] * mixed).astype(bf16)


def columns_of(received_ref, which, lanes):
    piece = received_ref[:, which, :, lanes].astype(f32)
    return piece.reshape(piece.shape[0] * piece.shape[1], LANES)


def stats_kernel(count, index, received_ref, output_ref, gain_ref, stats_ref, squares_ref, products_ref):
    @pl.when(index == 0)
    def _():
        squares_ref[...] = jnp.zeros_like(squares_ref)
        products_ref[...] = jnp.zeros_like(products_ref)

    squares, products = squares_ref[...], products_ref[...]
    for col in range(output_ref.shape[1] // LANES):
        lanes = slice(col * LANES, (col + 1) * LANES)
        summed = columns_of(received_ref, 1, lanes) + output_ref[:, lanes].astype(f32)
        squares = squares + summed * summed
        products = products + columns_of(received_ref, 0, lanes) * gain_ref[:, lanes] * summed
    squares_ref[...] = squares
    products_ref[...] = products

    @pl.when(index == count - 1)
    def _():
        for row, sums in ((0, squares), (1, products)):
            stats_ref[row : row + 1, :] = jnp.sum(sums.T, axis=0, keepdims=True)


def norm_kernel(received_ref, residual_ref, cot_ref, gain_ref, normed_ref, grad_ref, summed_ref):
    sources, rows, part = received_ref.shape
    width_all = residual_ref.shape[1]
    squares = jnp.zeros((rows, LANES), f32)
    products = jnp.zeros((rows, LANES), f32)
    for s in range(sources):
        where = slice(s * part, (s + 1) * part)
        summed = residual_ref[:, where].astype(f32) + received_ref[s].astype(f32)
        summed_ref[:, where] = summed
        scaled = cot_ref[:, where].astype(f32) * gain_ref[:, where]
        both = (summed * summed, scaled * summed)
        for col in range(part // LANES):
            lanes = slice(col * LANES, (col + 1) * LANES)
            squares = squares + both[0][:, lanes]
            products = products + both[1][:, lanes]
    inverse = lax.rsqrt(jnp.sum(squares, axis=1, keepdims=True) / width_all + norm_eps)
    along = inverse * jnp.sum(products, axis=1, keepdims=True) / width_all
    for s in range(sources):
        where = slice(s * part, (s + 1) * part)
        unit = summed_ref[:, where] * inverse
        gain = gain_ref[:, where]
        normed_ref[:, where] = (unit * gain).astype(bf16)
        grad_ref[:, where] = (inverse * (cot_ref[:, where].astype(f32) * gain - unit * along)).astype(bf16)


def head_kernel(
    width_all,
    index,
    streams_ref,
    first1_ref,
    first2_ref,
    halo_ref,
    taps_ref,
    skip_ref,
    filter_ref,
    stats_ref,
    received_ref,
    output_ref,
    gain_ref,
    mixed_ref,
    grad_ref,
    inner_ref,
    share_ref,
    first_ref,
    scratch,
    inverse_ref,
    along_ref,
):
    @pl.when(index == 0)
    def _():
        tokens = stats_ref.shape[1]
        squares = jnp.broadcast_to(stats_ref[0:1, :], (LANES, tokens)).T
        products = jnp.broadcast_to(stats_ref[1:2, :], (LANES, tokens)).T
        inverse = lax.rsqrt(squares / width_all + norm_eps)
        inverse_ref[...] = inverse
        along_ref[...] = inverse * products / width_all

    inverse, along = inverse_ref[...], along_ref[...]
    for col in range(streams_ref.shape[2] // LANES):
        lanes = slice(col * LANES, (col + 1) * LANES)
        cot = columns_of(received_ref, 0, lanes)
        unit = (columns_of(received_ref, 1, lanes) + output_ref[:, lanes].astype(f32)) * inverse
        share_ref[:, lanes] = jnp.sum(cot * unit, axis=0, keepdims=True)
        grad_half = (inverse * (cot * gain_ref[:, lanes] - unit * along)).astype(bf16)
        grad_ref[:, lanes] = grad_half
        grad = grad_half.astype(f32)
        f0 = feature(scratch, halo_ref, streams_ref, taps_ref, 0, lanes, 0)
        inner = (grad * f0).astype(bf16)
        inner_ref[:, lanes] = inner
        first_ref[:TAPS, lanes] = inner[:TAPS]
        features = []
        for s, top in ((1, first1_ref), (2, first2_ref)):
            taps = taps_ref[s, :, lanes]
            now = top[0, :, lanes].astype(f32)
            scratch[6:8, :] = edge(halo_ref, s, lanes)
            scratch[8:24, :] = now
            features.append(taps[0:1] * now[:8] + taps[1:2] * scratch[7:15, :] + taps[2:3] * scratch[6:14, :])
        half = filter_ref[col * PER : (col + 1) * PER].astype(bf16).astype(f32)
        bands = jnp.stack([band(half[g : g + 1], 0, 16) for g in range(PER)])
        conv = convolve(bands, inner, BLOCK, 16)[0][:8]
        grad_gated = conv + skip_ref[:, lanes] * inner[:16].astype(f32)[:8]
        scratch[0:2, :] = (grad[:8] * mixed_ref[0:8, lanes])[:2]
        scratch[2:4, :] = (grad_gated * features[1])[:2]
        scratch[4:6, :] = (grad_gated * features[0])[:2]
        scratch[6:8, :] = jnp.zeros((2, LANES), f32)
        rows = scratch[0:8, :]
        high = rows.astype(bf16)
        first_ref[TAPS : TAPS + 8, lanes] = high
        first_ref[TAPS + 8 : TAPS + 16, lanes] = (rows - high.astype(f32)).astype(bf16)


def sums_kernel(index, streams_ref, halo_ref, gated_ref, inner_ref, grad_ref, mixed_ref, gain_ref, early_ref, scratch):
    length = streams_ref.shape[1]
    blocks = length // BLOCK
    flip = anti_identity(SPAN)
    which = lane_group((BLOCK, blocks * LANES))
    masks = [jnp.where(which == g, 1.0, 0.0).astype(bf16) for g in range(PER)]
    zero = jnp.zeros((SPAN - TAPS - BLOCK, LANES), bf16)
    for col in range(streams_ref.shape[2] // LANES):
        lanes = slice(col * LANES, (col + 1) * LANES)
        gated = gated_ref[:, lanes]
        inner = inner_ref[:, lanes]
        extended = jnp.concatenate([zero, halo_ref[:TAPS, lanes], gated], axis=0)
        backward = dot(flip, windows(extended, length)).astype(bf16)
        grads = jnp.concatenate([inner[at : at + BLOCK] for at in range(0, length, BLOCK)], axis=1)
        pairs = dot_nt(jnp.concatenate([grads * mask for mask in masks], axis=0), backward)
        base = col * 16
        for g in range(PER):
            skewed = pltpu.roll(pairs[g * BLOCK : (g + 1) * BLOCK], SPAN - BLOCK + 1, 1, stride=1, stride_axis=0)
            early_ref[base + g : base + g + 1, :] = jnp.sum(skewed[:, :TAPS], axis=0, keepdims=True)
        early_ref[base + 8 : base + 9, :] = jnp.sum(inner.astype(f32) * gated.astype(f32), axis=0, keepdims=True)
        early_ref[base + 9 : base + 10, :] = gain_ref[:, lanes]
        grad_query = grad_ref[:, lanes].astype(f32) * mixed_ref[:, lanes]
        now = streams_ref[0, :, lanes].astype(f32)
        one, two = shifted(scratch, edge(halo_ref, 0, lanes), now)
        for j, shift in enumerate((now, one, two)):
            early_ref[base + 10 + j : base + 11 + j, :] = jnp.sum(grad_query * shift, axis=0, keepdims=True)
        early_ref[base + 13 : base + 16, :] = jnp.zeros((3, LANES), f32)


def backward_kernel(
    index,
    streams_ref,
    halo_ref,
    taps_ref,
    skip_ref,
    behind_ref,
    grad_ref,
    mixed_ref,
    inner_ref,
    after_ref,
    early_ref,
    stream_grad_ref,
    bundle_ref,
    scratch,
    ahead,
):
    length = streams_ref.shape[1]
    late = scratch.at[0]
    late[0:8, :] = jnp.zeros((8, LANES), f32)
    for col in range(streams_ref.shape[2] // LANES):
        lanes = slice(col * LANES, (col + 1) * LANES)
        inner = inner_ref[:, lanes]
        zero = jnp.zeros((SPAN - TAPS - BLOCK, LANES), bf16)
        extended = jnp.concatenate([inner, after_ref[:TAPS, lanes], zero], axis=0)
        parts = convolve(behind_ref[col * PER : (col + 1) * PER], extended, length)
        grad_gated = jnp.concatenate(parts, axis=0) + skip_ref[:, lanes] * inner.astype(f32)
        shifts, features = {}, {}
        for s in (1, 2):
            now = streams_ref[s - 1, :, lanes].astype(f32)
            one, two = shifted(scratch.at[s], edge(halo_ref, s, lanes), now)
            taps = taps_ref[s, :, lanes]
            shifts[s] = (now, one, two)
            features[s] = taps[0:1] * now + taps[1:2] * one + taps[2:3] * two
        grads = (
            grad_ref[:, lanes].astype(f32) * mixed_ref[:, lanes],
            grad_gated * features[2],
            grad_gated * features[1],
        )
        following = after_ref[TAPS : TAPS + 16, lanes].astype(f32)
        following = following[:8] + following[8:]
        for s in range(3):
            ahead[s, 0:length, :] = grads[s]
            ahead[s, length : length + 2, :] = following[2 * s : 2 * s + 2]
            taps = taps_ref[s, :, lanes]
            stream_grad_ref[s, :, lanes] = (
                taps[0:1] * grads[s] + taps[1:2] * ahead[s, 1 : length + 1, :] + taps[2:3] * ahead[s, 2 : length + 2, :]
            ).astype(bf16)
        for s in (1, 2):
            for j in range(3):
                row = (s - 1) * 3 + j
                late[row : row + 1, :] = jnp.sum(grads[s] * shifts[s][j], axis=0, keepdims=True)
        base = col * 24
        bundle_ref[base : base + 16, :] = early_ref[col * 16 : (col + 1) * 16, :].astype(bf16)
        bundle_ref[base + 16 : base + 24, :] = late[0:8, :].astype(bf16)


def from_behind(value, axis, steps):
    count = lax.axis_size(axis)
    first, last = (max(0, -steps), min(count, count - steps))
    return lax.ppermute(value, axis, [(source, source + steps) for source in range(first, last)])


def sent_to(value, axis, distances):
    half = value
    if value.dtype != bf16:
        value = lax.reduce_precision(value, 8, 7)
        half = value.astype(bf16)
    count = lax.axis_size(axis)
    return value, [lax.ppermute(half, axis, [(i, i ^ d) for i in range(count)]) for d in distances]


def added(value, others):
    terms = [term.astype(f32) for term in (value, *others)]
    while len(terms) > 1:
        terms = [terms[i] + terms[i + 1] for i in range(0, len(terms), 2)]
    return terms[0]


def close_kernel(mine_ref, other_ref, long_ref, short_ref, skip_ref, gain_ref):
    total = mine_ref[...].astype(f32) + other_ref[...].astype(f32)
    for col in range(skip_ref.shape[1] // LANES):
        lanes = slice(col * LANES, (col + 1) * LANES)
        at = col * 24
        long_ref[col * PER : (col + 1) * PER, :] = total[at : at + PER]
        skip_ref[:, lanes] = total[at + 8 : at + 9]
        gain_ref[:, lanes] = total[at + 9 : at + 10]
        for j in range(3):
            short_ref[0, j : j + 1, lanes] = total[at + 10 + j : at + 11 + j]
            for s in (1, 2):
                row = at + 16 + (s - 1) * 3 + j
                short_ref[s, j : j + 1, lanes] = total[row : row + 1]


def streamed(body, name, count, inputs, outputs, scratch_shapes=()):
    inputs = [(array if isinstance(array, tuple) else (array,), picks, split) for array, picks, split in inputs]
    firsts = [sum(len(arrays) for arrays, _, _ in inputs[:at]) for at in range(len(inputs) + 1)]

    def piece(ref, split, i, count=count):
        size = ref.shape[split] // count
        start = i * size
        if not isinstance(start, int):
            start = pl.multiple_of(start, size)
        return ref.at[tuple(pl.ds(start, size) if d == split else slice(None) for d in range(len(ref.shape)))]

    def kernel(*refs):
        n, m = len(inputs), len(outputs)
        sources, refs = refs[: firsts[-1]], refs[firsts[-1] :]
        targets, held, made = refs[:m], refs[m : m + n], refs[m + n : 2 * m + n]
        in_sem, out_sem = refs[2 * m + n : 2 * m + n + 2]
        own = refs[2 * m + n + 2 :]

        def fetch(at, i, array=0):
            arrays, picks, split = inputs[at]
            source, target = sources[firsts[at] + array], held[at]
            if picks:
                source = source.at[tuple(pl.ds(*picks[d]) if d in picks else slice(None) for d in range(arrays[0].ndim))]
            if isinstance(split, int):
                share = count // len(arrays)
                source, target = piece(source, split, i - array * share, share), piece(target, split, i)
            elif len(arrays) > 1:
                target = piece(target, split[0], array, len(arrays))
            return pltpu.make_async_copy(source, target, in_sem.at[at, array if isinstance(split, tuple) else i])

        def send(at, i):
            split = outputs[at][2]
            source, target = made[at], targets[at]
            if isinstance(split, int):
                source, target = piece(source, split, i), piece(target, split, i)
            return pltpu.make_async_copy(source, target, out_sem.at[at, i])

        whole_in = [at for at in range(n) if not isinstance(inputs[at][2], int)]
        split_in = [at for at in range(n) if isinstance(inputs[at][2], int)]
        whole_out = [at for at in range(m) if not isinstance(outputs[at][2], int)]
        split_out = [at for at in range(m) if isinstance(outputs[at][2], int)]
        whole_parts = [(at, array) for at in whole_in for array in range(len(inputs[at][0]))]
        for at, array in whole_parts:
            fetch(at, 0, array).start()
        for i in range(count):
            for at in split_in:
                fetch(at, i, i * len(inputs[at][0]) // count).start()
        for at, array in whole_parts:
            fetch(at, 0, array).wait()

        def step(i, carry):
            for at in split_in:
                target = piece(held[at], inputs[at][2], i)
                pltpu.make_async_copy(target, target, in_sem.at[at, i]).wait()
            views = [
                ref if split is None else piece(ref, split if isinstance(split, int) else split[0], i)
                for ref, split in zip((*held, *made), [x[2] for x in (*inputs, *outputs)])
            ]
            body(i, *views, *own)
            for at in split_out:
                send(at, i).start()
            return carry

        lax.fori_loop(0, count, step, 0)
        for at in whole_out:
            send(at, 0).start()
        for at in whole_out:
            send(at, 0).wait()
        for i in range(count):
            for at in split_out:
                send(at, i).wait()

    def held_shape(arrays, picks, split):
        shape = [picks[d][1] if d in picks else arrays[0].shape[d] for d in range(arrays[0].ndim)]
        if len(arrays) > 1:
            shape[split if isinstance(split, int) else split[0]] *= len(arrays)
        return tuple(shape)

    return pl.pallas_call(
        kernel,
        in_specs=[pl.BlockSpec(memory_space=pl.ANY)] * firsts[-1],
        out_specs=[pl.BlockSpec(memory_space=pl.ANY)] * len(outputs),
        out_shape=[jax.ShapeDtypeStruct(shape, dtype) for shape, dtype, _ in outputs],
        scratch_shapes=[pltpu.VMEM(held_shape(*each), each[0][0].dtype) for each in inputs]
        + [pltpu.VMEM(shape, dtype) for shape, dtype, _ in outputs]
        + [pltpu.SemaphoreType.DMA((len(inputs), count)), pltpu.SemaphoreType.DMA((len(outputs), count))]
        + list(scratch_shapes),
        compiler_params=params(VMEM_LIMIT),
        cost_estimate=pl.CostEstimate(flops=0, bytes_accessed=8000, transcendentals=0),
        name=name,
    )(*(array for arrays, _, _ in inputs for array in arrays))


def local(residual, streams, short_filter, long_filter, skip, gain, cotangent):
    tokens_here, channels = streams.shape[1:]
    groups = long_filter.shape[0]
    rows_here, width_all = residual.shape
    owners = lax.axis_size("tensor")
    assert long_filter.shape[1] == TAPS and channels == groups * WIDTH and tokens_here % (2 * TAPS) == 0
    columns = channels // LANES
    halves = 1
    part = channels // halves
    count = max(halves, channels // STEP)
    skip_row = skip[None, :]
    gain_row = gain[None, :]
    gain_here = lax.dynamic_slice_in_dim(gain, lax.axis_index("tensor") * channels, channels)[None, :]

    spec = pl.BlockSpec

    def padded(count=None):
        shape = (tokens_here + 8, LANES)
        return pltpu.VMEM(shape if count is None else (count,) + shape, f32)

    def kernel(body, name, micros, limit=VMEM_LIMIT, **how):
        return pl.pallas_call(
            body,
            compiler_params=params(limit),
            cost_estimate=pl.CostEstimate(flops=0, bytes_accessed=micros * 1000, transcendentals=0),
            name=name,
            **how,
        )

    packed, halo = kernel(
        open_kernel,
        "open",
        3,
        in_specs=[spec(memory_space=pl.ANY)] * 3 + [spec(memory_space=pltpu.VMEM)],
        out_specs=[spec(memory_space=pl.ANY)] * 2,
        out_shape=[
            jax.ShapeDtypeStruct((owners, 2, rows_here, channels), bf16),
            jax.ShapeDtypeStruct((TAPS + 8, channels), bf16),
        ],
        scratch_shapes=[
            pltpu.VMEM((owners, 2, rows_here, channels), bf16),
            pltpu.VMEM((2, TAPS + 16, channels), bf16),
            pltpu.VMEM((16, channels), bf16),
            pltpu.VMEM((TAPS + 8, channels), bf16),
            pltpu.VMEM((3, TAPS + 16, LANES), f32),
            pltpu.SemaphoreType.DMA((owners, 2)),
            pltpu.SemaphoreType.DMA((owners, 2)),
            pltpu.SemaphoreType.DMA((3,)),
        ],
    )(cotangent, residual, streams, short_filter)
    halo = from_behind(halo, "dp", 1)
    received = lax.all_to_all(packed, "tensor", split_axis=0, concat_axis=0, tiled=True)

    band_shape = jax.ShapeDtypeStruct((groups, BLOCK, SPAN), bf16)
    each = min(groups, 16)
    ahead_bands, behind_bands = kernel(
        bands_kernel,
        "bands",
        5,
        grid=(groups // each,),
        in_specs=[spec((each, TAPS), lambda i: (i, 0))],
        out_specs=[spec((each, BLOCK, SPAN), lambda i: (i, 0, 0))] * 2,
        out_shape=[band_shape] * 2,
    )(long_filter)

    output, mixed, gated = streamed(
        forward_kernel,
        "forward",
        count,
        [(streams, {}, 2), (halo, {}, 1), (short_filter, {}, (2,)), (skip_row, {}, (1,)), (ahead_bands, {}, 0)],
        [((tokens_here, channels), t, 1) for t in (bf16, f32, bf16)],
        [padded(3)],
    )

    (stats,) = streamed(
        functools.partial(stats_kernel, count),
        "stats",
        count,
        [(received, {}, 3), (output, {}, 1), (gain_here, {}, (1,))],
        [((2, tokens_here), f32, None)],
        [pltpu.VMEM((tokens_here, LANES), f32)] * 2,
    )
    stats = lax.psum(stats, "tensor")
    heads = []
    for k in range(halves):
        here = (k * part, part)
        heads.append(
            streamed(
                functools.partial(head_kernel, width_all),
                "head",
                count // halves,
                [
                    (streams, {0: (0, 1), 2: here}, 2),
                    (streams, {0: (1, 1), 1: (0, 16), 2: here}, 2),
                    (streams, {0: (2, 1), 1: (0, 16), 2: here}, 2),
                    (halo, {1: here}, 1),
                    (short_filter, {2: here}, (2,)),
                    (skip_row, {1: here}, (1,)),
                    (long_filter, {0: (k * groups // halves, groups // halves)}, 0),
                    (stats, {}, None),
                    (received, {3: here}, 3),
                    (output, {1: here}, 1),
                    (gain_here, {1: here}, (1,)),
                    (mixed, {0: (0, 16), 1: here}, 1),
                ],
                [
                    ((tokens_here, part), bf16, 1),
                    ((tokens_here, part), bf16, 1),
                    ((1, part), f32, (1,)),
                    ((TAPS + 16, part), bf16, 1),
                ],
                [padded()] + [pltpu.VMEM((tokens_here, LANES), f32)] * 2,
            )
        )
    grads, inner, shares, first = (tuple(column) for column in zip(*heads))
    after = [from_behind(piece, "dp", -1) for piece in first]
    leaving, inner = lax.optimization_barrier((output, inner))
    rows_received = lax.all_to_all(
        leaving.reshape(owners, rows_here, channels), "tensor", split_axis=0, concat_axis=0, tiled=True
    )

    (early,) = streamed(
        sums_kernel,
        "sums",
        count,
        [
            (streams, {0: (0, 1)}, 2),
            (halo, {}, 1),
            (gated, {}, 1),
            (inner, {}, 1),
            (grads, {}, 1),
            (mixed, {}, 1),
            (shares, {}, (1,)),
        ],
        [((columns * 16, LANES), f32, 0)],
        [padded()],
    )

    stream_grad, bundle = streamed(
        backward_kernel,
        "backward",
        count,
        [
            (streams, {0: (1, 2)}, 2),
            (halo, {}, 1),
            (short_filter, {}, (2,)),
            (skip_row, {}, (1,)),
            (behind_bands, {}, 0),
            (grads, {}, 1),
            (mixed, {}, 1),
            (inner, {}, 1),
            (tuple(after), {}, 1),
            (early, {}, 0),
        ],
        [(streams.shape, bf16, 2), ((columns * 24, LANES), bf16, 0)],
        [padded(3), padded(3)],
    )
    bits = (lax.axis_size("dp") - 1).bit_length()
    stages = [[1 << n] if n + 1 == bits else [1 << n, 2 << n, 3 << n] for n in range(0, bits, 2)]
    total = bundle
    for stage in stages[:-1]:
        mine, others = sent_to(total, "dp", stage)
        total = added(mine, others)
    block = min(rows_here, 32)
    by_rows = spec((block, width_all), lambda i: (i, 0))
    normed, grad_residual = kernel(
        norm_kernel,
        "norm",
        4,
        NORM_LIMIT,
        grid=(rows_here // block,),
        in_specs=[
            spec((owners, block, channels), lambda i: (0, i, 0)),
            by_rows,
            by_rows,
            spec((1, width_all), lambda i: (0, 0)),
        ],
        out_specs=[by_rows, by_rows],
        out_shape=[jax.ShapeDtypeStruct(residual.shape, bf16)] * 2,
        scratch_shapes=[pltpu.VMEM((block, width_all), f32)],
    )(rows_received, residual, cotangent, gain_row)

    mine, others = sent_to(total, "dp", stages[-1])
    mine, normed, grad_residual = lax.optimization_barrier((mine, normed, grad_residual))
    mine, other = (mine, others[0]) if len(others) == 1 else (added(mine, others[:1]), added(others[1], others[2:]))
    long_grad, short_grad, skip_grad, gain_grad = kernel(
        close_kernel,
        "close",
        1,
        SMALL_LIMIT,
        out_shape=[
            jax.ShapeDtypeStruct((groups, TAPS), f32),
            jax.ShapeDtypeStruct((3, 3, channels), f32),
            jax.ShapeDtypeStruct((1, channels), f32),
            jax.ShapeDtypeStruct((1, channels), f32),
        ],
    )(mine, other)
    skip_grad, gain_grad = skip_grad.reshape(channels), gain_grad.reshape(channels)
    return (normed, grad_residual, stream_grad, long_grad, short_grad, skip_grad, gain_grad)


def solution(mesh):
    placed = (
        P(("dp", "tensor"), None),
        P(None, "dp", "tensor"),
        P(None, None, "tensor"),
        P("tensor", None),
        P("tensor"),
        P(),
        P(("dp", "tensor"), None),
    )
    return jax.shard_map(
        local,
        mesh=mesh,
        in_specs=placed,
        out_specs=(
            P(("dp", "tensor"), None),
            P(("dp", "tensor"), None),
            P(None, "dp", "tensor"),
            P("tensor", None),
            P(None, None, "tensor"),
            P("tensor"),
            P("tensor"),
        ),
        check_vma=False,
    )
```

```python
import functools

import jax
import jax.numpy as jnp
from jax import lax
from jax.experimental import pallas as pl
from jax.experimental.pallas import tpu as pltpu
from jax.sharding import PartitionSpec as P

norm_eps = 1e-05
LANES = 128
TAPS = 128
WIDTH = 16
PER = LANES // WIDTH
BLOCK = 64
SPAN = 256
VMEM_LIMIT = 63.5
SMALL_LIMIT = 8
NORM_LIMIT = 63.5
STEP = 512
f32 = jnp.float32
bf16 = jnp.bfloat16


def params(limit):
    return pltpu.CompilerParams(vmem_limit_bytes=int(limit * 2**20))


def dot(a, b):
    return lax.dot_general(a, b, (((1,), (0,)), ((), ())), preferred_element_type=f32)


def dot_nt(a, b):
    return lax.dot_general(a, b, (((1,), (1,)), ((), ())), preferred_element_type=f32)


def lane_group(shape):
    return lax.broadcasted_iota(jnp.int32, shape, len(shape) - 1) % LANES // WIDTH


def pick_groups(stacked, rows):
    out = stacked[:rows]
    which = lane_group(out.shape)
    for g in range(1, PER):
        out = jnp.where(which == g, stacked[g * rows : (g + 1) * rows], out)
    return out


def shifted(scratch, halo, current):
    length = current.shape[0]
    scratch[6:8, :] = halo
    scratch[8 : 8 + length, :] = current
    return scratch[7 : 7 + length, :], scratch[6 : 6 + length, :]


def band(row, first, rows):
    wide = jnp.concatenate([row, jnp.zeros((1, SPAN - TAPS), f32)], axis=1)
    return pltpu.roll(jnp.broadcast_to(wide, (rows, SPAN)), first, 1, stride=1, stride_axis=0).astype(bf16)


def anti_identity(size):
    total = lax.broadcasted_iota(jnp.int32, (size, size), 0) + lax.broadcasted_iota(jnp.int32, (size, size), 1)
    return jnp.where(total == size - 1, 1.0, 0.0).astype(bf16)


def windows(extended, length):
    return jnp.concatenate([extended[at : at + SPAN] for at in range(0, length, BLOCK)], axis=1)


def convolve(bands, extended, length, rows=BLOCK):
    stacked = dot(bands.reshape(PER * rows, SPAN), windows(extended, length))
    result = pick_groups(stacked, rows)
    return [result[:, at : at + LANES] for at in range(0, result.shape[1], LANES)]


def bands_kernel(filter_ref, ahead_ref, behind_ref):
    half = filter_ref[...].astype(bf16)
    back = dot(half, anti_identity(TAPS))
    fore = half.astype(f32)
    for g in range(half.shape[0]):
        ahead_ref[g] = band(back[g : g + 1], SPAN - TAPS - BLOCK + 1, BLOCK)
        behind_ref[g] = band(fore[g : g + 1], 0, BLOCK)


def open_kernel(
    cot_ref, residual_ref, streams_ref, taps_ref, packed_ref, halo_ref, pieces, ends, last, rows, scratch, in_sem, out_sem, end_sem
):
    owners, _, _, channels = packed_ref.shape
    length = streams_ref.shape[1]
    back = ends.shape[1]
    ending = [
        pltpu.make_async_copy(streams_ref.at[pl.ds(1, 2), pl.ds(length - back, back), :], ends, end_sem.at[0]),
        pltpu.make_async_copy(streams_ref.at[0, pl.ds(length - 16, 16), :], last, end_sem.at[1]),
    ]
    for copy in ending:
        copy.start()
    places = [(j, which) for j in range(owners) for which in range(2)]
    arriving = [
        pltpu.make_async_copy(
            (cot_ref, residual_ref)[which].at[:, pl.ds(j * channels, channels)], pieces.at[j, which], in_sem.at[j, which]
        )
        for j, which in places
    ]
    leaving = [
        pltpu.make_async_copy(pieces.at[j, which], packed_ref.at[j, which], out_sem.at[j, which]) for j, which in places
    ]
    for copy in arriving:
        copy.start()
    for copy in ending:
        copy.wait()
    for col in range(channels // LANES):
        lanes = slice(col * LANES, (col + 1) * LANES)
        features = []
        for s in (1, 2):
            scratch[s, 0:back, :] = ends[s - 1, :, lanes].astype(f32)
            taps = taps_ref[s, :, lanes]
            now, one, two = (scratch[s, back - TAPS - n : back - n, :] for n in range(3))
            features.append(taps[0:1] * now + taps[1:2] * one + taps[2:3] * two)
        rows[:TAPS, lanes] = (features[0] * features[1]).astype(bf16)
        edges = scratch.at[0]
        edges[0:2, :] = last[:, lanes].astype(f32)[14:]
        edges[2:4, :] = scratch[1, back - 2 : back, :]
        edges[4:6, :] = scratch[2, back - 2 : back, :]
        edges[6:8, :] = jnp.zeros((2, LANES), f32)
        rows[TAPS : TAPS + 8, lanes] = edges[0:8, :].astype(bf16)
        if col == 0:
            for copy, onward in zip(arriving, leaving):
                copy.wait()
                onward.start()
    ending = pltpu.make_async_copy(rows, halo_ref, end_sem.at[2])
    ending.start()
    for copy in leaving:
        copy.wait()
    ending.wait()


def edge(halo_ref, s, lanes):
    return halo_ref[TAPS : TAPS + 8, lanes].astype(f32)[2 * s : 2 * s + 2]


def feature(scratch, halo_ref, streams_ref, taps_ref, s, lanes, index):
    now = streams_ref[index, :, lanes].astype(f32)
    one, two = shifted(scratch, edge(halo_ref, s, lanes), now)
    taps = taps_ref[s, :, lanes]
    return taps[0:1] * now + taps[1:2] * one + taps[2:3] * two


def forward_kernel(index, streams_ref, halo_ref, taps_ref, skip_ref, ahead_ref, output_ref, mixed_ref, gated_ref, scratch):
    length = streams_ref.shape[1]
    for col in range(streams_ref.shape[2] // LANES):
        lanes = slice(col * LANES, (col + 1) * LANES)
        f0, f1, f2 = (feature(scratch.at[s], halo_ref, streams_ref, taps_ref, s, lanes, s) for s in range(3))
        gated = (f1 * f2).astype(bf16)
        gated_ref[:, lanes] = gated
        zero = jnp.zeros((SPAN - TAPS - BLOCK, LANES), bf16)
        extended = jnp.concatenate([zero, halo_ref[:TAPS, lanes], gated], axis=0)
        skip = skip_ref[:, lanes]
        for b, result in enumerate(convolve(ahead_ref[col * PER : (col + 1) * PER], extended, length)):
            rows = slice(b * BLOCK, (b + 1) * BLOCK)
            mixed = result + skip * gated[rows].astype(f32)
            mixed_ref[rows, lanes] = mixed
            output_ref[rows, lanes] = (f0[rows] * mixed).astype(bf16)


def columns_of(received_ref, which, lanes):
    piece = received_ref[:, which, :, lanes].astype(f32)
    return piece.reshape(piece.shape[0] * piece.shape[1], LANES)


def stats_kernel(count, index, received_ref, output_ref, gain_ref, stats_ref, squares_ref, products_ref):
    @pl.when(index == 0)
    def _():
        squares_ref[...] = jnp.zeros_like(squares_ref)
        products_ref[...] = jnp.zeros_like(products_ref)

    squares, products = squares_ref[...], products_ref[...]
    for col in range(output_ref.shape[1] // LANES):
        lanes = slice(col * LANES, (col + 1) * LANES)
        summed = columns_of(received_ref, 1, lanes) + output_ref[:, lanes].astype(f32)
        squares = squares + summed * summed
        products = products + columns_of(received_ref, 0, lanes) * gain_ref[:, lanes] * summed
    squares_ref[...] = squares
    products_ref[...] = products

    @pl.when(index == count - 1)
    def _():
        for row, sums in ((0, squares), (1, products)):
            stats_ref[row : row + 1, :] = jnp.sum(sums.T, axis=0, keepdims=True)


def norm_kernel(received_ref, residual_ref, cot_ref, gain_ref, normed_ref, grad_ref, summed_ref):
    sources, rows, part = received_ref.shape
    width_all = residual_ref.shape[1]
    squares = jnp.zeros((rows, LANES), f32)
    products = jnp.zeros((rows, LANES), f32)
    for s in range(sources):
        where = slice(s * part, (s + 1) * part)
        summed = residual_ref[:, where].astype(f32) + received_ref[s].astype(f32)
        summed_ref[:, where] = summed
        scaled = cot_ref[:, where].astype(f32) * gain_ref[:, where]
        both = (summed * summed, scaled * summed)
        for col in range(part // LANES):
            lanes = slice(col * LANES, (col + 1) * LANES)
            squares = squares + both[0][:, lanes]
            products = products + both[1][:, lanes]
    inverse = lax.rsqrt(jnp.sum(squares, axis=1, keepdims=True) / width_all + norm_eps)
    along = inverse * jnp.sum(products, axis=1, keepdims=True) / width_all
    for s in range(sources):
        where = slice(s * part, (s + 1) * part)
        unit = summed_ref[:, where] * inverse
        gain = gain_ref[:, where]
        normed_ref[:, where] = (unit * gain).astype(bf16)
        grad_ref[:, where] = (inverse * (cot_ref[:, where].astype(f32) * gain - unit * along)).astype(bf16)


def head_kernel(
    width_all,
    index,
    streams_ref,
    first1_ref,
    first2_ref,
    halo_ref,
    taps_ref,
    skip_ref,
    filter_ref,
    stats_ref,
    received_ref,
    output_ref,
    gain_ref,
    mixed_ref,
    grad_ref,
    inner_ref,
    share_ref,
    first_ref,
    scratch,
    inverse_ref,
    along_ref,
):
    @pl.when(index == 0)
    def _():
        tokens = stats_ref.shape[1]
        squares = jnp.broadcast_to(stats_ref[0:1, :], (LANES, tokens)).T
        products = jnp.broadcast_to(stats_ref[1:2, :], (LANES, tokens)).T
        inverse = lax.rsqrt(squares / width_all + norm_eps)
        inverse_ref[...] = inverse
        along_ref[...] = inverse * products / width_all

    inverse, along = inverse_ref[...], along_ref[...]
    for col in range(streams_ref.shape[2] // LANES):
        lanes = slice(col * LANES, (col + 1) * LANES)
        cot = columns_of(received_ref, 0, lanes)
        unit = (columns_of(received_ref, 1, lanes) + output_ref[:, lanes].astype(f32)) * inverse
        share_ref[:, lanes] = jnp.sum(cot * unit, axis=0, keepdims=True)
        grad_half = (inverse * (cot * gain_ref[:, lanes] - unit * along)).astype(bf16)
        grad_ref[:, lanes] = grad_half
        grad = grad_half.astype(f32)
        f0 = feature(scratch, halo_ref, streams_ref, taps_ref, 0, lanes, 0)
        inner = (grad * f0).astype(bf16)
        inner_ref[:, lanes] = inner
        first_ref[:TAPS, lanes] = inner[:TAPS]
        features = []
        for s, top in ((1, first1_ref), (2, first2_ref)):
            taps = taps_ref[s, :, lanes]
            now = top[0, :, lanes].astype(f32)
            scratch[6:8, :] = edge(halo_ref, s, lanes)
            scratch[8:24, :] = now
            features.append(taps[0:1] * now[:8] + taps[1:2] * scratch[7:15, :] + taps[2:3] * scratch[6:14, :])
        half = filter_ref[col * PER : (col + 1) * PER].astype(bf16).astype(f32)
        bands = jnp.stack([band(half[g : g + 1], 0, 16) for g in range(PER)])
        conv = convolve(bands, inner, BLOCK, 16)[0][:8]
        grad_gated = conv + skip_ref[:, lanes] * inner[:16].astype(f32)[:8]
        scratch[0:2, :] = (grad[:8] * mixed_ref[0:8, lanes])[:2]
        scratch[2:4, :] = (grad_gated * features[1])[:2]
        scratch[4:6, :] = (grad_gated * features[0])[:2]
        scratch[6:8, :] = jnp.zeros((2, LANES), f32)
        rows = scratch[0:8, :]
        first_ref[TAPS : TAPS + 8, lanes] = rows.astype(bf16)


def sums_kernel(index, streams_ref, halo_ref, gated_ref, inner_ref, grad_ref, mixed_ref, gain_ref, early_ref, scratch):
    length = streams_ref.shape[1]
    blocks = length // BLOCK
    flip = anti_identity(SPAN)
    which = lane_group((BLOCK, blocks * LANES))
    masks = [jnp.where(which == g, 1.0, 0.0).astype(bf16) for g in range(PER)]
    zero = jnp.zeros((SPAN - TAPS - BLOCK, LANES), bf16)
    for col in range(streams_ref.shape[2] // LANES):
        lanes = slice(col * LANES, (col + 1) * LANES)
        gated = gated_ref[:, lanes]
        inner = inner_ref[:, lanes]
        extended = jnp.concatenate([zero, halo_ref[:TAPS, lanes], gated], axis=0)
        backward = dot(flip, windows(extended, length)).astype(bf16)
        grads = jnp.concatenate([inner[at : at + BLOCK] for at in range(0, length, BLOCK)], axis=1)
        pairs = dot_nt(jnp.concatenate([grads * mask for mask in masks], axis=0), backward)
        base = col * 16
        for g in range(PER):
            skewed = pltpu.roll(pairs[g * BLOCK : (g + 1) * BLOCK], SPAN - BLOCK + 1, 1, stride=1, stride_axis=0)
            early_ref[base + g : base + g + 1, :] = jnp.sum(skewed[:, :TAPS], axis=0, keepdims=True)
        early_ref[base + 8 : base + 9, :] = jnp.sum(inner.astype(f32) * gated.astype(f32), axis=0, keepdims=True)
        early_ref[base + 9 : base + 10, :] = gain_ref[:, lanes]
        grad_query = grad_ref[:, lanes].astype(f32) * mixed_ref[:, lanes]
        now = streams_ref[0, :, lanes].astype(f32)
        one, two = shifted(scratch, edge(halo_ref, 0, lanes), now)
        for j, shift in enumerate((now, one, two)):
            early_ref[base + 10 + j : base + 11 + j, :] = jnp.sum(grad_query * shift, axis=0, keepdims=True)
        early_ref[base + 13 : base + 16, :] = jnp.zeros((3, LANES), f32)


def backward_kernel(
    index,
    streams_ref,
    halo_ref,
    taps_ref,
    skip_ref,
    behind_ref,
    grad_ref,
    mixed_ref,
    inner_ref,
    after_ref,
    early_ref,
    stream_grad_ref,
    bundle_ref,
    scratch,
    ahead,
):
    length = streams_ref.shape[1]
    late = scratch.at[0]
    late[0:8, :] = jnp.zeros((8, LANES), f32)
    for col in range(streams_ref.shape[2] // LANES):
        lanes = slice(col * LANES, (col + 1) * LANES)
        inner = inner_ref[:, lanes]
        zero = jnp.zeros((SPAN - TAPS - BLOCK, LANES), bf16)
        extended = jnp.concatenate([inner, after_ref[:TAPS, lanes], zero], axis=0)
        parts = convolve(behind_ref[col * PER : (col + 1) * PER], extended, length)
        grad_gated = jnp.concatenate(parts, axis=0) + skip_ref[:, lanes] * inner.astype(f32)
        shifts, features = {}, {}
        for s in (1, 2):
            now = streams_ref[s - 1, :, lanes].astype(f32)
            one, two = shifted(scratch.at[s], edge(halo_ref, s, lanes), now)
            taps = taps_ref[s, :, lanes]
            shifts[s] = (now, one, two)
            features[s] = taps[0:1] * now + taps[1:2] * one + taps[2:3] * two
        grads = (
            grad_ref[:, lanes].astype(f32) * mixed_ref[:, lanes],
            grad_gated * features[2],
            grad_gated * features[1],
        )
        following = after_ref[TAPS : TAPS + 8, lanes].astype(f32)
        for s in range(3):
            ahead[s, 0:length, :] = grads[s]
            ahead[s, length : length + 2, :] = following[2 * s : 2 * s + 2]
            taps = taps_ref[s, :, lanes]
            stream_grad_ref[s, :, lanes] = (
                taps[0:1] * grads[s] + taps[1:2] * ahead[s, 1 : length + 1, :] + taps[2:3] * ahead[s, 2 : length + 2, :]
            ).astype(bf16)
        for s in (1, 2):
            for j in range(3):
                row = (s - 1) * 3 + j
                late[row : row + 1, :] = jnp.sum(grads[s] * shifts[s][j], axis=0, keepdims=True)
        base = col * 24
        bundle_ref[base : base + 16, :] = early_ref[col * 16 : (col + 1) * 16, :].astype(bf16)
        bundle_ref[base + 16 : base + 24, :] = late[0:8, :].astype(bf16)


def from_behind(value, axis, steps):
    count = lax.axis_size(axis)
    first, last = (max(0, -steps), min(count, count - steps))
    return lax.ppermute(value, axis, [(source, source + steps) for source in range(first, last)])


def sent_to(value, axis, distances):
    half = value
    if value.dtype != bf16:
        value = lax.reduce_precision(value, 8, 7)
        half = value.astype(bf16)
    count = lax.axis_size(axis)
    return value, [lax.ppermute(half, axis, [(i, i ^ d) for i in range(count)]) for d in distances]


def added(value, others):
    terms = [term.astype(f32) for term in (value, *others)]
    while len(terms) > 1:
        terms = [terms[i] + terms[i + 1] for i in range(0, len(terms), 2)]
    return terms[0]


def close_kernel(mine_ref, other_ref, long_ref, short_ref, skip_ref, gain_ref):
    total = mine_ref[...].astype(f32) + other_ref[...].astype(f32)
    for col in range(skip_ref.shape[1] // LANES):
        lanes = slice(col * LANES, (col + 1) * LANES)
        at = col * 24
        long_ref[col * PER : (col + 1) * PER, :] = total[at : at + PER]
        skip_ref[:, lanes] = total[at + 8 : at + 9]
        gain_ref[:, lanes] = total[at + 9 : at + 10]
        for j in range(3):
            short_ref[0, j : j + 1, lanes] = total[at + 10 + j : at + 11 + j]
            for s in (1, 2):
                row = at + 16 + (s - 1) * 3 + j
                short_ref[s, j : j + 1, lanes] = total[row : row + 1]


def streamed(body, name, count, inputs, outputs, scratch_shapes=()):
    inputs = [(array if isinstance(array, tuple) else (array,), picks, split) for array, picks, split in inputs]
    firsts = [sum(len(arrays) for arrays, _, _ in inputs[:at]) for at in range(len(inputs) + 1)]

    def piece(ref, split, i, count=count):
        size = ref.shape[split] // count
        start = i * size
        if not isinstance(start, int):
            start = pl.multiple_of(start, size)
        return ref.at[tuple(pl.ds(start, size) if d == split else slice(None) for d in range(len(ref.shape)))]

    def kernel(*refs):
        n, m = len(inputs), len(outputs)
        sources, refs = refs[: firsts[-1]], refs[firsts[-1] :]
        targets, held, made = refs[:m], refs[m : m + n], refs[m + n : 2 * m + n]
        in_sem, out_sem = refs[2 * m + n : 2 * m + n + 2]
        own = refs[2 * m + n + 2 :]

        def fetch(at, i, array=0):
            arrays, picks, split = inputs[at]
            source, target = sources[firsts[at] + array], held[at]
            if picks:
                source = source.at[tuple(pl.ds(*picks[d]) if d in picks else slice(None) for d in range(arrays[0].ndim))]
            if isinstance(split, int):
                share = count // len(arrays)
                source, target = piece(source, split, i - array * share, share), piece(target, split, i)
            elif len(arrays) > 1:
                target = piece(target, split[0], array, len(arrays))
            return pltpu.make_async_copy(source, target, in_sem.at[at, array if isinstance(split, tuple) else i])

        def send(at, i):
            split = outputs[at][2]
            source, target = made[at], targets[at]
            if isinstance(split, int):
                source, target = piece(source, split, i), piece(target, split, i)
            return pltpu.make_async_copy(source, target, out_sem.at[at, i])

        whole_in = [at for at in range(n) if not isinstance(inputs[at][2], int)]
        split_in = [at for at in range(n) if isinstance(inputs[at][2], int)]
        whole_out = [at for at in range(m) if not isinstance(outputs[at][2], int)]
        split_out = [at for at in range(m) if isinstance(outputs[at][2], int)]
        whole_parts = [(at, array) for at in whole_in for array in range(len(inputs[at][0]))]
        for at, array in whole_parts:
            fetch(at, 0, array).start()
        for i in range(count):
            for at in split_in:
                fetch(at, i, i * len(inputs[at][0]) // count).start()
        for at, array in whole_parts:
            fetch(at, 0, array).wait()

        def step(i, carry):
            for at in split_in:
                target = piece(held[at], inputs[at][2], i)
                pltpu.make_async_copy(target, target, in_sem.at[at, i]).wait()
            views = [
                ref if split is None else piece(ref, split if isinstance(split, int) else split[0], i)
                for ref, split in zip((*held, *made), [x[2] for x in (*inputs, *outputs)])
            ]
            body(i, *views, *own)
            for at in split_out:
                send(at, i).start()
            return carry

        lax.fori_loop(0, count, step, 0)
        for at in whole_out:
            send(at, 0).start()
        for at in whole_out:
            send(at, 0).wait()
        for i in range(count):
            for at in split_out:
                send(at, i).wait()

    def held_shape(arrays, picks, split):
        shape = [picks[d][1] if d in picks else arrays[0].shape[d] for d in range(arrays[0].ndim)]
        if len(arrays) > 1:
            shape[split if isinstance(split, int) else split[0]] *= len(arrays)
        return tuple(shape)

    return pl.pallas_call(
        kernel,
        in_specs=[pl.BlockSpec(memory_space=pl.ANY)] * firsts[-1],
        out_specs=[pl.BlockSpec(memory_space=pl.ANY)] * len(outputs),
        out_shape=[jax.ShapeDtypeStruct(shape, dtype) for shape, dtype, _ in outputs],
        scratch_shapes=[pltpu.VMEM(held_shape(*each), each[0][0].dtype) for each in inputs]
        + [pltpu.VMEM(shape, dtype) for shape, dtype, _ in outputs]
        + [pltpu.SemaphoreType.DMA((len(inputs), count)), pltpu.SemaphoreType.DMA((len(outputs), count))]
        + list(scratch_shapes),
        compiler_params=params(VMEM_LIMIT),
        cost_estimate=pl.CostEstimate(flops=0, bytes_accessed=8000, transcendentals=0),
        name=name,
    )(*(array for arrays, _, _ in inputs for array in arrays))


def local(residual, streams, short_filter, long_filter, skip, gain, cotangent):
    tokens_here, channels = streams.shape[1:]
    groups = long_filter.shape[0]
    rows_here, width_all = residual.shape
    owners = lax.axis_size("tensor")
    assert long_filter.shape[1] == TAPS and channels == groups * WIDTH and tokens_here % (2 * TAPS) == 0
    columns = channels // LANES
    halves = 1
    part = channels // halves
    count = max(halves, channels // STEP)
    skip_row = skip[None, :]
    gain_row = gain[None, :]
    gain_here = lax.dynamic_slice_in_dim(gain, lax.axis_index("tensor") * channels, channels)[None, :]

    spec = pl.BlockSpec

    def padded(count=None):
        shape = (tokens_here + 8, LANES)
        return pltpu.VMEM(shape if count is None else (count,) + shape, f32)

    def kernel(body, name, micros, limit=VMEM_LIMIT, **how):
        return pl.pallas_call(
            body,
            compiler_params=params(limit),
            cost_estimate=pl.CostEstimate(flops=0, bytes_accessed=micros * 1000, transcendentals=0),
            name=name,
            **how,
        )

    packed, halo = kernel(
        open_kernel,
        "open",
        3,
        in_specs=[spec(memory_space=pl.ANY)] * 3 + [spec(memory_space=pltpu.VMEM)],
        out_specs=[spec(memory_space=pl.ANY)] * 2,
        out_shape=[
            jax.ShapeDtypeStruct((owners, 2, rows_here, channels), bf16),
            jax.ShapeDtypeStruct((TAPS + 8, channels), bf16),
        ],
        scratch_shapes=[
            pltpu.VMEM((owners, 2, rows_here, channels), bf16),
            pltpu.VMEM((2, TAPS + 16, channels), bf16),
            pltpu.VMEM((16, channels), bf16),
            pltpu.VMEM((TAPS + 8, channels), bf16),
            pltpu.VMEM((3, TAPS + 16, LANES), f32),
            pltpu.SemaphoreType.DMA((owners, 2)),
            pltpu.SemaphoreType.DMA((owners, 2)),
            pltpu.SemaphoreType.DMA((3,)),
        ],
    )(cotangent, residual, streams, short_filter)
    halo = from_behind(halo, "dp", 1)
    received = lax.all_to_all(packed, "tensor", split_axis=0, concat_axis=0, tiled=True)

    band_shape = jax.ShapeDtypeStruct((groups, BLOCK, SPAN), bf16)
    each = min(groups, 16)
    ahead_bands, behind_bands = kernel(
        bands_kernel,
        "bands",
        5,
        grid=(groups // each,),
        in_specs=[spec((each, TAPS), lambda i: (i, 0))],
        out_specs=[spec((each, BLOCK, SPAN), lambda i: (i, 0, 0))] * 2,
        out_shape=[band_shape] * 2,
    )(long_filter)

    output, mixed, gated = streamed(
        forward_kernel,
        "forward",
        count,
        [(streams, {}, 2), (halo, {}, 1), (short_filter, {}, (2,)), (skip_row, {}, (1,)), (ahead_bands, {}, 0)],
        [((tokens_here, channels), t, 1) for t in (bf16, f32, bf16)],
        [padded(3)],
    )

    (stats,) = streamed(
        functools.partial(stats_kernel, count),
        "stats",
        count,
        [(received, {}, 3), (output, {}, 1), (gain_here, {}, (1,))],
        [((2, tokens_here), f32, None)],
        [pltpu.VMEM((tokens_here, LANES), f32)] * 2,
    )
    stats = lax.psum(stats, "tensor")
    heads = []
    for k in range(halves):
        here = (k * part, part)
        heads.append(
            streamed(
                functools.partial(head_kernel, width_all),
                "head",
                count // halves,
                [
                    (streams, {0: (0, 1), 2: here}, 2),
                    (streams, {0: (1, 1), 1: (0, 16), 2: here}, 2),
                    (streams, {0: (2, 1), 1: (0, 16), 2: here}, 2),
                    (halo, {1: here}, 1),
                    (short_filter, {2: here}, (2,)),
                    (skip_row, {1: here}, (1,)),
                    (long_filter, {0: (k * groups // halves, groups // halves)}, 0),
                    (stats, {}, None),
                    (received, {3: here}, 3),
                    (output, {1: here}, 1),
                    (gain_here, {1: here}, (1,)),
                    (mixed, {0: (0, 16), 1: here}, 1),
                ],
                [
                    ((tokens_here, part), bf16, 1),
                    ((tokens_here, part), bf16, 1),
                    ((1, part), f32, (1,)),
                    ((TAPS + 8, part), bf16, 1),
                ],
                [padded()] + [pltpu.VMEM((tokens_here, LANES), f32)] * 2,
            )
        )
    grads, inner, shares, first = (tuple(column) for column in zip(*heads))
    after = [from_behind(piece, "dp", -1) for piece in first]
    leaving, inner = lax.optimization_barrier((output, inner))
    rows_received = lax.all_to_all(
        leaving.reshape(owners, rows_here, channels), "tensor", split_axis=0, concat_axis=0, tiled=True
    )

    (early,) = streamed(
        sums_kernel,
        "sums",
        count,
        [
            (streams, {0: (0, 1)}, 2),
            (halo, {}, 1),
            (gated, {}, 1),
            (inner, {}, 1),
            (grads, {}, 1),
            (mixed, {}, 1),
            (shares, {}, (1,)),
        ],
        [((columns * 16, LANES), f32, 0)],
        [padded()],
    )

    stream_grad, bundle = streamed(
        backward_kernel,
        "backward",
        count,
        [
            (streams, {0: (1, 2)}, 2),
            (halo, {}, 1),
            (short_filter, {}, (2,)),
            (skip_row, {}, (1,)),
            (behind_bands, {}, 0),
            (grads, {}, 1),
            (mixed, {}, 1),
            (inner, {}, 1),
            (tuple(after), {}, 1),
            (early, {}, 0),
        ],
        [(streams.shape, bf16, 2), ((columns * 24, LANES), bf16, 0)],
        [padded(3), padded(3)],
    )
    bits = (lax.axis_size("dp") - 1).bit_length()
    stages = [[1 << n] if n + 1 == bits else [1 << n, 2 << n, 3 << n] for n in range(0, bits, 2)]
    total = bundle
    for stage in stages[:-1]:
        mine, others = sent_to(total, "dp", stage)
        total = added(mine, others)
    block = min(rows_here, 32)
    by_rows = spec((block, width_all), lambda i: (i, 0))
    normed, grad_residual = kernel(
        norm_kernel,
        "norm",
        4,
        NORM_LIMIT,
        grid=(rows_here // block,),
        in_specs=[
            spec((owners, block, channels), lambda i: (0, i, 0)),
            by_rows,
            by_rows,
            spec((1, width_all), lambda i: (0, 0)),
        ],
        out_specs=[by_rows, by_rows],
        out_shape=[jax.ShapeDtypeStruct(residual.shape, bf16)] * 2,
        scratch_shapes=[pltpu.VMEM((block, width_all), f32)],
    )(rows_received, residual, cotangent, gain_row)

    mine, others = sent_to(total, "dp", stages[-1])
    mine, normed, grad_residual = lax.optimization_barrier((mine, normed, grad_residual))
    mine, other = (mine, others[0]) if len(others) == 1 else (added(mine, others[:1]), added(others[1], others[2:]))
    long_grad, short_grad, skip_grad, gain_grad = kernel(
        close_kernel,
        "close",
        1,
        SMALL_LIMIT,
        out_shape=[
            jax.ShapeDtypeStruct((groups, TAPS), f32),
            jax.ShapeDtypeStruct((3, 3, channels), f32),
            jax.ShapeDtypeStruct((1, channels), f32),
            jax.ShapeDtypeStruct((1, channels), f32),
        ],
    )(mine, other)
    skip_grad, gain_grad = skip_grad.reshape(channels), gain_grad.reshape(channels)
    return (normed, grad_residual, stream_grad, long_grad, short_grad, skip_grad, gain_grad)


def solution(mesh):
    placed = (
        P(("dp", "tensor"), None),
        P(None, "dp", "tensor"),
        P(None, None, "tensor"),
        P("tensor", None),
        P("tensor"),
        P(),
        P(("dp", "tensor"), None),
    )
    return jax.shard_map(
        local,
        mesh=mesh,
        in_specs=placed,
        out_specs=(
            P(("dp", "tensor"), None),
            P(("dp", "tensor"), None),
            P(None, "dp", "tensor"),
            P("tensor", None),
            P(None, None, "tensor"),
            P("tensor"),
            P("tensor"),
        ),
        check_vma=False,
    )
```

```python
import functools

import jax
import jax.numpy as jnp
from jax import lax
from jax.experimental import pallas as pl
from jax.experimental.pallas import tpu as pltpu
from jax.sharding import PartitionSpec as P

norm_eps = 1e-05
LANES = 128
TAPS = 128
WIDTH = 16
PER = LANES // WIDTH
BLOCK = 64
SPAN = 256
VMEM_LIMIT = 63.5
SMALL_LIMIT = 8
NORM_LIMIT = 63.5
STEP = 512
f32 = jnp.float32
bf16 = jnp.bfloat16


def params(limit):
    return pltpu.CompilerParams(vmem_limit_bytes=int(limit * 2**20))


def dot(a, b):
    return lax.dot_general(a, b, (((1,), (0,)), ((), ())), preferred_element_type=f32)


def dot_nt(a, b):
    return lax.dot_general(a, b, (((1,), (1,)), ((), ())), preferred_element_type=f32)


def lane_group(shape):
    return lax.broadcasted_iota(jnp.int32, shape, len(shape) - 1) % LANES // WIDTH


def pick_groups(stacked, rows):
    lane = lane_group((rows, LANES))
    picked = []
    for at in range(0, stacked.shape[1], LANES):
        parts = [stacked[g * rows : (g + 1) * rows, at : at + LANES] for g in range(PER)]
        bit = PER // 2
        while len(parts) > 1:
            upper = lane % (2 * bit) >= bit
            half = len(parts) // 2
            parts = [jnp.where(upper, parts[i + half], parts[i]) for i in range(half)]
            bit //= 2
        picked.append(parts[0])
    return jnp.concatenate(picked, axis=1)


def shifted(scratch, halo, current):
    length = current.shape[0]
    scratch[6:8, :] = halo
    scratch[8 : 8 + length, :] = current
    return scratch[7 : 7 + length, :], scratch[6 : 6 + length, :]


def band(row, first, rows):
    wide = jnp.concatenate([row, jnp.zeros((1, SPAN - TAPS), f32)], axis=1)
    return pltpu.roll(jnp.broadcast_to(wide, (rows, SPAN)), first, 1, stride=1, stride_axis=0).astype(bf16)


def anti_identity(size):
    total = lax.broadcasted_iota(jnp.int32, (size, size), 0) + lax.broadcasted_iota(jnp.int32, (size, size), 1)
    return jnp.where(total == size - 1, 1.0, 0.0).astype(bf16)


def windows(extended, length):
    return jnp.concatenate([extended[at : at + SPAN] for at in range(0, length, BLOCK)], axis=1)


def convolve(bands, extended, length, rows=BLOCK):
    stacked = dot(bands.reshape(PER * rows, SPAN), windows(extended, length))
    result = pick_groups(stacked, rows)
    return [result[:, at : at + LANES] for at in range(0, result.shape[1], LANES)]


def bands_kernel(filter_ref, ahead_ref, behind_ref):
    half = filter_ref[...].astype(bf16)
    back = dot(half, anti_identity(TAPS))
    fore = half.astype(f32)
    for g in range(half.shape[0]):
        ahead_ref[g] = band(back[g : g + 1], SPAN - TAPS - BLOCK + 1, BLOCK)
        behind_ref[g] = band(fore[g : g + 1], 0, BLOCK)


def open_kernel(
    cot_ref, residual_ref, streams_ref, taps_ref, packed_ref, halo_ref, pieces, ends, last, rows, scratch, in_sem, out_sem, end_sem
):
    owners, _, _, channels = packed_ref.shape
    length = streams_ref.shape[1]
    back = ends.shape[1]
    ending = [
        pltpu.make_async_copy(streams_ref.at[pl.ds(1, 2), pl.ds(length - back, back), :], ends, end_sem.at[0]),
        pltpu.make_async_copy(streams_ref.at[0, pl.ds(length - 16, 16), :], last, end_sem.at[1]),
    ]
    for copy in ending:
        copy.start()
    places = [(j, which) for j in range(owners) for which in range(2)]
    arriving = [
        pltpu.make_async_copy(
            (cot_ref, residual_ref)[which].at[:, pl.ds(j * channels, channels)], pieces.at[j, which], in_sem.at[j, which]
        )
        for j, which in places
    ]
    leaving = [
        pltpu.make_async_copy(pieces.at[j, which], packed_ref.at[j, which], out_sem.at[j, which]) for j, which in places
    ]
    for copy in arriving:
        copy.start()
    for copy in ending:
        copy.wait()
    for col in range(channels // LANES):
        lanes = slice(col * LANES, (col + 1) * LANES)
        features = []
        for s in (1, 2):
            scratch[s, 0:back, :] = ends[s - 1, :, lanes].astype(f32)
            taps = taps_ref[s, :, lanes]
            now, one, two = (scratch[s, back - TAPS - n : back - n, :] for n in range(3))
            features.append(taps[0:1] * now + taps[1:2] * one + taps[2:3] * two)
        rows[:TAPS, lanes] = (features[0] * features[1]).astype(bf16)
        edges = scratch.at[0]
        edges[0:2, :] = last[:, lanes].astype(f32)[14:]
        edges[2:4, :] = scratch[1, back - 2 : back, :]
        edges[4:6, :] = scratch[2, back - 2 : back, :]
        edges[6:8, :] = jnp.zeros((2, LANES), f32)
        rows[TAPS : TAPS + 8, lanes] = edges[0:8, :].astype(bf16)
        if col == 0:
            for copy, onward in zip(arriving, leaving):
                copy.wait()
                onward.start()
    ending = pltpu.make_async_copy(rows, halo_ref, end_sem.at[2])
    ending.start()
    for copy in leaving:
        copy.wait()
    ending.wait()


def edge(halo_ref, s, lanes):
    return halo_ref[TAPS : TAPS + 8, lanes].astype(f32)[2 * s : 2 * s + 2]


def feature(scratch, halo_ref, streams_ref, taps_ref, s, lanes, index):
    now = streams_ref[index, :, lanes].astype(f32)
    one, two = shifted(scratch, edge(halo_ref, s, lanes), now)
    taps = taps_ref[s, :, lanes]
    return taps[0:1] * now + taps[1:2] * one + taps[2:3] * two


def forward_kernel(index, streams_ref, halo_ref, taps_ref, skip_ref, ahead_ref, output_ref, mixed_ref, gated_ref, scratch):
    length = streams_ref.shape[1]
    for col in range(streams_ref.shape[2] // LANES):
        lanes = slice(col * LANES, (col + 1) * LANES)
        f0, f1, f2 = (feature(scratch.at[s], halo_ref, streams_ref, taps_ref, s, lanes, s) for s in range(3))
        gated = (f1 * f2).astype(bf16)
        gated_ref[:, lanes] = gated
        zero = jnp.zeros((SPAN - TAPS - BLOCK, LANES), bf16)
        extended = jnp.concatenate([zero, halo_ref[:TAPS, lanes], gated], axis=0)
        skip = skip_ref[:, lanes]
        for b, result in enumerate(convolve(ahead_ref[col * PER : (col + 1) * PER], extended, length)):
            rows = slice(b * BLOCK, (b + 1) * BLOCK)
            mixed = result + skip * gated[rows].astype(f32)
            mixed_ref[rows, lanes] = mixed
            output_ref[rows, lanes] = (f0[rows] * mixed).astype(bf16)


def columns_of(received_ref, which, lanes):
    piece = received_ref[:, which, :, lanes].astype(f32)
    return piece.reshape(piece.shape[0] * piece.shape[1], LANES)


def stats_kernel(count, index, received_ref, output_ref, gain_ref, stats_ref, squares_ref, products_ref):
    @pl.when(index == 0)
    def _():
        squares_ref[...] = jnp.zeros_like(squares_ref)
        products_ref[...] = jnp.zeros_like(products_ref)

    squares, products = squares_ref[...], products_ref[...]
    for col in range(output_ref.shape[1] // LANES):
        lanes = slice(col * LANES, (col + 1) * LANES)
        summed = columns_of(received_ref, 1, lanes) + output_ref[:, lanes].astype(f32)
        squares = squares + summed * summed
        products = products + columns_of(received_ref, 0, lanes) * gain_ref[:, lanes] * summed
    squares_ref[...] = squares
    products_ref[...] = products

    @pl.when(index == count - 1)
    def _():
        for row, sums in ((0, squares), (1, products)):
            stats_ref[row : row + 1, :] = jnp.sum(sums.T, axis=0, keepdims=True)


def norm_kernel(received_ref, residual_ref, cot_ref, gain_ref, normed_ref, grad_ref, summed_ref):
    sources, rows, part = received_ref.shape
    width_all = residual_ref.shape[1]
    squares = jnp.zeros((rows, LANES), f32)
    products = jnp.zeros((rows, LANES), f32)
    for s in range(sources):
        where = slice(s * part, (s + 1) * part)
        summed = residual_ref[:, where].astype(f32) + received_ref[s].astype(f32)
        summed_ref[:, where] = summed
        scaled = cot_ref[:, where].astype(f32) * gain_ref[:, where]
        both = (summed * summed, scaled * summed)
        for col in range(part // LANES):
            lanes = slice(col * LANES, (col + 1) * LANES)
            squares = squares + both[0][:, lanes]
            products = products + both[1][:, lanes]
    inverse = lax.rsqrt(jnp.sum(squares, axis=1, keepdims=True) / width_all + norm_eps)
    along = inverse * jnp.sum(products, axis=1, keepdims=True) / width_all
    for s in range(sources):
        where = slice(s * part, (s + 1) * part)
        unit = summed_ref[:, where] * inverse
        gain = gain_ref[:, where]
        normed_ref[:, where] = (unit * gain).astype(bf16)
        grad_ref[:, where] = (inverse * (cot_ref[:, where].astype(f32) * gain - unit * along)).astype(bf16)


def head_kernel(
    width_all,
    index,
    streams_ref,
    first1_ref,
    first2_ref,
    halo_ref,
    taps_ref,
    skip_ref,
    filter_ref,
    stats_ref,
    received_ref,
    output_ref,
    gain_ref,
    mixed_ref,
    grad_ref,
    inner_ref,
    share_ref,
    first_ref,
    scratch,
    inverse_ref,
    along_ref,
):
    @pl.when(index == 0)
    def _():
        tokens = stats_ref.shape[1]
        squares = jnp.broadcast_to(stats_ref[0:1, :], (LANES, tokens)).T
        products = jnp.broadcast_to(stats_ref[1:2, :], (LANES, tokens)).T
        inverse = lax.rsqrt(squares / width_all + norm_eps)
        inverse_ref[...] = inverse
        along_ref[...] = inverse * products / width_all

    inverse, along = inverse_ref[...], along_ref[...]
    for col in range(streams_ref.shape[2] // LANES):
        lanes = slice(col * LANES, (col + 1) * LANES)
        cot = columns_of(received_ref, 0, lanes)
        unit = (columns_of(received_ref, 1, lanes) + output_ref[:, lanes].astype(f32)) * inverse
        share_ref[:, lanes] = jnp.sum(cot * unit, axis=0, keepdims=True)
        grad_half = (inverse * (cot * gain_ref[:, lanes] - unit * along)).astype(bf16)
        grad_ref[:, lanes] = grad_half
        grad = grad_half.astype(f32)
        f0 = feature(scratch, halo_ref, streams_ref, taps_ref, 0, lanes, 0)
        inner = (grad * f0).astype(bf16)
        inner_ref[:, lanes] = inner
        first_ref[:TAPS, lanes] = inner[:TAPS]
        features = []
        for s, top in ((1, first1_ref), (2, first2_ref)):
            taps = taps_ref[s, :, lanes]
            now = top[0, :, lanes].astype(f32)
            scratch[6:8, :] = edge(halo_ref, s, lanes)
            scratch[8:24, :] = now
            features.append(taps[0:1] * now[:8] + taps[1:2] * scratch[7:15, :] + taps[2:3] * scratch[6:14, :])
        half = filter_ref[col * PER : (col + 1) * PER].astype(bf16).astype(f32)
        bands = jnp.stack([band(half[g : g + 1], 0, 16) for g in range(PER)])
        conv = convolve(bands, inner, BLOCK, 16)[0][:8]
        grad_gated = conv + skip_ref[:, lanes] * inner[:16].astype(f32)[:8]
        scratch[0:2, :] = (grad[:8] * mixed_ref[0:8, lanes])[:2]
        scratch[2:4, :] = (grad_gated * features[1])[:2]
        scratch[4:6, :] = (grad_gated * features[0])[:2]
        scratch[6:8, :] = jnp.zeros((2, LANES), f32)
        rows = scratch[0:8, :]
        first_ref[TAPS : TAPS + 8, lanes] = rows.astype(bf16)


def sums_kernel(index, streams_ref, halo_ref, gated_ref, inner_ref, grad_ref, mixed_ref, gain_ref, early_ref, scratch):
    length = streams_ref.shape[1]
    blocks = length // BLOCK
    flip = anti_identity(SPAN)
    which = lane_group((BLOCK, blocks * LANES))
    masks = [jnp.where(which == g, 1.0, 0.0).astype(bf16) for g in range(PER)]
    zero = jnp.zeros((SPAN - TAPS - BLOCK, LANES), bf16)
    for col in range(streams_ref.shape[2] // LANES):
        lanes = slice(col * LANES, (col + 1) * LANES)
        gated = gated_ref[:, lanes]
        inner = inner_ref[:, lanes]
        extended = jnp.concatenate([zero, halo_ref[:TAPS, lanes], gated], axis=0)
        backward = dot(flip, windows(extended, length)).astype(bf16)
        grads = jnp.concatenate([inner[at : at + BLOCK] for at in range(0, length, BLOCK)], axis=1)
        pairs = dot_nt(jnp.concatenate([grads * mask for mask in masks], axis=0), backward)
        base = col * 16
        for g in range(PER):
            skewed = pltpu.roll(pairs[g * BLOCK : (g + 1) * BLOCK], SPAN - BLOCK + 1, 1, stride=1, stride_axis=0)
            early_ref[base + g : base + g + 1, :] = jnp.sum(skewed[:, :TAPS], axis=0, keepdims=True)
        early_ref[base + 8 : base + 9, :] = jnp.sum(inner.astype(f32) * gated.astype(f32), axis=0, keepdims=True)
        early_ref[base + 9 : base + 10, :] = gain_ref[:, lanes]
        grad_query = grad_ref[:, lanes].astype(f32) * mixed_ref[:, lanes]
        now = streams_ref[0, :, lanes].astype(f32)
        one, two = shifted(scratch, edge(halo_ref, 0, lanes), now)
        for j, shift in enumerate((now, one, two)):
            early_ref[base + 10 + j : base + 11 + j, :] = jnp.sum(grad_query * shift, axis=0, keepdims=True)
        early_ref[base + 13 : base + 16, :] = jnp.zeros((3, LANES), f32)


def backward_kernel(
    index,
    streams_ref,
    halo_ref,
    taps_ref,
    skip_ref,
    behind_ref,
    grad_ref,
    mixed_ref,
    inner_ref,
    after_ref,
    early_ref,
    stream_grad_ref,
    bundle_ref,
    scratch,
    ahead,
):
    length = streams_ref.shape[1]
    late = scratch.at[0]
    late[0:8, :] = jnp.zeros((8, LANES), f32)
    for col in range(streams_ref.shape[2] // LANES):
        lanes = slice(col * LANES, (col + 1) * LANES)
        inner = inner_ref[:, lanes]
        zero = jnp.zeros((SPAN - TAPS - BLOCK, LANES), bf16)
        extended = jnp.concatenate([inner, after_ref[:TAPS, lanes], zero], axis=0)
        parts = convolve(behind_ref[col * PER : (col + 1) * PER], extended, length)
        grad_gated = jnp.concatenate(parts, axis=0) + skip_ref[:, lanes] * inner.astype(f32)
        shifts, features = {}, {}
        for s in (1, 2):
            now = streams_ref[s - 1, :, lanes].astype(f32)
            one, two = shifted(scratch.at[s], edge(halo_ref, s, lanes), now)
            taps = taps_ref[s, :, lanes]
            shifts[s] = (now, one, two)
            features[s] = taps[0:1] * now + taps[1:2] * one + taps[2:3] * two
        grads = (
            grad_ref[:, lanes].astype(f32) * mixed_ref[:, lanes],
            grad_gated * features[2],
            grad_gated * features[1],
        )
        following = after_ref[TAPS : TAPS + 8, lanes].astype(f32)
        for s in range(3):
            ahead[s, 0:length, :] = grads[s]
            ahead[s, length : length + 2, :] = following[2 * s : 2 * s + 2]
            taps = taps_ref[s, :, lanes]
            stream_grad_ref[s, :, lanes] = (
                taps[0:1] * grads[s] + taps[1:2] * ahead[s, 1 : length + 1, :] + taps[2:3] * ahead[s, 2 : length + 2, :]
            ).astype(bf16)
        for s in (1, 2):
            for j in range(3):
                row = (s - 1) * 3 + j
                late[row : row + 1, :] = jnp.sum(grads[s] * shifts[s][j], axis=0, keepdims=True)
        base = col * 24
        bundle_ref[base : base + 16, :] = early_ref[col * 16 : (col + 1) * 16, :].astype(bf16)
        bundle_ref[base + 16 : base + 24, :] = late[0:8, :].astype(bf16)


def from_behind(value, axis, steps):
    count = lax.axis_size(axis)
    first, last = (max(0, -steps), min(count, count - steps))
    return lax.ppermute(value, axis, [(source, source + steps) for source in range(first, last)])


def sent_to(value, axis, distances):
    half = value
    if value.dtype != bf16:
        value = lax.reduce_precision(value, 8, 7)
        half = value.astype(bf16)
    count = lax.axis_size(axis)
    return value, [lax.ppermute(half, axis, [(i, i ^ d) for i in range(count)]) for d in distances]


def added(value, others):
    terms = [term.astype(f32) for term in (value, *others)]
    while len(terms) > 1:
        terms = [terms[i] + terms[i + 1] for i in range(0, len(terms), 2)]
    return terms[0]


def close_kernel(mine_ref, other_ref, long_ref, short_ref, skip_ref, gain_ref):
    total = mine_ref[...].astype(f32) + other_ref[...].astype(f32)
    for col in range(skip_ref.shape[1] // LANES):
        lanes = slice(col * LANES, (col + 1) * LANES)
        at = col * 24
        long_ref[col * PER : (col + 1) * PER, :] = total[at : at + PER]
        skip_ref[:, lanes] = total[at + 8 : at + 9]
        gain_ref[:, lanes] = total[at + 9 : at + 10]
        for j in range(3):
            short_ref[0, j : j + 1, lanes] = total[at + 10 + j : at + 11 + j]
            for s in (1, 2):
                row = at + 16 + (s - 1) * 3 + j
                short_ref[s, j : j + 1, lanes] = total[row : row + 1]


def streamed(body, name, count, inputs, outputs, scratch_shapes=()):
    inputs = [(array if isinstance(array, tuple) else (array,), picks, split) for array, picks, split in inputs]
    firsts = [sum(len(arrays) for arrays, _, _ in inputs[:at]) for at in range(len(inputs) + 1)]

    def piece(ref, split, i, count=count):
        size = ref.shape[split] // count
        start = i * size
        if not isinstance(start, int):
            start = pl.multiple_of(start, size)
        return ref.at[tuple(pl.ds(start, size) if d == split else slice(None) for d in range(len(ref.shape)))]

    def kernel(*refs):
        n, m = len(inputs), len(outputs)
        sources, refs = refs[: firsts[-1]], refs[firsts[-1] :]
        targets, held, made = refs[:m], refs[m : m + n], refs[m + n : 2 * m + n]
        in_sem, out_sem = refs[2 * m + n : 2 * m + n + 2]
        own = refs[2 * m + n + 2 :]

        def fetch(at, i, array=0):
            arrays, picks, split = inputs[at]
            source, target = sources[firsts[at] + array], held[at]
            if picks:
                source = source.at[tuple(pl.ds(*picks[d]) if d in picks else slice(None) for d in range(arrays[0].ndim))]
            if isinstance(split, int):
                share = count // len(arrays)
                source, target = piece(source, split, i - array * share, share), piece(target, split, i)
            elif len(arrays) > 1:
                target = piece(target, split[0], array, len(arrays))
            return pltpu.make_async_copy(source, target, in_sem.at[at, array if isinstance(split, tuple) else i])

        def send(at, i):
            split = outputs[at][2]
            source, target = made[at], targets[at]
            if isinstance(split, int):
                source, target = piece(source, split, i), piece(target, split, i)
            return pltpu.make_async_copy(source, target, out_sem.at[at, i])

        whole_in = [at for at in range(n) if not isinstance(inputs[at][2], int)]
        split_in = [at for at in range(n) if isinstance(inputs[at][2], int)]
        whole_out = [at for at in range(m) if not isinstance(outputs[at][2], int)]
        split_out = [at for at in range(m) if isinstance(outputs[at][2], int)]
        whole_parts = [(at, array) for at in whole_in for array in range(len(inputs[at][0]))]
        for at, array in whole_parts:
            fetch(at, 0, array).start()
        for i in range(count):
            for at in split_in:
                fetch(at, i, i * len(inputs[at][0]) // count).start()
        for at, array in whole_parts:
            fetch(at, 0, array).wait()

        def step(i, carry):
            for at in split_in:
                target = piece(held[at], inputs[at][2], i)
                pltpu.make_async_copy(target, target, in_sem.at[at, i]).wait()
            views = [
                ref if split is None else piece(ref, split if isinstance(split, int) else split[0], i)
                for ref, split in zip((*held, *made), [x[2] for x in (*inputs, *outputs)])
            ]
            body(i, *views, *own)
            for at in split_out:
                send(at, i).start()
            return carry

        lax.fori_loop(0, count, step, 0)
        for at in whole_out:
            send(at, 0).start()
        for at in whole_out:
            send(at, 0).wait()
        for i in range(count):
            for at in split_out:
                send(at, i).wait()

    def held_shape(arrays, picks, split):
        shape = [picks[d][1] if d in picks else arrays[0].shape[d] for d in range(arrays[0].ndim)]
        if len(arrays) > 1:
            shape[split if isinstance(split, int) else split[0]] *= len(arrays)
        return tuple(shape)

    return pl.pallas_call(
        kernel,
        in_specs=[pl.BlockSpec(memory_space=pl.ANY)] * firsts[-1],
        out_specs=[pl.BlockSpec(memory_space=pl.ANY)] * len(outputs),
        out_shape=[jax.ShapeDtypeStruct(shape, dtype) for shape, dtype, _ in outputs],
        scratch_shapes=[pltpu.VMEM(held_shape(*each), each[0][0].dtype) for each in inputs]
        + [pltpu.VMEM(shape, dtype) for shape, dtype, _ in outputs]
        + [pltpu.SemaphoreType.DMA((len(inputs), count)), pltpu.SemaphoreType.DMA((len(outputs), count))]
        + list(scratch_shapes),
        compiler_params=params(VMEM_LIMIT),
        cost_estimate=pl.CostEstimate(flops=0, bytes_accessed=8000, transcendentals=0),
        name=name,
    )(*(array for arrays, _, _ in inputs for array in arrays))


def local(residual, streams, short_filter, long_filter, skip, gain, cotangent):
    tokens_here, channels = streams.shape[1:]
    groups = long_filter.shape[0]
    rows_here, width_all = residual.shape
    owners = lax.axis_size("tensor")
    assert long_filter.shape[1] == TAPS and channels == groups * WIDTH and tokens_here % (2 * TAPS) == 0
    columns = channels // LANES
    halves = 1
    part = channels // halves
    count = max(halves, channels // STEP)
    skip_row = skip[None, :]
    gain_row = gain[None, :]
    gain_here = lax.dynamic_slice_in_dim(gain, lax.axis_index("tensor") * channels, channels)[None, :]

    spec = pl.BlockSpec

    def padded(count=None):
        shape = (tokens_here + 8, LANES)
        return pltpu.VMEM(shape if count is None else (count,) + shape, f32)

    def kernel(body, name, micros, limit=VMEM_LIMIT, **how):
        return pl.pallas_call(
            body,
            compiler_params=params(limit),
            cost_estimate=pl.CostEstimate(flops=0, bytes_accessed=micros * 1000, transcendentals=0),
            name=name,
            **how,
        )

    packed, halo = kernel(
        open_kernel,
        "open",
        3,
        in_specs=[spec(memory_space=pl.ANY)] * 3 + [spec(memory_space=pltpu.VMEM)],
        out_specs=[spec(memory_space=pl.ANY)] * 2,
        out_shape=[
            jax.ShapeDtypeStruct((owners, 2, rows_here, channels), bf16),
            jax.ShapeDtypeStruct((TAPS + 8, channels), bf16),
        ],
        scratch_shapes=[
            pltpu.VMEM((owners, 2, rows_here, channels), bf16),
            pltpu.VMEM((2, TAPS + 16, channels), bf16),
            pltpu.VMEM((16, channels), bf16),
            pltpu.VMEM((TAPS + 8, channels), bf16),
            pltpu.VMEM((3, TAPS + 16, LANES), f32),
            pltpu.SemaphoreType.DMA((owners, 2)),
            pltpu.SemaphoreType.DMA((owners, 2)),
            pltpu.SemaphoreType.DMA((3,)),
        ],
    )(cotangent, residual, streams, short_filter)
    halo = from_behind(halo, "dp", 1)
    received = lax.all_to_all(packed, "tensor", split_axis=0, concat_axis=0, tiled=True)

    band_shape = jax.ShapeDtypeStruct((groups, BLOCK, SPAN), bf16)
    each = min(groups, 16)
    ahead_bands, behind_bands = kernel(
        bands_kernel,
        "bands",
        5,
        grid=(groups // each,),
        in_specs=[spec((each, TAPS), lambda i: (i, 0))],
        out_specs=[spec((each, BLOCK, SPAN), lambda i: (i, 0, 0))] * 2,
        out_shape=[band_shape] * 2,
    )(long_filter)

    output, mixed, gated = streamed(
        forward_kernel,
        "forward",
        count,
        [(streams, {}, 2), (halo, {}, 1), (short_filter, {}, (2,)), (skip_row, {}, (1,)), (ahead_bands, {}, 0)],
        [((tokens_here, channels), t, 1) for t in (bf16, f32, bf16)],
        [padded(3)],
    )

    (stats,) = streamed(
        functools.partial(stats_kernel, count),
        "stats",
        count,
        [(received, {}, 3), (output, {}, 1), (gain_here, {}, (1,))],
        [((2, tokens_here), f32, None)],
        [pltpu.VMEM((tokens_here, LANES), f32)] * 2,
    )
    stats = lax.psum(stats, "tensor")
    heads = []
    for k in range(halves):
        here = (k * part, part)
        heads.append(
            streamed(
                functools.partial(head_kernel, width_all),
                "head",
                count // halves,
                [
                    (streams, {0: (0, 1), 2: here}, 2),
                    (streams, {0: (1, 1), 1: (0, 16), 2: here}, 2),
                    (streams, {0: (2, 1), 1: (0, 16), 2: here}, 2),
                    (halo, {1: here}, 1),
                    (short_filter, {2: here}, (2,)),
                    (skip_row, {1: here}, (1,)),
                    (long_filter, {0: (k * groups // halves, groups // halves)}, 0),
                    (stats, {}, None),
                    (received, {3: here}, 3),
                    (output, {1: here}, 1),
                    (gain_here, {1: here}, (1,)),
                    (mixed, {0: (0, 16), 1: here}, 1),
                ],
                [
                    ((tokens_here, part), bf16, 1),
                    ((tokens_here, part), bf16, 1),
                    ((1, part), f32, (1,)),
                    ((TAPS + 8, part), bf16, 1),
                ],
                [padded()] + [pltpu.VMEM((tokens_here, LANES), f32)] * 2,
            )
        )
    grads, inner, shares, first = (tuple(column) for column in zip(*heads))
    after = [from_behind(piece, "dp", -1) for piece in first]
    leaving, inner = lax.optimization_barrier((output, inner))
    rows_received = lax.all_to_all(
        leaving.reshape(owners, rows_here, channels), "tensor", split_axis=0, concat_axis=0, tiled=True
    )

    (early,) = streamed(
        sums_kernel,
        "sums",
        count,
        [
            (streams, {0: (0, 1)}, 2),
            (halo, {}, 1),
            (gated, {}, 1),
            (inner, {}, 1),
            (grads, {}, 1),
            (mixed, {}, 1),
            (shares, {}, (1,)),
        ],
        [((columns * 16, LANES), f32, 0)],
        [padded()],
    )

    stream_grad, bundle = streamed(
        backward_kernel,
        "backward",
        count,
        [
            (streams, {0: (1, 2)}, 2),
            (halo, {}, 1),
            (short_filter, {}, (2,)),
            (skip_row, {}, (1,)),
            (behind_bands, {}, 0),
            (grads, {}, 1),
            (mixed, {}, 1),
            (inner, {}, 1),
            (tuple(after), {}, 1),
            (early, {}, 0),
        ],
        [(streams.shape, bf16, 2), ((columns * 24, LANES), bf16, 0)],
        [padded(3), padded(3)],
    )
    bits = (lax.axis_size("dp") - 1).bit_length()
    stages = [[1 << n] if n + 1 == bits else [1 << n, 2 << n, 3 << n] for n in range(0, bits, 2)]
    total = bundle
    for stage in stages[:-1]:
        mine, others = sent_to(total, "dp", stage)
        total = added(mine, others)
    block = min(rows_here, 32)
    by_rows = spec((block, width_all), lambda i: (i, 0))
    normed, grad_residual = kernel(
        norm_kernel,
        "norm",
        4,
        NORM_LIMIT,
        grid=(rows_here // block,),
        in_specs=[
            spec((owners, block, channels), lambda i: (0, i, 0)),
            by_rows,
            by_rows,
            spec((1, width_all), lambda i: (0, 0)),
        ],
        out_specs=[by_rows, by_rows],
        out_shape=[jax.ShapeDtypeStruct(residual.shape, bf16)] * 2,
        scratch_shapes=[pltpu.VMEM((block, width_all), f32)],
    )(rows_received, residual, cotangent, gain_row)

    mine, others = sent_to(total, "dp", stages[-1])
    mine, normed, grad_residual = lax.optimization_barrier((mine, normed, grad_residual))
    mine, other = (mine, others[0]) if len(others) == 1 else (added(mine, others[:1]), added(others[1], others[2:]))
    long_grad, short_grad, skip_grad, gain_grad = kernel(
        close_kernel,
        "close",
        1,
        SMALL_LIMIT,
        out_shape=[
            jax.ShapeDtypeStruct((groups, TAPS), f32),
            jax.ShapeDtypeStruct((3, 3, channels), f32),
            jax.ShapeDtypeStruct((1, channels), f32),
            jax.ShapeDtypeStruct((1, channels), f32),
        ],
    )(mine, other)
    skip_grad, gain_grad = skip_grad.reshape(channels), gain_grad.reshape(channels)
    return (normed, grad_residual, stream_grad, long_grad, short_grad, skip_grad, gain_grad)


def solution(mesh):
    placed = (
        P(("dp", "tensor"), None),
        P(None, "dp", "tensor"),
        P(None, None, "tensor"),
        P("tensor", None),
        P("tensor"),
        P(),
        P(("dp", "tensor"), None),
    )
    return jax.shard_map(
        local,
        mesh=mesh,
        in_specs=placed,
        out_specs=(
            P(("dp", "tensor"), None),
            P(("dp", "tensor"), None),
            P(None, "dp", "tensor"),
            P("tensor", None),
            P(None, None, "tensor"),
            P("tensor"),
            P("tensor"),
        ),
        check_vma=False,
    )
```
